32 devices in a mesh: dp: 16 (over z, x, core), tensor: 2 (over y).
Axes of the slice: x: 2, y: 2, z: 4, core: 2. Of those that a mesh axis runs over, the one named last changes fastest.
Arguments:
- tokens: bfloat16 [4096, 1024], P('dp'), may hold values from -6 to 6
- cotangent: bfloat16 [4096, 1024], P('dp'), may hold values from -6 to 6
- seq_lens: int32 [64], P('dp'), may hold values from 0 to 256, as said below
- layer_norm_gain: float32 [2, 1024], replicated, may hold values from 0.1 to 1.9
- layer_norm_bias: float32 [2, 1024], replicated, may hold values from -2 to 2
- w_qkv: bfloat16 [3, 1024, 1024], P(None, 'dp', 'tensor'), may hold values from -1 to 1
- b_qv: float32 [2, 1024], P(None, 'tensor'), may hold values from -2 to 2
- w_out: bfloat16 [1024, 1024], P('dp', 'tensor'), may hold values from -0.75 to 0.75
- b_out: float32 [1024], replicated, may hold values from -2 to 2
- w_fc1: bfloat16 [1024, 4096], P('dp', 'tensor'), may hold values from -0.1875 to 0.1875
- b_fc1: float32 [4096], P('tensor'), may hold values from -3 to 3
- w_fc2: bfloat16 [1024, 4096], P('dp', 'tensor'), may hold values from -0.09375 to 0.09375
- b_fc2: float32 [1024], replicated, may hold values from -2 to 2
Outputs:
- output: bfloat16 [4096, 1024], P('dp')
- grad_tokens: float32 [4096, 1024], P('dp')
- grad_norm_gain: float32 [2, 1024], replicated
- grad_norm_bias: float32 [2, 1024], replicated
- grad_w_qkv: float32 [3, 1024, 1024], P(None, 'dp', 'tensor')
- grad_b_qv: float32 [2, 1024], P(None, 'tensor')
- grad_w_out: float32 [1024, 1024], P('dp', 'tensor')
- grad_b_out: float32 [1024], replicated
- grad_w_fc1: float32 [1024, 4096], P('dp', 'tensor')
- grad_b_fc1: float32 [4096], P('tensor')
- grad_w_fc2: float32 [1024, 4096], P('dp', 'tensor')
- grad_b_fc2: float32 [1024], replicated
The draws below stay inside these ranges and needn't reach their ends.
Inputs may be any that keep to these rules, and one draw needn't show every extreme that they name: `seq_lens`: each device's 4 lengths are whole sequences laid one after another from its first row; they sum to at most 256, and some device holds a single sequence of exactly 256 rows. Rows after a device's sequences are padding.
All inputs are finite; a program needn't handle non-finite values.
Results may differ from the reference program's by a relative error of at most 0.014.
Values may be sent and summed in bfloat16 or wider, within the bound.
A program may use at most 128 MiB of HBM per device.

```python
import jax
import jax.numpy as jnp
from jax import lax

D = 1024
HEAD_DIM = 64
FF = 4096
TOK_DEV = 256
SEQ_DEV = 4
TOKENS = 4096
SEQS = 64
N_DP = 16


def draw_seq_lens(key, part):
    device_count = SEQS // SEQ_DEV
    key_used = jax.random.fold_in(key, 11)
    key_full = jax.random.fold_in(key, 12)
    key_cuts = jax.random.fold_in(key, 13)
    used = jax.random.randint(key_used, (device_count,), TOK_DEV // 4, TOK_DEV + 1)
    full_device = jax.random.randint(key_full, (), 0, device_count)
    cuts = jax.random.randint(key_cuts, (device_count, SEQ_DEV - 1), 0, TOK_DEV + 1)
    cuts = jnp.sort(jnp.minimum(cuts, used[:, None]), axis=1)
    edges = jnp.concatenate([jnp.zeros((device_count, 1), jnp.int32), cuts.astype(jnp.int32), used[:, None].astype(jnp.int32)], axis=1)
    lengths = edges[:, 1:] - edges[:, :-1]
    single = jnp.zeros((SEQ_DEV,), jnp.int32).at[0].set(TOK_DEV)
    chosen = (jnp.arange(device_count) == full_device)[:, None]
    lengths = jnp.where(chosen, single[None, :], lengths)
    return lengths.reshape(-1).astype(jnp.int32)


def draw_w_qkv(key, part):
    key_base = jax.random.fold_in(key, 21)
    base = jax.random.normal(key_base, (3, D, D), jnp.float32) * D ** (-0.5)
    weights = base
    return jnp.clip(weights, -1.0, 1.0).astype(jnp.bfloat16)


def strengthened(drawn, stream_key, source, target, shards_of, factor):
    owner, partner = [(jnp.arange(drawn.shape[dim]) // (drawn.shape[dim] // shards_of)).reshape([-1 if axis == dim else 1 for axis in range(drawn.ndim)]) for dim in (source, target)]
    chosen = jax.random.permutation(stream_key, shards_of)[partner]
    strong = (owner == chosen) | (owner == (partner + shards_of // 2) % shards_of)
    return jnp.where(strong, factor * drawn, drawn)


def block_scale(own_key, shape, split, smallest, top_value):
    level, own = 1.0, jax.random.fold_in(own_key, 6)
    for position, parts in split:
        draws = jnp.exp(jax.random.uniform(jax.random.fold_in(own, position), (parts,), jnp.float32, smallest / len(split), top_value / len(split)))
        level = level * jnp.repeat(draws, shape[position] // parts).reshape([-1 if axis == position else 1 for axis in range(len(shape))])
    return level


def gaussian(rng, dims, width, reach, pieces=(), kind=jnp.bfloat16):
    loudness = block_scale(rng, dims, pieces, -0.22, 0.18) if pieces else 1.0
    drawn = jax.random.normal(rng, dims, jnp.float32) * width * loudness
    return jnp.minimum(jnp.maximum(drawn, -reach), reach).astype(kind)


def noise_with(rng, shape, width, most, shards, heavy, kind=jnp.bfloat16):
    drawn = width * jax.random.normal(rng, shape, jnp.float32)
    if shards:
        drawn = drawn * block_scale(rng, shape, shards, -0.22, 0.18)
    return jnp.clip(strengthened(drawn, jax.random.fold_in(rng, 3), *heavy), -most, most).astype(kind)


def setup_inputs(seed: int = 0) -> dict:
    splits = jax.random.split(jax.random.key(seed), 14)
    tokens = gaussian(splits[0], (TOKENS, D), 1.0, 6.0, ((0, 16),))
    cotangent = noise_with(splits[1], (TOKENS, D), 1.0, 6.0, ((0, 16),), (0, 1, 16, 2.0))
    seq_lens = draw_seq_lens(jax.random.fold_in(splits[13], 71), 0)
    layer_norm_gain = jnp.clip(1.0 + 0.18 * jax.random.normal(splits[3], (2, D), jnp.float32), 0.1, 1.9)
    layer_norm_bias = gaussian(splits[4], (2, D), 0.3, 2.0, (), jnp.float32)
    w_qkv = draw_w_qkv(jax.random.fold_in(splits[13], 71), 0)
    b_qv = gaussian(splits[6], (2, D), 0.3, 2.0, ((1, 2),), jnp.float32)
    w_out = gaussian(splits[7], (D, D), (D // 16) ** -0.5, 0.75, ((0, 16), (1, 2)))
    b_out = gaussian(splits[8], (D,), 0.3, 2.0, (), jnp.float32)
    w_fc1 = gaussian(splits[9], (D, FF), D ** -0.5, 0.1875, ((0, 16), (1, 2)))
    b_fc1 = gaussian(splits[10], (FF,), 0.5, 3.0, ((0, 2),), jnp.float32)
    w_fc2 = gaussian(splits[11], (D, FF), FF ** -0.5, 0.09375, ((0, 16), (1, 2)))
    b_fc2 = gaussian(splits[12], (D,), 0.3, 2.0, (), jnp.float32)
    return {"tokens": tokens, "cotangent": cotangent, "seq_lens": seq_lens, "layer_norm_gain": layer_norm_gain, "layer_norm_bias": layer_norm_bias, "w_qkv": w_qkv, "b_qv": b_qv, "w_out": w_out, "b_out": b_out, "w_fc1": w_fc1, "b_fc1": b_fc1, "w_fc2": w_fc2, "b_fc2": b_fc2}


NORM_EPS = 1e-05
GELU_COEF = 0.7978845608028654

def product(spec, left, right):
    return jnp.einsum(spec, left.astype(jnp.float32), right.astype(jnp.float32))

def seq_masks(lengths, row_count):
    ends = jnp.cumsum(lengths, dtype=jnp.int32)
    places = jnp.arange(row_count, dtype=jnp.int32)
    segment = lax.optimization_barrier(jnp.sum((places[:, None] >= ends[None, :]).astype(jnp.int32), axis=1))
    allowed = (segment[:, None] == segment[None, :]) & (places[:, None] >= places[None, :])
    live_rows = places < ends[-1]
    return (allowed, live_rows)

def layer_norm_forward(hidden, gain, shift):
    center = hidden - lax.optimization_barrier(jnp.mean(hidden, axis=-1, keepdims=True))
    inv_std = lax.rsqrt(lax.optimization_barrier(jnp.mean(center * center, axis=-1, keepdims=True)) + NORM_EPS)
    normal_x = center * inv_std
    return (normal_x * gain + shift, normal_x, inv_std)

def layer_norm_backward(grad_out, gain, normal_x, inv_std):
    scaled = grad_out * gain
    return inv_std * (scaled - lax.optimization_barrier(jnp.mean(scaled, axis=-1, keepdims=True)) - normal_x * lax.optimization_barrier(jnp.mean(scaled * normal_x, axis=-1, keepdims=True)))

def gelu_parts(pre_act):
    inner = GELU_COEF * (pre_act + 0.044715 * pre_act * pre_act * pre_act)
    tanh_val = jnp.tanh(inner)
    value = 0.5 * pre_act * (1.0 + tanh_val)
    slope = 0.5 * (1.0 + tanh_val) + 0.5 * pre_act * (1.0 - tanh_val * tanh_val) * GELU_COEF * (1.0 + 3.0 * 0.044715 * pre_act * pre_act)
    return (value, slope)

def split_heads(matrix):
    return matrix.reshape(matrix.shape[0], matrix.shape[1] // HEAD_DIM, HEAD_DIM)

def head_scores(query, key_rows, allowed):
    scores = product('qhd,khd->hqk', split_heads(query), split_heads(key_rows)) * HEAD_DIM ** (-0.5)
    return jnp.where(allowed[None], scores, -1e+30)

def attend(query, key_rows, value, allowed):
    scores = head_scores(query, key_rows, allowed)
    row_max = lax.optimization_barrier(jnp.max(scores, axis=-1, keepdims=True))
    logsum = row_max + jnp.log(lax.optimization_barrier(jnp.sum(jnp.exp(scores - row_max), axis=-1, keepdims=True)))
    weights = jnp.exp(scores - logsum).astype(jnp.bfloat16)
    mixed = product('hqk,khd->qhd', weights, split_heads(value)).astype(jnp.bfloat16)
    return (mixed.reshape(query.shape[0], -1), logsum)

def attend_back(query, key_rows, value, heads_out, d_heads, logsum, allowed):
    scores = head_scores(query, key_rows, allowed)
    probs = jnp.exp(scores - logsum)
    probs_low = probs.astype(jnp.bfloat16)
    d_split = split_heads(d_heads)
    d_prob = product('qhd,khd->hqk', d_split, split_heads(value))
    delta = lax.optimization_barrier(jnp.sum(d_split.astype(jnp.float32) * split_heads(heads_out).astype(jnp.float32), axis=-1))
    d_score = (probs * (d_prob - jnp.transpose(delta)[:, :, None]) * HEAD_DIM ** (-0.5)).astype(jnp.bfloat16)
    d_query = product('hqk,khd->qhd', d_score, split_heads(key_rows)).astype(jnp.bfloat16)
    d_key = product('hqk,qhd->khd', d_score, split_heads(query)).astype(jnp.bfloat16)
    d_value = product('hqk,qhd->khd', probs_low, d_split).astype(jnp.bfloat16)
    row_count = query.shape[0]
    return (d_query.reshape(row_count, -1), d_key.reshape(row_count, -1), d_value.reshape(row_count, -1))

def one_block(block_in, block_cot, lengths, layer_norm_gain, layer_norm_bias, w_qkv, b_qv, w_out, b_out, w_fc1, b_fc1, w_fc2, b_fc2):
    allowed, live_rows = seq_masks(lengths, block_in.shape[0])
    input_tokens = block_in.astype(jnp.float32)
    first_normalized, first_centered_scaled, first_inverse_deviation = layer_norm_forward(input_tokens, layer_norm_gain[0], layer_norm_bias[0])
    low1 = first_normalized.astype(jnp.bfloat16)
    proj = product('td,idc->itc', low1, w_qkv)
    query = (proj[0] + b_qv[0]).astype(jnp.bfloat16)
    key_rows = proj[1].astype(jnp.bfloat16)
    value = (proj[2] + b_qv[1]).astype(jnp.bfloat16)
    heads_out, logsum = attend(query, key_rows, value, allowed)
    first_hidden_state = input_tokens + jnp.dot(heads_out, w_out.T, preferred_element_type=jnp.float32) + b_out
    second_normalized, second_centered_scaled, second_inverse_deviation = layer_norm_forward(first_hidden_state, layer_norm_gain[1], layer_norm_bias[1])
    low2 = second_normalized.astype(jnp.bfloat16)
    pre_act = jnp.dot(low2, w_fc1, preferred_element_type=jnp.float32) + b_fc1
    act, slope = gelu_parts(pre_act)
    act_low = act.astype(jnp.bfloat16)
    result = first_hidden_state + jnp.dot(act_low, w_fc2.T, preferred_element_type=jnp.float32) + b_fc2
    output = jnp.where(live_rows[:, None], result, 0.0).astype(jnp.bfloat16)
    grad_y = jnp.where(live_rows[:, None], block_cot, jnp.zeros_like(block_cot))
    flat_output_gradient = grad_y.astype(jnp.float32)
    d_pre = (jnp.dot(grad_y, w_fc2, preferred_element_type=jnp.float32) * slope).astype(jnp.bfloat16)
    g_fc2 = jnp.dot(grad_y.T, act_low, preferred_element_type=jnp.float32)
    g_bfc2 = lax.optimization_barrier(jnp.sum(flat_output_gradient, axis=0))
    g_fc1 = jnp.dot(low2.T, d_pre, preferred_element_type=jnp.float32)
    g_bfc1 = lax.optimization_barrier(jnp.sum(d_pre.astype(jnp.float32), axis=0))
    second_norm_delta = jnp.dot(d_pre, w_fc1.T, preferred_element_type=jnp.float32)
    second_gain_gradient = lax.optimization_barrier(jnp.sum(second_norm_delta * second_centered_scaled, axis=0))
    g_shift2 = lax.optimization_barrier(jnp.sum(second_norm_delta, axis=0))
    hidden_first_gradient = flat_output_gradient + layer_norm_backward(second_norm_delta, layer_norm_gain[1], second_centered_scaled, second_inverse_deviation)
    grad_low = hidden_first_gradient.astype(jnp.bfloat16)
    g_out = jnp.dot(grad_low.T, heads_out, preferred_element_type=jnp.float32)
    g_bout = lax.optimization_barrier(jnp.sum(hidden_first_gradient, axis=0))
    d_heads = jnp.dot(grad_low, w_out, preferred_element_type=jnp.float32).astype(jnp.bfloat16)
    d_query, d_key, d_value = attend_back(query, key_rows, value, heads_out, d_heads, logsum, allowed)
    stacked = jnp.stack([d_query, d_key, d_value])
    g_qkv = product('td,itc->idc', low1, stacked)
    g_bqv = jnp.stack([lax.optimization_barrier(jnp.sum(d_query.astype(jnp.float32), axis=0)), lax.optimization_barrier(jnp.sum(d_value.astype(jnp.float32), axis=0))])
    first_norm_delta = product('itc,idc->td', stacked, w_qkv)
    first_gain_gradient = lax.optimization_barrier(jnp.sum(first_norm_delta * first_centered_scaled, axis=0))
    g_shift1 = lax.optimization_barrier(jnp.sum(first_norm_delta, axis=0))
    input_gradient = hidden_first_gradient + layer_norm_backward(first_norm_delta, layer_norm_gain[0], first_centered_scaled, first_inverse_deviation)
    grads = (jnp.stack([first_gain_gradient, second_gain_gradient]), jnp.stack([g_shift1, g_shift2]), g_qkv, g_bqv, g_out, g_bout, g_fc1, g_bfc1, g_fc2, g_bfc2)
    return (output, input_gradient, grads)

def reference(tokens, cotangent, seq_lens, layer_norm_gain, layer_norm_bias, w_qkv, b_qv, w_out, b_out, w_fc1, b_fc1, w_fc2, b_fc2):
    block_ins = tokens.reshape(N_DP, TOK_DEV, D)
    block_cots = cotangent.reshape(N_DP, TOK_DEV, D)
    block_lens = seq_lens.reshape(N_DP, SEQ_DEV)
    zero_grads = (jnp.zeros((2, D), jnp.float32), jnp.zeros((2, D), jnp.float32), jnp.zeros((3, D, D), jnp.float32), jnp.zeros((2, D), jnp.float32), jnp.zeros((D, D), jnp.float32), jnp.zeros((D,), jnp.float32), jnp.zeros((D, FF), jnp.float32), jnp.zeros((FF,), jnp.float32), jnp.zeros((D, FF), jnp.float32), jnp.zeros((D,), jnp.float32))

    def step_block(carry, items):
        block_in, block_cot, lengths = items
        output, input_gradient, grads = one_block(block_in, block_cot, lengths, layer_norm_gain, layer_norm_bias, w_qkv, b_qv, w_out, b_out, w_fc1, b_fc1, w_fc2, b_fc2)
        carry = tuple((total + part for total, part in zip(carry, grads)))
        return (carry, (output, input_gradient))
    totals, (outputs, grad_ins) = lax.scan(step_block, zero_grads, (block_ins, block_cots, block_lens))
    return (outputs.reshape(TOKENS, D), grad_ins.reshape(TOKENS, D), totals[0], totals[1], totals[2], totals[3], totals[4], totals[5], totals[6], totals[7], totals[8], totals[9])
```

```python
import jax
import jax.numpy as jnp
from jax import lax
from jax.experimental import pallas as pl
from jax.experimental.pallas import tpu as pltpu
from jax.sharding import PartitionSpec as P

HEAD_DIM = 64


NORM_EPS = 1e-05
GELU_COEF = 0.7978845608028654


def product(spec, left, right):
    return jnp.einsum(spec, left, right, preferred_element_type=jnp.float32)


def seq_masks(lengths, row_count):
    slots = jnp.arange(lengths.shape[0])
    ends = jnp.sum(jnp.where(slots[:, None] <= slots[None, :], lengths[:, None], 0), axis=0)
    places = jnp.arange(row_count, dtype=jnp.int32)
    segment = jnp.sum((places[:, None] >= ends[None, :]).astype(jnp.int32), axis=1)
    allowed = (segment[:, None] == segment[None, :]) & (places[:, None] >= places[None, :])
    live_rows = places < ends[-1]
    return (allowed, live_rows)


def layer_norm_forward(hidden, gain, shift):
    center = hidden - jnp.mean(hidden, axis=-1, keepdims=True)
    inv_std = lax.rsqrt(jnp.mean(center * center, axis=-1, keepdims=True) + NORM_EPS)
    normal_x = center * inv_std
    return (normal_x * gain + shift, normal_x, inv_std)


def layer_norm_backward(grad_out, gain, normal_x, inv_std):
    scaled = grad_out * gain
    return inv_std * (
        scaled
        - jnp.mean(scaled, axis=-1, keepdims=True)
        - normal_x * jnp.mean(scaled * normal_x, axis=-1, keepdims=True)
    )


def gelu_parts(pre_act):
    inner = GELU_COEF * (pre_act + 0.044715 * pre_act * pre_act * pre_act)
    tanh_val = jnp.tanh(inner)
    value = 0.5 * pre_act * (1.0 + tanh_val)
    slope = 0.5 * (1.0 + tanh_val) + 0.5 * pre_act * (1.0 - tanh_val * tanh_val) * GELU_COEF * (
        1.0 + 3.0 * 0.044715 * pre_act * pre_act
    )
    return (value, slope)


def split_heads(matrix):
    return matrix.reshape(matrix.shape[0], matrix.shape[1] // HEAD_DIM, HEAD_DIM)


def head_scores(query, key_rows, allowed):
    scores = product("qhd,khd->hqk", split_heads(query), split_heads(key_rows)) * HEAD_DIM ** (-0.5)
    return jnp.where(allowed[None], scores, -1e30)


def attend(query, key_rows, value, allowed):
    scores = head_scores(query, key_rows, allowed)
    row_max = jnp.max(scores, axis=-1, keepdims=True)
    logsum = row_max + jnp.log(jnp.sum(jnp.exp(scores - row_max), axis=-1, keepdims=True))
    weights = jnp.exp(scores - logsum).astype(jnp.bfloat16)
    mixed = product("hqk,khd->qhd", weights, split_heads(value)).astype(jnp.bfloat16)
    return (mixed.reshape(query.shape[0], -1), logsum)


def attend_back(query, key_rows, value, heads_out, d_heads, logsum, allowed):
    scores = head_scores(query, key_rows, allowed)
    probs = jnp.exp(scores - logsum)
    probs_low = probs.astype(jnp.bfloat16)
    d_split = split_heads(d_heads)
    d_prob = product("qhd,khd->hqk", d_split, split_heads(value))
    delta = jnp.sum(
        d_split.astype(jnp.float32) * split_heads(heads_out).astype(jnp.float32), axis=-1
    )
    d_score = (probs * (d_prob - jnp.transpose(delta)[:, :, None]) * HEAD_DIM ** (-0.5)).astype(
        jnp.bfloat16
    )
    d_query = product("hqk,khd->qhd", d_score, split_heads(key_rows)).astype(jnp.bfloat16)
    d_key = product("hqk,qhd->khd", d_score, split_heads(query)).astype(jnp.bfloat16)
    d_value = product("hqk,qhd->khd", probs_low, d_split).astype(jnp.bfloat16)
    row_count = query.shape[0]
    return (
        d_query.reshape(row_count, -1),
        d_key.reshape(row_count, -1),
        d_value.reshape(row_count, -1),
    )


def sum_tensor(part):
    low = lax.optimization_barrier(part.astype(jnp.bfloat16))
    count = lax.axis_size("tensor")
    if count != 2:
        return lax.psum(low, "tensor").astype(jnp.float32)
    other = lax.ppermute(low, "tensor", [(0, 1), (1, 0)])
    return low.astype(jnp.float32) + other.astype(jnp.float32)


def chip_at(place, chips):
    place = (place + chips) % chips
    back = place // (chips // 2)
    return 2 * (place * (1 - back) + (chips - 1 - place) * back) + back


def ring_place(chips):
    device = lax.axis_index("dp")
    core, chip = device % 2, device // 2
    column, row = chip % 2, chip // 2
    place = row * (1 - column) + (chips - 1 - row) * column
    return device, chip, core, place


def send(source, target, send_sem, recv_sem, device):
    return pltpu.make_async_remote_copy(
        src_ref=source,
        dst_ref=target,
        send_sem=send_sem,
        recv_sem=recv_sem,
        device_id={"dp": device},
        device_id_type=pl.DeviceIdType.MESH,
    )


def meet(devices):
    barrier = pltpu.get_barrier_semaphore()
    for device in devices:
        pl.semaphore_signal(
            barrier, inc=1, device_id={"dp": device}, device_id_type=pl.DeviceIdType.MESH
        )
    pl.semaphore_wait(barrier, len(devices))


def gather_kernel(chips, own, out, rs, rr, ls, lr, ps, pr, own_sem):
    device, chip, core, place = ring_place(chips)
    right = 2 * chip_at(place + 1, chips) + core
    left = 2 * chip_at(place - 1, chips) + core
    partner = 2 * chip + 1 - core
    meet((right, left, partner))
    top, width = chips // 2, own.shape[1]
    half = width // 2

    def block(step, whose, hop, side):
        at = out.at[2 * chip_at(place + step, chips) + whose]
        if hop < top:
            return at
        return at.at[:, pl.ds(side * half, half)]

    started = []

    def go(copy):
        copy.start()
        started.append(copy)

    go(send(own, out.at[device], rs.at[0], rr.at[0], right))
    go(send(own, out.at[device], ls.at[0], lr.at[0], left))
    go(send(own, out.at[device], ps.at[0], pr.at[0], partner))
    keep = pltpu.make_async_copy(own, out.at[device], own_sem)
    keep.start()
    passed = [block(0, 1 - core, 0, 0)]
    for hop in range(1, top + 1):
        for side, sign, s_sem, r_sem, onward in ((0, -1, rs, rr, right), (1, 1, ls, lr, left)):
            here = block(sign * hop, core, hop, side)
            send(here, here, s_sem.at[hop - 1], r_sem.at[hop - 1], onward).wait_recv()
            if hop < top:
                part = block(sign * hop, core, hop + 1, side)
                go(send(part, part, s_sem.at[hop], r_sem.at[hop], onward))
            slot = len(passed)
            go(send(here, here, ps.at[slot], pr.at[slot], partner))
            passed.append(block(sign * hop, 1 - core, hop, side))
    for slot, here in enumerate(passed):
        send(here, here, ps.at[slot], pr.at[slot], partner).wait_recv()
    for copy in started:
        copy.wait_send()
    keep.wait()


def gather_rows(shard):
    count = lax.axis_size("dp")
    chips = count // 2
    top = chips // 2
    dma = pltpu.SemaphoreType.DMA
    out = pl.pallas_call(
        lambda *refs: gather_kernel(chips, *refs),
        out_shape=jax.ShapeDtypeStruct((count, *shard.shape), shard.dtype),
        in_specs=[pl.BlockSpec(memory_space=pltpu.VMEM)],
        out_specs=pl.BlockSpec(memory_space=pl.ANY),
        scratch_shapes=[dma((top,))] * 4 + [dma((chips + 1,))] * 2 + [dma],
        compiler_params=pltpu.CompilerParams(collective_id=0, has_side_effects=True),
        name="gather_rows",
    )(shard)
    return out.reshape(count * shard.shape[0], shard.shape[1])


def scatter_kernel(
    chips, grads, vec, out, vec_out,
    pbuf, rbuf, lbuf, rstage, lstage, vpart, vslots,
    ps, pr, rs, rr, ls, lr, vps, vpr, vrs, vrr, vls, vlr,
):
    device, chip, core, place = ring_place(chips)
    right = 2 * chip_at(place + 1, chips) + core
    left = 2 * chip_at(place - 1, chips) + core
    partner = 2 * chip + 1 - core
    meet((right, left, partner))
    top, width = chips // 2, out.shape[1]
    half = width // 2
    low, high = pl.ds(0, half), pl.ds(half, half)
    started = []

    def go(copy):
        copy.start()
        started.append(copy)

    order = [top]
    for step in range(1, top):
        order += [top - step, step - top]
    order.append(0)
    go(send(vec, vpart, vps.at[0], vpr.at[0], partner))
    for slot, step in enumerate(order):
        mine = grads.at[2 * chip_at(place + step, chips) + 1 - core]
        go(send(mine, pbuf.at[slot], ps.at[slot], pr.at[slot], partner))

    def pair_sum(slot):
        spot = pbuf.at[slot]
        send(spot, spot, ps.at[slot], pr.at[slot], partner).wait_recv()
        mine = grads[2 * chip_at(place + order[slot], chips) + core]
        return mine.astype(jnp.float32) + pbuf[slot].astype(jnp.float32)

    def arrived(spot, s_sem, r_sem):
        send(spot, spot, s_sem, r_sem, partner).wait_recv()

    first = pair_sum(0).astype(jnp.bfloat16)
    rstage[0, :, :half] = first[:, :half]
    go(send(rstage.at[0, :, low], rbuf.at[0, :, low], rs.at[0], rr.at[0], right))
    lstage[0, :, half:] = first[:, half:]
    go(send(lstage.at[0, :, high], lbuf.at[0, :, high], ls.at[0], lr.at[0], left))
    arrived(vpart, vps.at[0], vpr.at[0])
    vslots[chip] = vec[...] + vpart[...]
    go(send(vslots.at[chip], vslots.at[chip], vrs.at[0], vrr.at[0], right))
    go(send(vslots.at[chip], vslots.at[chip], vls.at[0], vlr.at[0], left))
    for step in range(1, top):
        for side, buf, stage, s_sem, r_sem, onward in (
            (0, rbuf, rstage, rs, rr, right),
            (1, lbuf, lstage, ls, lr, left),
        ):
            total = pair_sum(2 * step - 1 + side)
            if step == 1:
                cols = (low, high)[side]
                arrived(buf.at[0, :, cols], s_sem.at[0], r_sem.at[0])
                more = buf[0, :, side * half : (side + 1) * half].astype(jnp.float32)
                if side == 0:
                    stage[step, :, :half] = (total[:, :half] + more).astype(jnp.bfloat16)
                    stage[step, :, half:] = total[:, half:].astype(jnp.bfloat16)
                else:
                    stage[step, :, :half] = total[:, :half].astype(jnp.bfloat16)
                    stage[step, :, half:] = (total[:, half:] + more).astype(jnp.bfloat16)
            else:
                arrived(buf.at[step - 1], s_sem.at[step - 1], r_sem.at[step - 1])
                stage[step] = (total + buf[step - 1].astype(jnp.float32)).astype(jnp.bfloat16)
            go(send(stage.at[step], buf.at[step], s_sem.at[step], r_sem.at[step], onward))
        spot = vslots.at[chip_at(place - step, chips)]
        arrived(spot, vrs.at[step - 1], vrr.at[step - 1])
        go(send(spot, spot, vrs.at[step], vrr.at[step], right))
        spot = vslots.at[chip_at(place + step, chips)]
        arrived(spot, vls.at[step - 1], vlr.at[step - 1])
        if step < top - 1:
            go(send(spot, spot, vls.at[step], vlr.at[step], left))
    spot = vslots.at[chip_at(place - top, chips)]
    arrived(spot, vrs.at[top - 1], vrr.at[top - 1])
    vec_out[...] = jnp.sum(vslots[...], axis=0)
    total = pair_sum(len(order) - 1)
    arrived(rbuf.at[top - 1], rs.at[top - 1], rr.at[top - 1])
    arrived(lbuf.at[top - 1], ls.at[top - 1], lr.at[top - 1])
    out[...] = total + rbuf[top - 1].astype(jnp.float32) + lbuf[top - 1].astype(jnp.float32)
    for copy in started:
        copy.wait_send()


def scatter_rows(grads, vectors):
    count = lax.axis_size("dp")
    chips = count // 2
    top = chips // 2
    rows, width = grads.shape[0] // count, grads.shape[1]
    lines = vectors.shape[0] // 128
    dma, vmem = pltpu.SemaphoreType.DMA, pl.BlockSpec(memory_space=pltpu.VMEM)
    block = (rows, width)
    shard, sums = pl.pallas_call(
        lambda *refs: scatter_kernel(chips, *refs),
        out_shape=(
            jax.ShapeDtypeStruct(block, jnp.float32),
            jax.ShapeDtypeStruct((lines, 128), jnp.float32),
        ),
        in_specs=[vmem, vmem],
        out_specs=(vmem, vmem),
        scratch_shapes=[pltpu.VMEM((chips, *block), jnp.bfloat16)]
        + [pltpu.VMEM((top, *block), jnp.bfloat16)] * 4
        + [pltpu.VMEM((lines, 128), jnp.float32), pltpu.VMEM((chips, lines, 128), jnp.float32)]
        + [dma((chips,))] * 2
        + [dma((top,))] * 4
        + [dma((1,))] * 2
        + [dma((top,))] * 4,
        compiler_params=pltpu.CompilerParams(collective_id=1, has_side_effects=True),
        name="scatter_rows",
    )(grads.reshape(count, rows, width), vectors.reshape(lines, 128))
    return shard, sums.reshape(-1)


GELU_CUBE = 0.044715
F32, BF16 = jnp.float32, jnp.bfloat16


def mm(left, right, dims=((1,), (0,))):
    return lax.dot_general(left, right, (dims, ((), ())), preferred_element_type=F32)


class Names:
    def __init__(self, names, refs):
        for name, ref in zip(names, refs):
            setattr(self, name, ref)


IN_NAMES = [
    "tok", "cot", "lens", "gain", "shift", "w_qkv", "b_qv", "w_out", "b_out", "w_fc1", "b_fc1",
    "w_fc2", "b_fc2",
]
OUT_NAMES = [
    "y", "g_tok", "o_gain", "o_shift", "g_qkv", "o_bqv", "g_out", "o_bout", "g_fc1", "o_bfc1",
    "g_fc2", "o_bfc2",
]


def layer_scratch(chips, rows, row_count, width, heads, hidden):
    count, top = 2 * chips, chips // 2
    dma = pltpu.SemaphoreType.DMA
    tall = (row_count, width)
    low = dict(
        wq=(count, 3, rows, heads), wo=(count, rows, heads),
        wf1=(count, rows, hidden), wf2=(count, rows, hidden),
        n1=tall, n2=tall, gy=tall, ghb=tall,
        z=(row_count, hidden), zp=(row_count, hidden),
        du=(row_count, hidden), dup=(row_count, hidden),
        qkv=(3, row_count, heads), o=(row_count, heads), op=(row_count, heads),
        dh=(row_count, heads),
        dqkv=(3, row_count, heads), dqkvp=(3, row_count, heads),
        xt=(4, 2, chips, rows, row_count), xtp=(4, chips, rows, row_count),
        grads=(3, chips, rows, hidden), rbuf=(3, 2, top, rows, hidden),
        ysend=(4, *tall), yrecv=(4, *tall),
    )
    full = dict(
        xh1=tall, xh2=tall, h1=tall, gh1=tall, rs1=(row_count, 1), rs2=(row_count, 1),
        u=(row_count, hidden), pf=(heads // HEAD_DIM, row_count, row_count),
        mask=(row_count, row_count), vec=(16, width), vslots=(count, 8, 128), vres=(16, width),
    )
    sems = dict(
        gs=(6, 2, top), gr=(6, 2, top), ps=(6, chips + 1), pr=(6, chips + 1),
        ss=(6, 2, top), sr=(6, 2, top), as_=(10,), ar=(10,), ys=(4, 4), yr=(4, 4),
        vs=(2, count), vr=(2, count), loc=(6,),
    )
    shapes = {k: pltpu.VMEM(s, BF16) for k, s in low.items()}
    shapes |= {k: pltpu.VMEM(s, F32) for k, s in full.items()}
    shapes |= {k: dma(s) for k, s in sems.items()}
    return shapes


def layer_kernel(chips, scratch_names, *refs):
    r = Names(IN_NAMES + OUT_NAMES + scratch_names, refs)
    device, chip, core, place = ring_place(chips)
    side_y = lax.axis_index("tensor")
    count, top = 2 * chips, chips // 2
    right = 2 * chip_at(place + 1, chips) + core
    left = 2 * chip_at(place - 1, chips) + core
    partner = 2 * chip + 1 - core
    onward = (right, left)
    row_count, width = r.tok.shape
    rows, heads = r.w_out.shape
    hidden = r.w_fc1.shape[1]
    half_hidden = hidden // 2
    started = []

    def remote(source, target, send_sem, recv_sem, **where):
        return pltpu.make_async_remote_copy(
            src_ref=source, dst_ref=target, send_sem=send_sem, recv_sem=recv_sem,
            device_id=where, device_id_type=pl.DeviceIdType.MESH,
        )

    def go(copy):
        copy.start()
        started.append(copy)

    barrier = pltpu.get_barrier_semaphore()
    for j in range(1, count):
        pl.semaphore_signal(
            barrier, inc=1, device_id={"dp": lax.rem(device + j, count)},
            device_id_type=pl.DeviceIdType.MESH,
        )
    pl.semaphore_signal(
        barrier, inc=1, device_id={"tensor": 1 - side_y}, device_id_type=pl.DeviceIdType.MESH
    )
    pl.semaphore_wait(barrier, count)

    buffers = (r.wq, r.wo, r.wf1, r.wf1, r.wf2, r.wf2)
    owns = (r.w_qkv, r.w_out, r.w_fc1, r.w_fc1, r.w_fc2, r.w_fc2)
    base = (0, 0, 0, half_hidden, 0, half_hidden)
    span = (heads, heads, half_hidden, half_hidden, half_hidden, half_hidden)

    def cut(i, ref, side=None):
        start, size = base[i], span[i]
        if side is not None:
            size = size // 2
            start = start + side * size
        if start == 0 and size == ref.shape[-1]:
            return ref
        if len(ref.shape) == 3:
            return ref.at[:, :, pl.ds(start, size)]
        return ref.at[:, pl.ds(start, size)]

    def block(i, step, whose, hop, side):
        at = buffers[i].at[2 * chip_at(place + step, chips) + whose]
        return cut(i, at, side if hop == top else None)

    def keep(i):
        return pltpu.make_async_copy(
            cut(i, owns[i]), cut(i, buffers[i].at[device]), r.loc.at[i]
        )

    def start_item(i):
        own, there = cut(i, owns[i]), cut(i, buffers[i].at[device])
        for side in (0, 1):
            go(remote(own, there, r.gs.at[i, side, 0], r.gr.at[i, side, 0], dp=onward[side]))
        go(remote(own, there, r.ps.at[i, 0], r.pr.at[i, 0], dp=partner))
        keep(i).start()

    def hop_item(i, hop):
        for side, sign in ((0, -1), (1, 1)):
            here = block(i, sign * hop, core, hop, side)
            remote(
                here, here, r.gs.at[i, side, hop - 1], r.gr.at[i, side, hop - 1], dp=onward[side]
            ).wait_recv()
            if hop < top:
                part = block(i, sign * hop, core, hop + 1, side)
                go(remote(
                    part, part, r.gs.at[i, side, hop], r.gr.at[i, side, hop], dp=onward[side]
                ))
            slot = 2 * hop - 1 + side
            go(remote(here, here, r.ps.at[i, slot], r.pr.at[i, slot], dp=partner))

    def finish_item(i):
        keep(i).wait()
        for slot in range(chips + 1):
            hop, side = (slot + 1) // 2, (slot + 1) % 2
            here = block(i, (-1, 1)[side] * hop, 1 - core, hop, side)
            remote(here, here, r.ps.at[i, slot], r.pr.at[i, slot], dp=partner).wait_recv()

    def swap(k, source, target):
        go(remote(source, target, r.as_.at[k], r.ar.at[k], dp=partner))

    def swapped(k, target):
        remote(target, target, r.as_.at[k], r.ar.at[k], dp=partner).wait_recv()

    quarter = width // 4
    group = count // 4

    def exchange(k, c):
        at = pl.ds(c * quarter, quarter)
        go(remote(
            r.ysend.at[k, :, at], r.yrecv.at[k, :, at], r.ys.at[k, c], r.yr.at[k, c],
            tensor=1 - side_y,
        ))

    def exchanged(k):
        for c in range(4):
            spot = r.yrecv.at[k, :, pl.ds(c * quarter, quarter)]
            remote(spot, spot, r.ys.at[k, c], r.yr.at[k, c], tensor=1 - side_y).wait_recv()

    scatter_span = half_hidden
    half = scatter_span // 2

    def scatter_start(i):
        k, col = i // 2, (i % 2) * scatter_span
        far = r.grads.at[k, chip_at(place + top, chips)]
        for side in (0, 1):
            at = pl.ds(col + side * half, half)
            go(remote(
                far.at[:, at], r.rbuf.at[k, side, 0, :, at], r.ss.at[i, side, 0],
                r.sr.at[i, side, 0], dp=onward[side],
            ))

    def scatter_step(i, s):
        k, col = i // 2, (i % 2) * scatter_span
        for side, sign in ((0, 1), (1, -1)):
            target = chip_at(place + sign * (top - s), chips)
            at = pl.ds(col + side * half, half) if s == 1 else pl.ds(col, scatter_span)
            spot = r.rbuf.at[k, side, s - 1, :, at]
            remote(
                spot, spot, r.ss.at[i, side, s - 1], r.sr.at[i, side, s - 1], dp=onward[side]
            ).wait_recv()
            total = r.grads[k, target, :, at].astype(F32) + spot[...].astype(F32)
            r.grads[k, target, :, at] = total.astype(BF16)
            at = pl.ds(col, scatter_span)
            go(remote(
                r.grads.at[k, target, :, at], r.rbuf.at[k, side, s, :, at],
                r.ss.at[i, side, s], r.sr.at[i, side, s], dp=onward[side],
            ))

    def scatter_end(i):
        k, col = i // 2, (i % 2) * scatter_span
        at = pl.ds(col, scatter_span)
        total = r.grads[k, chip, :, at].astype(F32)
        for side in (0, 1):
            spot = r.rbuf.at[k, side, top - 1, :, at]
            remote(
                spot, spot, r.ss.at[i, side, top - 1], r.sr.at[i, side, top - 1], dp=onward[side]
            ).wait_recv()
            total = total + spot[...].astype(F32)
        if k == 0:
            r.g_fc2[:, at] = total
        elif k == 1:
            r.g_fc1[:, at] = total
        else:
            for piece in range(scatter_span // heads):
                value = total[:, piece * heads : (piece + 1) * heads]
                which = col // heads + piece
                if which < 3:
                    r.g_qkv[which] = value
                else:
                    r.g_out[...] = value

    def grad_tile(k, column, size, terms):
        total = None
        for lhs, rhs in terms:
            part = mm(lhs.reshape(chips * rows, row_count), rhs)
            total = part if total is None else total + part
        r.grads[k, :, :, pl.ds(column, size)] = total.reshape(chips, rows, size).astype(BF16)

    chunk = 32

    def row_loop(fn, carry=()):
        def step(i, c):
            return fn(pl.ds(pl.multiple_of(i * chunk, chunk), chunk), i * chunk, c)
        return lax.fori_loop(0, row_count // chunk, step, carry)

    def fold(value):
        return jnp.sum(value.reshape(chunk // 8, 8, value.shape[1]), axis=0)

    def transposed(k, source):
        per = 2 * rows
        for c in range(chips):
            flipped = source[:, c * per : (c + 1) * per].T
            r.xt[k, 0, c] = flipped[:rows]
            r.xt[k, 1, c] = flipped[rows:]
        swap(k, r.xt.at[k, 1 - core], r.xtp.at[k])

    start_item(0)
    start_item(1)
    start_item(2)
    ends = []
    for j in range(r.lens.shape[0]):
        ends.append(r.lens[j] if j == 0 else ends[-1] + r.lens[j])
    at_row = lax.broadcasted_iota(jnp.int32, (row_count, row_count), 0)
    at_col = lax.broadcasted_iota(jnp.int32, (row_count, row_count), 1)
    seg_row = sum((at_row >= e).astype(jnp.int32) for e in ends)
    seg_col = sum((at_col >= e).astype(jnp.int32) for e in ends)
    allowed = (seg_row == seg_col) & (at_row >= at_col)
    r.mask[...] = allowed.astype(F32)
    r.vec[...] = jnp.zeros_like(r.vec)

    def is_live(first):
        return first + lax.broadcasted_iota(jnp.int32, (chunk, width), 0) < ends[-1]

    def first_norm(at, first, c):
        x = r.tok[at, :].astype(F32)
        x = x - jnp.mean(x, axis=1, keepdims=True)
        inv = lax.rsqrt(jnp.mean(x * x, axis=1, keepdims=True) + NORM_EPS)
        x = x * inv
        r.xh1[at, :] = x
        r.rs1[at, :] = inv
        r.n1[at, :] = (x * r.gain[0:1, :] + r.shift[0:1, :]).astype(BF16)
        g = jnp.where(is_live(first), r.cot[at, :].astype(F32), 0.0)
        r.gy[at, :] = g.astype(BF16)
        return (c[0] + fold(g),)

    (total,) = row_loop(first_norm, (jnp.zeros((8, width), F32),))
    r.vec[8:9, :] = jnp.sum(total, axis=0, keepdims=True)
    transposed(0, r.n1)
    transposed(1, r.gy)

    hop_item(0, 1)
    hop_item(1, 1)
    start_item(3)
    hop_item(0, 2)
    hop_item(1, 2)
    start_item(4)
    hop_item(0, 3)
    hop_item(1, 3)
    hop_item(2, 1)
    start_item(5)
    hop_item(0, 4)
    hop_item(1, 4)
    finish_item(0)

    for i in range(3):
        part = mm(r.n1[...], r.wq[:, i].reshape(width, heads))
        if i != 1:
            part = part + r.b_qv[i // 2 : i // 2 + 1, :]
        r.qkv[i] = part.astype(BF16)
    hop_item(3, 1)
    lane = lax.broadcasted_iota(jnp.int32, (1, 2 * HEAD_DIM), 1)
    picks = [(lane // HEAD_DIM == j).astype(F32).astype(BF16) for j in (0, 1)]
    first_half = lax.broadcasted_iota(jnp.int32, (row_count, 2 * HEAD_DIM), 1) < HEAD_DIM
    pairs = heads // (2 * HEAD_DIM)
    scale = HEAD_DIM ** (-0.5)
    between = [(2, 2), (4, 1), (3, 2), (5, 1)]
    for p in range(pairs):
        at = pl.ds(p * 2 * HEAD_DIM, 2 * HEAD_DIM)
        q, k, v = r.qkv[0, :, at], r.qkv[1, :, at], r.qkv[2, :, at]
        mixed = []
        for j in (0, 1):
            s = mm(q * picks[j], k, ((1,), (1,))) * scale
            s = jnp.where(r.mask[...] > 0.5, s, -1e30)
            e = jnp.exp(s - jnp.max(s, axis=1, keepdims=True))
            e = e / jnp.sum(e, axis=1, keepdims=True)
            r.pf[2 * p + j] = e
            mixed.append(mm(e.astype(BF16), v))
        r.o[:, at] = jnp.where(first_half, mixed[0], mixed[1]).astype(BF16)
        hop_item(*between[p])
    finish_item(1)
    for c in range(4):
        w = r.wo[c * group : (c + 1) * group].reshape(quarter, heads)
        r.ysend[0, :, pl.ds(c * quarter, quarter)] = mm(r.o[...], w, ((1,), (1,))).astype(BF16)
        exchange(0, c)
    swap(8, r.o, r.op)
    hop_item(2, 3)
    hop_item(3, 3)
    hop_item(4, 2)
    hop_item(2, 4)
    hop_item(3, 4)
    exchanged(0)

    def second_norm(at, first, c):
        x = r.tok[at, :].astype(F32)
        x = x + (r.ysend[0, at, :].astype(F32) + r.yrecv[0, at, :].astype(F32)) + r.b_out[...]
        r.h1[at, :] = x
        x = x - jnp.mean(x, axis=1, keepdims=True)
        inv = lax.rsqrt(jnp.mean(x * x, axis=1, keepdims=True) + NORM_EPS)
        x = x * inv
        r.xh2[at, :] = x
        r.rs2[at, :] = inv
        r.n2[at, :] = (x * r.gain[1:2, :] + r.shift[1:2, :]).astype(BF16)
        return c

    row_loop(second_norm)
    transposed(2, r.n2)
    hop_item(5, 2)
    finish_item(2)
    finish_item(3)

    tile = hidden // 4
    later = [(4, 3), (5, 3), (4, 4), (5, 4)]
    for t in range(4):
        at = pl.ds(t * tile, tile)
        r.u[:, at] = mm(r.n2[...], r.wf1[:, :, at].reshape(width, tile)) + r.b_fc1[:, at]

        def gelu(rows_at, first, c):
            u = r.u[rows_at, at]
            t_ = jnp.tanh(GELU_COEF * (u + GELU_CUBE * u * u * u))
            r.z[rows_at, at] = (0.5 * u * (1.0 + t_)).astype(BF16)
            r.u[rows_at, at] = 0.5 * (1.0 + t_) + 0.5 * u * (1.0 - t_ * t_) * GELU_COEF * (
                1.0 + 3.0 * GELU_CUBE * u * u
            )
            return c

        row_loop(gelu)
        if t % 2 == 1:
            cols = pl.ds((t // 2) * half_hidden, half_hidden)
            swap(4 + t // 2, r.z.at[:, cols], r.zp.at[:, cols])
        hop_item(*later[t])
    swapped(1, r.xtp.at[1])
    for h in (0, 1):
        cols = pl.ds(h * half_hidden, half_hidden)
        swapped(4 + h, r.zp.at[:, cols])
        for t in (2 * h, 2 * h + 1):
            at = pl.ds(t * tile, tile)
            grad_tile(0, t * tile, tile, ((r.xt[1, core], r.z[:, at]), (r.xtp[1], r.zp[:, at])))
        scatter_start(h)
    finish_item(4)
    finish_item(5)
    for t in range(4):
        at = pl.ds(t * tile, tile)
        d = mm(r.gy[...], r.wf2[:, :, at].reshape(width, tile)) * r.u[:, at]
        d = d.astype(BF16)
        r.du[:, at] = d
        row, col = (t * tile) // width, (t * tile) % width
        r.vec[6 + row : 7 + row, col : col + tile] = jnp.sum(
            d.astype(F32), axis=0, keepdims=True
        )
        if t % 2 == 1:
            cols = pl.ds((t // 2) * half_hidden, half_hidden)
            swap(6 + t // 2, r.du.at[:, cols], r.dup.at[:, cols])
    for c in range(4):
        w = r.wf1[c * group : (c + 1) * group].reshape(quarter, hidden)
        r.ysend[1, :, pl.ds(c * quarter, quarter)] = mm(r.du[...], w, ((1,), (1,))).astype(BF16)
        exchange(1, c)
    scatter_step(0, 1)
    swapped(2, r.xtp.at[2])
    for h in (0, 1):
        cols = pl.ds(h * half_hidden, half_hidden)
        swapped(6 + h, r.dup.at[:, cols])
        for t in (2 * h, 2 * h + 1):
            at = pl.ds(t * tile, tile)
            grad_tile(1, t * tile, tile, ((r.xt[2, core], r.du[:, at]), (r.xtp[2], r.dup[:, at])))
        scatter_start(2 + h)
        if h == 0:
            scatter_step(1, 1)
    for c in range(4):
        w = r.wf2[c * group : (c + 1) * group].reshape(quarter, hidden)
        r.ysend[2, :, pl.ds(c * quarter, quarter)] = mm(r.z[...], w, ((1,), (1,))).astype(BF16)
        exchange(2, c)
    scatter_step(0, 2)
    exchanged(1)

    def norm_back(k, gain_row, xh, rs, above, store):
        def step(at, first, c):
            dn = r.ysend[k, at, :].astype(F32) + r.yrecv[k, at, :].astype(F32)
            x = xh[at, :]
            scaled = dn * r.gain[gain_row : gain_row + 1, :]
            m1 = jnp.mean(scaled, axis=1, keepdims=True)
            m2 = jnp.mean(scaled * x, axis=1, keepdims=True)
            g = above[at, :].astype(F32) + rs[at, :] * (scaled - m1 - x * m2)
            store(at, g)
            return (c[0] + fold(dn * x), c[1] + fold(dn), c[2] + fold(g))

        zero = jnp.zeros((8, width), F32)
        return [jnp.sum(s, axis=0, keepdims=True) for s in row_loop(step, (zero, zero, zero))]

    def store_gh1(at, g):
        r.gh1[at, :] = g
        r.ghb[at, :] = g.astype(BF16)

    sums = norm_back(1, 1, r.xh2, r.rs2, r.gy, store_gh1)
    r.vec[1:2, :] = sums[0]
    r.vec[3:4, :] = sums[1]
    r.vec[5:6, :] = sums[2]
    transposed(3, r.ghb)
    scatter_step(1, 2)

    r.dh[...] = mm(r.ghb[...], r.wo[...].reshape(width, heads)).astype(BF16)
    scatter_step(2, 1)
    steps = [(0, 3), (1, 3), (3, 1), (2, 2)]
    for p in range(pairs):
        at = pl.ds(p * 2 * HEAD_DIM, 2 * HEAD_DIM)
        q, k, v = r.qkv[0, :, at], r.qkv[1, :, at], r.qkv[2, :, at]
        d_out, o = r.dh[:, at], r.o[:, at]
        parts = []
        for j in (0, 1):
            mine = d_out * picks[j]
            delta = jnp.sum(mine.astype(F32) * o.astype(F32), axis=1, keepdims=True)
            prob = r.pf[2 * p + j]
            ds = (prob * (mm(mine, v, ((1,), (1,))) - delta) * scale).astype(BF16)
            parts.append((
                mm(ds, k),
                mm(ds, q, ((0,), (0,))),
                mm(prob.astype(BF16), d_out, ((0,), (0,))),
            ))
        for i in range(3):
            r.dqkv[i, :, at] = jnp.where(first_half, parts[0][i], parts[1][i]).astype(BF16)
        scatter_step(*steps[p])
    swap(9, r.dqkv, r.dqkvp)
    for c in range(4):
        total = None
        for i in range(3):
            w = r.wq[c * group : (c + 1) * group, i].reshape(quarter, heads)
            part = mm(r.dqkv[i], w, ((1,), (1,)))
            total = part if total is None else total + part
        r.ysend[3, :, pl.ds(c * quarter, quarter)] = total.astype(BF16)
        exchange(3, c)
    for i in (0, 2):
        r.vec[4:5, pl.ds((i // 2) * heads, heads)] = jnp.sum(
            r.dqkv[i].astype(F32), axis=0, keepdims=True
        )
    swapped(0, r.xtp.at[0])
    swapped(9, r.dqkvp)
    scatter_step(3, 2)
    for i in (0, 1):
        grad_tile(2, i * heads, heads, ((r.xt[0, core], r.dqkv[i]), (r.xtp[0], r.dqkvp[i])))
    scatter_start(4)
    grad_tile(2, 2 * heads, heads, ((r.xt[0, core], r.dqkv[2]), (r.xtp[0], r.dqkvp[2])))
    swapped(3, r.xtp.at[3])
    swapped(8, r.op)
    grad_tile(2, 3 * heads, heads, ((r.xt[3, core], r.o[...]), (r.xtp[3], r.op[...])))
    scatter_start(5)
    scatter_step(2, 3)
    scatter_step(3, 3)
    scatter_end(0)
    scatter_end(1)
    scatter_step(4, 1)
    scatter_step(5, 1)

    exchanged(2)

    def finish_output(at, first, c):
        y = r.h1[at, :] + (r.ysend[2, at, :].astype(F32) + r.yrecv[2, at, :].astype(F32))
        y = jnp.where(is_live(first), y + r.b_fc2[...], 0.0)
        r.y[at, :] = y.astype(BF16)
        return c

    row_loop(finish_output)
    exchanged(3)

    def store_tokens(at, g):
        r.g_tok[at, :] = g

    sums = norm_back(3, 0, r.xh1, r.rs1, r.gh1, store_tokens)
    r.vec[0:1, :] = sums[0]
    r.vec[2:3, :] = sums[1]

    def tile_of(ref, dev):
        return ref.at[
            pl.ds(pl.multiple_of(8 * (dev % 2), 8), 8),
            pl.ds(pl.multiple_of(128 * (dev // 2), 128), 128),
        ]

    for j in range(1, count):
        peer = lax.rem(device + j, count)
        go(remote(
            tile_of(r.vec, peer), r.vslots.at[device], r.vs.at[0, j], r.vr.at[0, j], dp=peer
        ))
    r.vslots[device] = tile_of(r.vec, device)[...]
    scatter_step(4, 2)
    scatter_step(5, 2)
    scatter_end(2)
    scatter_end(3)
    for j in range(1, count):
        spot = r.vslots.at[lax.rem(device + count - j, count)]
        remote(spot, spot, r.vs.at[0, j], r.vr.at[0, j], dp=partner).wait_recv()
    mine = tile_of(r.vres, device)
    mine[...] = jnp.sum(r.vslots[...], axis=0)
    for j in range(1, count):
        go(remote(mine, mine, r.vs.at[1, j], r.vr.at[1, j], dp=lax.rem(device + j, count)))
    scatter_step(4, 3)
    scatter_step(5, 3)
    for j in range(1, count):
        spot = tile_of(r.vres, lax.rem(device + count - j, count))
        remote(spot, spot, r.vs.at[1, j], r.vr.at[1, j], dp=partner).wait_recv()
    r.o_gain[...] = r.vres[0:2, :]
    r.o_shift[...] = r.vres[2:4, :]
    r.o_bqv[0:1, :] = r.vres[4:5, :heads]
    r.o_bqv[1:2, :] = r.vres[4:5, heads : 2 * heads]
    r.o_bout[...] = r.vres[5:6, :]
    for j in range(hidden // width):
        r.o_bfc1[:, pl.ds(j * width, width)] = r.vres[6 + j : 7 + j, :]
    r.o_bfc2[...] = r.vres[8:9, :]
    scatter_end(4)
    scatter_end(5)
    for copy in started:
        copy.wait_send()


def one_kernel(tokens, cotangent, seq_lens, gain, shift, w_qkv, b_qv, w_out, b_out, w_fc1, b_fc1, w_fc2, b_fc2):
    chips = lax.axis_size("dp") // 2
    row_count, width = tokens.shape
    rows, heads = w_out.shape
    hidden = w_fc1.shape[1]
    vmem, hbm = pl.BlockSpec(memory_space=pltpu.VMEM), pl.BlockSpec(memory_space=pl.ANY)
    smem = pl.BlockSpec(memory_space=pltpu.SMEM)
    scratch = layer_scratch(chips, rows, row_count, width, heads, hidden)
    names = list(scratch)

    def made(*shape, kind=F32):
        return jax.ShapeDtypeStruct(shape, kind)

    outs = pl.pallas_call(
        lambda *refs: layer_kernel(chips, names, *refs),
        out_shape=(
            made(row_count, width, kind=BF16), made(row_count, width), made(2, width),
            made(2, width), made(3, rows, heads), made(2, heads), made(rows, heads),
            made(1, width), made(rows, hidden), made(1, hidden), made(rows, hidden),
            made(1, width),
        ),
        in_specs=[vmem, vmem, smem, vmem, vmem, hbm, vmem, hbm, vmem, hbm, vmem, hbm, vmem],
        out_specs=(vmem,) * 12,
        scratch_shapes=list(scratch.values()),
        compiler_params=pltpu.CompilerParams(
            collective_id=2, has_side_effects=True, vmem_limit_bytes=63 * 2**20
        ),
        name="layer",
    )(
        tokens, cotangent, seq_lens, gain, shift, w_qkv, b_qv, w_out, b_out[None], w_fc1,
        b_fc1[None], w_fc2, b_fc2[None],
    )
    outs = list(outs)
    for i in (7, 9, 11):
        outs[i] = outs[i].reshape(-1)
    return tuple(outs)


def fits_one_kernel(tokens, w_out, w_fc1):
    chips = lax.axis_size("dp") // 2
    rows, heads = w_out.shape
    width, hidden = tokens.shape[1], w_fc1.shape[1]
    return (
        lax.axis_size("tensor") == 2
        and 4 <= chips <= 8
        and chips % 2 == 0
        and width == 128 * chips
        and rows % 16 == 0
        and tokens.shape[0] % 32 == 0
        and 2 * heads == width
        and 4 * heads == hidden
    )


def body(
    tokens,
    cotangent,
    seq_lens,
    layer_norm_gain,
    layer_norm_bias,
    w_qkv,
    b_qv,
    w_out,
    b_out,
    w_fc1,
    b_fc1,
    w_fc2,
    b_fc2,
):
    if fits_one_kernel(tokens, w_out, w_fc1):
        return one_kernel(
            tokens, cotangent, seq_lens, layer_norm_gain, layer_norm_bias, w_qkv, b_qv, w_out,
            b_out, w_fc1, b_fc1, w_fc2, b_fc2,
        )
    heads_width, hidden_width = w_out.shape[1], w_fc1.shape[1]
    attn_shards = jnp.concatenate([w_qkv[0], w_qkv[1], w_qkv[2], w_out], axis=1)
    mlp_shards = jnp.concatenate([w_fc1, w_fc2], axis=1)
    mlp_full = lax.all_gather(mlp_shards, "dp", axis=0, tiled=True)
    attn_full = gather_rows(attn_shards)
    qkv_full, out_full = attn_full[:, : 3 * heads_width], attn_full[:, 3 * heads_width :]
    fc1_full, fc2_full = mlp_full[:, :hidden_width], mlp_full[:, hidden_width:]
    allowed, live_rows = seq_masks(seq_lens, tokens.shape[0])
    input_tokens = tokens.astype(jnp.float32)
    first_normalized, first_centered_scaled, first_inverse_deviation = layer_norm_forward(
        input_tokens, layer_norm_gain[0], layer_norm_bias[0]
    )
    low1 = first_normalized.astype(jnp.bfloat16)
    proj = product("td,dc->tc", low1, qkv_full)
    query = (proj[:, :heads_width] + b_qv[0]).astype(jnp.bfloat16)
    key_rows = proj[:, heads_width : 2 * heads_width].astype(jnp.bfloat16)
    value = (proj[:, 2 * heads_width :] + b_qv[1]).astype(jnp.bfloat16)
    heads_out, logsum = attend(query, key_rows, value, allowed)
    attn_part = product("tc,dc->td", heads_out, out_full)
    attn_mix = sum_tensor(attn_part)
    first_hidden_state = input_tokens + attn_mix + b_out
    second_normalized, second_centered_scaled, second_inverse_deviation = layer_norm_forward(
        first_hidden_state, layer_norm_gain[1], layer_norm_bias[1]
    )
    low2 = second_normalized.astype(jnp.bfloat16)
    pre_act = jnp.dot(low2, fc1_full, preferred_element_type=jnp.float32) + b_fc1
    act, slope = gelu_parts(pre_act)
    act_low = act.astype(jnp.bfloat16)
    mlp_part = product("tf,df->td", act_low, fc2_full)
    mlp_mix = sum_tensor(mlp_part)
    result = first_hidden_state + mlp_mix + b_fc2
    output = jnp.where(live_rows[:, None], result, 0.0).astype(jnp.bfloat16)
    qkv_back, out_back, fc1_back, fc2_back = (qkv_full, out_full, fc1_full, fc2_full)
    grad_y = jnp.where(live_rows[:, None], cotangent, jnp.zeros_like(cotangent))
    flat_output_gradient = grad_y.astype(jnp.float32)
    d_pre = (jnp.dot(grad_y, fc2_back, preferred_element_type=jnp.float32) * slope).astype(
        jnp.bfloat16
    )
    g_fc2 = product("td,tf->df", grad_y, act_low)
    g_bfc2 = jnp.sum(flat_output_gradient, axis=0)
    g_fc1 = product("td,tf->df", low2, d_pre)
    g_mlp = jnp.concatenate([g_fc1.astype(jnp.bfloat16), g_fc2.astype(jnp.bfloat16)], axis=1)
    shard_mlp = lax.psum_scatter(g_mlp, "dp", scatter_dimension=0, tiled=True)
    g_bfc1 = jnp.sum(d_pre.astype(jnp.float32), axis=0)
    d_norm2_part = product("tf,df->td", d_pre, fc1_back)
    second_norm_delta = sum_tensor(d_norm2_part)
    second_gain_gradient = jnp.sum(second_norm_delta * second_centered_scaled, axis=0)
    g_shift2 = jnp.sum(second_norm_delta, axis=0)
    hidden_first_gradient = flat_output_gradient + layer_norm_backward(
        second_norm_delta, layer_norm_gain[1], second_centered_scaled, second_inverse_deviation
    )
    grad_low = hidden_first_gradient.astype(jnp.bfloat16)
    g_out = product("td,tc->dc", grad_low, heads_out)
    g_bout = jnp.sum(hidden_first_gradient, axis=0)
    d_heads = jnp.dot(grad_low, out_back, preferred_element_type=jnp.float32).astype(jnp.bfloat16)
    d_query, d_key, d_value = attend_back(
        query, key_rows, value, heads_out, d_heads, logsum, allowed
    )
    stacked = jnp.concatenate([d_query, d_key, d_value], axis=1)
    g_qkv = product("td,tc->dc", low1, stacked)
    g_attn = jnp.concatenate([g_qkv.astype(jnp.bfloat16), g_out.astype(jnp.bfloat16)], axis=1)
    g_bqv = jnp.stack(
        [jnp.sum(d_query.astype(jnp.float32), axis=0), jnp.sum(d_value.astype(jnp.float32), axis=0)]
    )
    d_norm1_part = product("tc,dc->td", stacked, qkv_back)
    first_norm_delta = sum_tensor(d_norm1_part)
    first_gain_gradient = jnp.sum(first_norm_delta * first_centered_scaled, axis=0)
    g_shift1 = jnp.sum(first_norm_delta, axis=0)
    input_gradient = hidden_first_gradient + layer_norm_backward(
        first_norm_delta, layer_norm_gain[0], first_centered_scaled, first_inverse_deviation
    )
    shard_mlp = shard_mlp.astype(jnp.float32)
    shard_fc1, shard_fc2 = shard_mlp[:, :hidden_width], shard_mlp[:, hidden_width:]
    vectors = jnp.concatenate(
        [
            first_gain_gradient,
            second_gain_gradient,
            g_shift1,
            g_shift2,
            g_bqv.reshape(-1),
            g_bout,
            g_bfc1,
            g_bfc2,
        ]
    )
    shard_attn, vectors = scatter_rows(g_attn, vectors)
    shard_qkv = jnp.stack([shard_attn[:, i * heads_width : (i + 1) * heads_width] for i in range(3)])
    shard_out = shard_attn[:, 3 * heads_width :]
    width = tokens.shape[1]
    cuts = [2 * width, 4 * width, 4 * width + 2 * heads_width]
    cuts += [cuts[-1] + width, cuts[-1] + width + hidden_width]
    gain_sum, shift_sum, bqv_sum, bout_sum, bfc1_sum, bfc2_sum = jnp.split(vectors, cuts)
    gain_sum, shift_sum = gain_sum.reshape(2, width), shift_sum.reshape(2, width)
    bqv_sum = bqv_sum.reshape(2, heads_width)
    return (
        output,
        input_gradient,
        gain_sum,
        shift_sum,
        shard_qkv,
        bqv_sum,
        shard_out,
        bout_sum,
        shard_fc1,
        bfc1_sum,
        shard_fc2,
        bfc2_sum,
    )


def solution(mesh):
    in_specs = (
        P("dp", None),
        P("dp", None),
        P("dp"),
        P(),
        P(),
        P(None, "dp", "tensor"),
        P(None, "tensor"),
        P("dp", "tensor"),
        P(),
        P("dp", "tensor"),
        P("tensor"),
        P("dp", "tensor"),
        P(),
    )
    out_specs = (
        P("dp", None),
        P("dp", None),
        P(),
        P(),
        P(None, "dp", "tensor"),
        P(None, "tensor"),
        P("dp", "tensor"),
        P(),
        P("dp", "tensor"),
        P("tensor"),
        P("dp", "tensor"),
        P(),
    )
    return jax.shard_map(body, mesh=mesh, in_specs=in_specs, out_specs=out_specs, check_vma=False)
```

```python
import jax
import jax.numpy as jnp
from jax import lax
from jax.experimental import pallas as pl
from jax.experimental.pallas import tpu as pltpu
from jax.sharding import PartitionSpec as P

HEAD_DIM = 64


NORM_EPS = 1e-05
GELU_COEF = 0.7978845608028654


def product(spec, left, right):
    return jnp.einsum(spec, left, right, preferred_element_type=jnp.float32)


def seq_masks(lengths, row_count):
    slots = jnp.arange(lengths.shape[0])
    ends = jnp.sum(jnp.where(slots[:, None] <= slots[None, :], lengths[:, None], 0), axis=0)
    places = jnp.arange(row_count, dtype=jnp.int32)
    segment = jnp.sum((places[:, None] >= ends[None, :]).astype(jnp.int32), axis=1)
    allowed = (segment[:, None] == segment[None, :]) & (places[:, None] >= places[None, :])
    live_rows = places < ends[-1]
    return (allowed, live_rows)


def layer_norm_forward(hidden, gain, shift):
    center = hidden - jnp.mean(hidden, axis=-1, keepdims=True)
    inv_std = lax.rsqrt(jnp.mean(center * center, axis=-1, keepdims=True) + NORM_EPS)
    normal_x = center * inv_std
    return (normal_x * gain + shift, normal_x, inv_std)


def layer_norm_backward(grad_out, gain, normal_x, inv_std):
    scaled = grad_out * gain
    return inv_std * (
        scaled
        - jnp.mean(scaled, axis=-1, keepdims=True)
        - normal_x * jnp.mean(scaled * normal_x, axis=-1, keepdims=True)
    )


def gelu_parts(pre_act):
    inner = GELU_COEF * (pre_act + 0.044715 * pre_act * pre_act * pre_act)
    tanh_val = jnp.tanh(inner)
    value = 0.5 * pre_act * (1.0 + tanh_val)
    slope = 0.5 * (1.0 + tanh_val) + 0.5 * pre_act * (1.0 - tanh_val * tanh_val) * GELU_COEF * (
        1.0 + 3.0 * 0.044715 * pre_act * pre_act
    )
    return (value, slope)


def split_heads(matrix):
    return matrix.reshape(matrix.shape[0], matrix.shape[1] // HEAD_DIM, HEAD_DIM)


def head_scores(query, key_rows, allowed):
    scores = product("qhd,khd->hqk", split_heads(query), split_heads(key_rows)) * HEAD_DIM ** (-0.5)
    return jnp.where(allowed[None], scores, -1e30)


def attend(query, key_rows, value, allowed):
    scores = head_scores(query, key_rows, allowed)
    row_max = jnp.max(scores, axis=-1, keepdims=True)
    logsum = row_max + jnp.log(jnp.sum(jnp.exp(scores - row_max), axis=-1, keepdims=True))
    weights = jnp.exp(scores - logsum).astype(jnp.bfloat16)
    mixed = product("hqk,khd->qhd", weights, split_heads(value)).astype(jnp.bfloat16)
    return (mixed.reshape(query.shape[0], -1), logsum)


def attend_back(query, key_rows, value, heads_out, d_heads, logsum, allowed):
    scores = head_scores(query, key_rows, allowed)
    probs = jnp.exp(scores - logsum)
    probs_low = probs.astype(jnp.bfloat16)
    d_split = split_heads(d_heads)
    d_prob = product("qhd,khd->hqk", d_split, split_heads(value))
    delta = jnp.sum(
        d_split.astype(jnp.float32) * split_heads(heads_out).astype(jnp.float32), axis=-1
    )
    d_score = (probs * (d_prob - jnp.transpose(delta)[:, :, None]) * HEAD_DIM ** (-0.5)).astype(
        jnp.bfloat16
    )
    d_query = product("hqk,khd->qhd", d_score, split_heads(key_rows)).astype(jnp.bfloat16)
    d_key = product("hqk,qhd->khd", d_score, split_heads(query)).astype(jnp.bfloat16)
    d_value = product("hqk,qhd->khd", probs_low, d_split).astype(jnp.bfloat16)
    row_count = query.shape[0]
    return (
        d_query.reshape(row_count, -1),
        d_key.reshape(row_count, -1),
        d_value.reshape(row_count, -1),
    )


def sum_tensor(part):
    low = lax.optimization_barrier(part.astype(jnp.bfloat16))
    count = lax.axis_size("tensor")
    if count != 2:
        return lax.psum(low, "tensor").astype(jnp.float32)
    other = lax.ppermute(low, "tensor", [(0, 1), (1, 0)])
    return low.astype(jnp.float32) + other.astype(jnp.float32)


def chip_at(place, chips):
    place = (place + chips) % chips
    back = place // (chips // 2)
    return 2 * (place * (1 - back) + (chips - 1 - place) * back) + back


def ring_place(chips):
    device = lax.axis_index("dp")
    core, chip = device % 2, device // 2
    column, row = chip % 2, chip // 2
    place = row * (1 - column) + (chips - 1 - row) * column
    return device, chip, core, place


def send(source, target, send_sem, recv_sem, device):
    return pltpu.make_async_remote_copy(
        src_ref=source,
        dst_ref=target,
        send_sem=send_sem,
        recv_sem=recv_sem,
        device_id={"dp": device},
        device_id_type=pl.DeviceIdType.MESH,
    )


def meet(devices):
    barrier = pltpu.get_barrier_semaphore()
    for device in devices:
        pl.semaphore_signal(
            barrier, inc=1, device_id={"dp": device}, device_id_type=pl.DeviceIdType.MESH
        )
    pl.semaphore_wait(barrier, len(devices))


def gather_kernel(chips, own, out, rs, rr, ls, lr, ps, pr, own_sem):
    device, chip, core, place = ring_place(chips)
    right = 2 * chip_at(place + 1, chips) + core
    left = 2 * chip_at(place - 1, chips) + core
    partner = 2 * chip + 1 - core
    meet((right, left, partner))
    top, width = chips // 2, own.shape[1]
    half = width // 2

    def block(step, whose, hop, side):
        at = out.at[2 * chip_at(place + step, chips) + whose]
        if hop < top:
            return at
        return at.at[:, pl.ds(side * half, half)]

    started = []

    def go(copy):
        copy.start()
        started.append(copy)

    go(send(own, out.at[device], rs.at[0], rr.at[0], right))
    go(send(own, out.at[device], ls.at[0], lr.at[0], left))
    go(send(own, out.at[device], ps.at[0], pr.at[0], partner))
    keep = pltpu.make_async_copy(own, out.at[device], own_sem)
    keep.start()
    passed = [block(0, 1 - core, 0, 0)]
    for hop in range(1, top + 1):
        for side, sign, s_sem, r_sem, onward in ((0, -1, rs, rr, right), (1, 1, ls, lr, left)):
            here = block(sign * hop, core, hop, side)
            send(here, here, s_sem.at[hop - 1], r_sem.at[hop - 1], onward).wait_recv()
            if hop < top:
                part = block(sign * hop, core, hop + 1, side)
                go(send(part, part, s_sem.at[hop], r_sem.at[hop], onward))
            slot = len(passed)
            go(send(here, here, ps.at[slot], pr.at[slot], partner))
            passed.append(block(sign * hop, 1 - core, hop, side))
    for slot, here in enumerate(passed):
        send(here, here, ps.at[slot], pr.at[slot], partner).wait_recv()
    for copy in started:
        copy.wait_send()
    keep.wait()


def gather_rows(shard):
    count = lax.axis_size("dp")
    chips = count // 2
    top = chips // 2
    dma = pltpu.SemaphoreType.DMA
    out = pl.pallas_call(
        lambda *refs: gather_kernel(chips, *refs),
        out_shape=jax.ShapeDtypeStruct((count, *shard.shape), shard.dtype),
        in_specs=[pl.BlockSpec(memory_space=pltpu.VMEM)],
        out_specs=pl.BlockSpec(memory_space=pl.ANY),
        scratch_shapes=[dma((top,))] * 4 + [dma((chips + 1,))] * 2 + [dma],
        compiler_params=pltpu.CompilerParams(collective_id=0, has_side_effects=True),
        name="gather_rows",
    )(shard)
    return out.reshape(count * shard.shape[0], shard.shape[1])


def scatter_kernel(
    chips, grads, vec, out, vec_out,
    pbuf, rbuf, lbuf, rstage, lstage, vpart, vslots,
    ps, pr, rs, rr, ls, lr, vps, vpr, vrs, vrr, vls, vlr,
):
    device, chip, core, place = ring_place(chips)
    right = 2 * chip_at(place + 1, chips) + core
    left = 2 * chip_at(place - 1, chips) + core
    partner = 2 * chip + 1 - core
    meet((right, left, partner))
    top, width = chips // 2, out.shape[1]
    half = width // 2
    low, high = pl.ds(0, half), pl.ds(half, half)
    started = []

    def go(copy):
        copy.start()
        started.append(copy)

    order = [top]
    for step in range(1, top):
        order += [top - step, step - top]
    order.append(0)
    go(send(vec, vpart, vps.at[0], vpr.at[0], partner))
    for slot, step in enumerate(order):
        mine = grads.at[2 * chip_at(place + step, chips) + 1 - core]
        go(send(mine, pbuf.at[slot], ps.at[slot], pr.at[slot], partner))

    def pair_sum(slot):
        spot = pbuf.at[slot]
        send(spot, spot, ps.at[slot], pr.at[slot], partner).wait_recv()
        mine = grads[2 * chip_at(place + order[slot], chips) + core]
        return mine.astype(jnp.float32) + pbuf[slot].astype(jnp.float32)

    def arrived(spot, s_sem, r_sem):
        send(spot, spot, s_sem, r_sem, partner).wait_recv()

    first = pair_sum(0).astype(jnp.bfloat16)
    rstage[0, :, :half] = first[:, :half]
    go(send(rstage.at[0, :, low], rbuf.at[0, :, low], rs.at[0], rr.at[0], right))
    lstage[0, :, half:] = first[:, half:]
    go(send(lstage.at[0, :, high], lbuf.at[0, :, high], ls.at[0], lr.at[0], left))
    arrived(vpart, vps.at[0], vpr.at[0])
    vslots[chip] = vec[...] + vpart[...]
    go(send(vslots.at[chip], vslots.at[chip], vrs.at[0], vrr.at[0], right))
    go(send(vslots.at[chip], vslots.at[chip], vls.at[0], vlr.at[0], left))
    for step in range(1, top):
        for side, buf, stage, s_sem, r_sem, onward in (
            (0, rbuf, rstage, rs, rr, right),
            (1, lbuf, lstage, ls, lr, left),
        ):
            total = pair_sum(2 * step - 1 + side)
            if step == 1:
                cols = (low, high)[side]
                arrived(buf.at[0, :, cols], s_sem.at[0], r_sem.at[0])
                more = buf[0, :, side * half : (side + 1) * half].astype(jnp.float32)
                if side == 0:
                    stage[step, :, :half] = (total[:, :half] + more).astype(jnp.bfloat16)
                    stage[step, :, half:] = total[:, half:].astype(jnp.bfloat16)
                else:
                    stage[step, :, :half] = total[:, :half].astype(jnp.bfloat16)
                    stage[step, :, half:] = (total[:, half:] + more).astype(jnp.bfloat16)
            else:
                arrived(buf.at[step - 1], s_sem.at[step - 1], r_sem.at[step - 1])
                stage[step] = (total + buf[step - 1].astype(jnp.float32)).astype(jnp.bfloat16)
            go(send(stage.at[step], buf.at[step], s_sem.at[step], r_sem.at[step], onward))
        spot = vslots.at[chip_at(place - step, chips)]
        arrived(spot, vrs.at[step - 1], vrr.at[step - 1])
        go(send(spot, spot, vrs.at[step], vrr.at[step], right))
        spot = vslots.at[chip_at(place + step, chips)]
        arrived(spot, vls.at[step - 1], vlr.at[step - 1])
        if step < top - 1:
            go(send(spot, spot, vls.at[step], vlr.at[step], left))
    spot = vslots.at[chip_at(place - top, chips)]
    arrived(spot, vrs.at[top - 1], vrr.at[top - 1])
    vec_out[...] = jnp.sum(vslots[...], axis=0)
    total = pair_sum(len(order) - 1)
    arrived(rbuf.at[top - 1], rs.at[top - 1], rr.at[top - 1])
    arrived(lbuf.at[top - 1], ls.at[top - 1], lr.at[top - 1])
    out[...] = total + rbuf[top - 1].astype(jnp.float32) + lbuf[top - 1].astype(jnp.float32)
    for copy in started:
        copy.wait_send()


def scatter_rows(grads, vectors):
    count = lax.axis_size("dp")
    chips = count // 2
    top = chips // 2
    rows, width = grads.shape[0] // count, grads.shape[1]
    lines = vectors.shape[0] // 128
    dma, vmem = pltpu.SemaphoreType.DMA, pl.BlockSpec(memory_space=pltpu.VMEM)
    block = (rows, width)
    shard, sums = pl.pallas_call(
        lambda *refs: scatter_kernel(chips, *refs),
        out_shape=(
            jax.ShapeDtypeStruct(block, jnp.float32),
            jax.ShapeDtypeStruct((lines, 128), jnp.float32),
        ),
        in_specs=[vmem, vmem],
        out_specs=(vmem, vmem),
        scratch_shapes=[pltpu.VMEM((chips, *block), jnp.bfloat16)]
        + [pltpu.VMEM((top, *block), jnp.bfloat16)] * 4
        + [pltpu.VMEM((lines, 128), jnp.float32), pltpu.VMEM((chips, lines, 128), jnp.float32)]
        + [dma((chips,))] * 2
        + [dma((top,))] * 4
        + [dma((1,))] * 2
        + [dma((top,))] * 4,
        compiler_params=pltpu.CompilerParams(collective_id=1, has_side_effects=True),
        name="scatter_rows",
    )(grads.reshape(count, rows, width), vectors.reshape(lines, 128))
    return shard, sums.reshape(-1)


GELU_CUBE = 0.044715
F32, BF16 = jnp.float32, jnp.bfloat16


def mm(left, right, dims=((1,), (0,))):
    return lax.dot_general(left, right, (dims, ((), ())), preferred_element_type=F32)


class Names:
    def __init__(self, names, refs):
        for name, ref in zip(names, refs):
            setattr(self, name, ref)


STAGED = ("tok", "cot", "gain", "shift", "b_qv", "b_out", "b_fc1", "b_fc2")
IN_NAMES = [
    "far_tok", "far_cot", "lens", "far_gain", "far_shift", "w_qkv", "far_b_qv", "w_out",
    "far_b_out", "w_fc1", "far_b_fc1", "w_fc2", "far_b_fc2",
]
OUT_NAMES = ["far_y", "far_gtok", "far_gqkv", "far_gout", "far_gfc1", "far_gfc2", "far_vec"]


def layer_scratch(chips, rows, row_count, width, heads, hidden):
    count, top = 2 * chips, chips // 2
    dma = pltpu.SemaphoreType.DMA
    tall = (row_count, width)
    low = dict(
        wq=(count, 3, rows, heads), wo=(count, rows, heads),
        wf1=(count, rows, hidden), wf2=(count, rows, hidden),
        n1=tall, n2=tall, gy=tall, ghb=tall,
        z=(row_count, hidden), zp=(row_count, hidden),
        du=(row_count, hidden), dup=(row_count, hidden),
        qkv=(3, row_count, heads), o=(row_count, heads), op=(row_count, heads),
        dh=(row_count, heads),
        dqkv=(3, row_count, heads), dqkvp=(3, row_count, heads),
        xt=(4, 2, chips, rows, row_count), xtp=(4, chips, rows, row_count),
        grads=(3, chips, rows, hidden), rbuf=(3, 2, top, rows, hidden),
        ysend=(4, *tall), yrecv=(4, *tall), tok=tall, cot=tall,
    )
    full = dict(
        xh1=tall, xh2=tall, h1=tall, gh1=tall, rs1=(row_count, 1), rs2=(row_count, 1),
        u=(row_count, hidden), pf=(heads // HEAD_DIM, row_count, row_count),
        mask=(row_count, row_count), vec=(16, width), vslots=(count, 8, 128), vres=(16, width),
        gain=(2, width), shift=(2, width), b_qv=(2, heads), b_out=(1, width),
        b_fc1=(1, hidden), b_fc2=(1, width),
        g_qkv=(3, rows, heads), g_out=(rows, heads), g_fc1=(rows, hidden), g_fc2=(rows, hidden),
    )
    sems = dict(
        gs=(8, 2, top), gr=(8, 2, top), ps=(8, chips + 1), pr=(8, chips + 1),
        ss=(6, 2, top), sr=(6, 2, top), as_=(10,), ar=(10,), ys=(4, 4), yr=(4, 4),
        vs=(2, count), vr=(2, count), loc=(8,), ins=(8,), outs=(8,),
    )
    shapes = {k: pltpu.VMEM(s, BF16) for k, s in low.items()}
    shapes |= {k: pltpu.VMEM(s, F32) for k, s in full.items()}
    shapes |= {k: dma(s) for k, s in sems.items()}
    return shapes


def layer_kernel(chips, scratch_names, *refs):
    r = Names(IN_NAMES + OUT_NAMES + scratch_names, refs)
    device, chip, core, place = ring_place(chips)
    side_y = lax.axis_index("tensor")
    count, top = 2 * chips, chips // 2
    right = 2 * chip_at(place + 1, chips) + core
    left = 2 * chip_at(place - 1, chips) + core
    partner = 2 * chip + 1 - core
    onward = (right, left)
    row_count, width = r.far_tok.shape
    rows, heads = r.w_out.shape
    hidden = r.w_fc1.shape[1]
    half_hidden = hidden // 2
    started = []

    def remote(source, target, send_sem, recv_sem, **where):
        return pltpu.make_async_remote_copy(
            src_ref=source, dst_ref=target, send_sem=send_sem, recv_sem=recv_sem,
            device_id=where, device_id_type=pl.DeviceIdType.MESH,
        )

    def go(copy):
        copy.start()
        started.append(copy)

    staged = []
    for j, name in enumerate(STAGED):
        copy = pltpu.make_async_copy(getattr(r, "far_" + name), getattr(r, name), r.ins.at[j])
        copy.start()
        staged.append(copy)

    barrier = pltpu.get_barrier_semaphore()

    def greet(**where):
        pl.semaphore_signal(
            barrier, inc=1, device_id=where, device_id_type=pl.DeviceIdType.MESH
        )

    for other in (right, left, partner):
        greet(dp=other)
    greet(tensor=1 - side_y)
    pl.semaphore_wait(barrier, 4)

    base = (0, 0, 0, 0, 0, half_hidden, 0, half_hidden)
    span = (heads,) * 4 + (half_hidden,) * 4

    def cut(i, ref, side=None):
        start, size = base[i], span[i]
        if side is not None:
            size = size // 2
            start = start + side * size
        if start == 0 and size == ref.shape[-1]:
            return ref
        return ref.at[:, pl.ds(start, size)]

    def own(i):
        if i < 3:
            return r.w_qkv.at[i]
        return cut(i, (r.w_out, r.w_fc1, r.w_fc1, r.w_fc2, r.w_fc2)[i - 3])

    def spot_of(i, dev, side=None):
        if i < 3:
            return cut(i, r.wq.at[dev, i], side)
        return cut(i, (r.wo, r.wf1, r.wf1, r.wf2, r.wf2)[i - 3].at[dev], side)

    def block(i, step, whose, hop, side):
        dev = 2 * chip_at(place + step, chips) + whose
        return spot_of(i, dev, side if hop == top else None)

    def keep(i):
        return pltpu.make_async_copy(own(i), spot_of(i, device), r.loc.at[i])

    def start_item(i):
        mine, there = own(i), spot_of(i, device)
        for side in (0, 1):
            go(remote(mine, there, r.gs.at[i, side, 0], r.gr.at[i, side, 0], dp=onward[side]))
        go(remote(mine, there, r.ps.at[i, 0], r.pr.at[i, 0], dp=partner))
        keep(i).start()

    def hop_item(i, hop):
        for side, sign in ((0, -1), (1, 1)):
            here = block(i, sign * hop, core, hop, side)
            remote(
                here, here, r.gs.at[i, side, hop - 1], r.gr.at[i, side, hop - 1], dp=onward[side]
            ).wait_recv()
            if hop < top:
                part = block(i, sign * hop, core, hop + 1, side)
                go(remote(
                    part, part, r.gs.at[i, side, hop], r.gr.at[i, side, hop], dp=onward[side]
                ))
            slot = 2 * hop - 1 + side
            go(remote(here, here, r.ps.at[i, slot], r.pr.at[i, slot], dp=partner))

    def finish_item(i):
        keep(i).wait()
        for slot in range(chips + 1):
            hop, side = (slot + 1) // 2, (slot + 1) % 2
            here = block(i, (-1, 1)[side] * hop, 1 - core, hop, side)
            remote(here, here, r.ps.at[i, slot], r.pr.at[i, slot], dp=partner).wait_recv()

    def swap(k, source, target):
        go(remote(source, target, r.as_.at[k], r.ar.at[k], dp=partner))

    def swapped(k, target):
        remote(target, target, r.as_.at[k], r.ar.at[k], dp=partner).wait_recv()

    quarter = width // 4
    group = count // 4

    def exchange(k, c):
        at = pl.ds(c * quarter, quarter)
        go(remote(
            r.ysend.at[k, :, at], r.yrecv.at[k, :, at], r.ys.at[k, c], r.yr.at[k, c],
            tensor=1 - side_y,
        ))

    def exchanged(k):
        for c in range(4):
            spot = r.yrecv.at[k, :, pl.ds(c * quarter, quarter)]
            remote(spot, spot, r.ys.at[k, c], r.yr.at[k, c], tensor=1 - side_y).wait_recv()

    scatter_span = half_hidden
    half = scatter_span // 2

    def scatter_start(i):
        k, col = i // 2, (i % 2) * scatter_span
        far = r.grads.at[k, chip_at(place + top, chips)]
        for side in (0, 1):
            at = pl.ds(col + side * half, half)
            go(remote(
                far.at[:, at], r.rbuf.at[k, side, 0, :, at], r.ss.at[i, side, 0],
                r.sr.at[i, side, 0], dp=onward[side],
            ))

    def scatter_step(i, s):
        k, col = i // 2, (i % 2) * scatter_span
        for side, sign in ((0, 1), (1, -1)):
            target = chip_at(place + sign * (top - s), chips)
            at = pl.ds(col + side * half, half) if s == 1 else pl.ds(col, scatter_span)
            spot = r.rbuf.at[k, side, s - 1, :, at]
            remote(
                spot, spot, r.ss.at[i, side, s - 1], r.sr.at[i, side, s - 1], dp=onward[side]
            ).wait_recv()
            total = r.grads[k, target, :, at].astype(F32) + spot[...].astype(F32)
            r.grads[k, target, :, at] = total.astype(BF16)
            at = pl.ds(col, scatter_span)
            go(remote(
                r.grads.at[k, target, :, at], r.rbuf.at[k, side, s, :, at],
                r.ss.at[i, side, s], r.sr.at[i, side, s], dp=onward[side],
            ))

    def scatter_end(i):
        k, col = i // 2, (i % 2) * scatter_span
        at = pl.ds(col, scatter_span)
        total = r.grads[k, chip, :, at].astype(F32)
        for side in (0, 1):
            spot = r.rbuf.at[k, side, top - 1, :, at]
            remote(
                spot, spot, r.ss.at[i, side, top - 1], r.sr.at[i, side, top - 1], dp=onward[side]
            ).wait_recv()
            total = total + spot[...].astype(F32)
        if k == 0:
            r.g_fc2[:, at] = total
        elif k == 1:
            r.g_fc1[:, at] = total
        else:
            for piece in range(scatter_span // heads):
                value = total[:, piece * heads : (piece + 1) * heads]
                which = col // heads + piece
                if which < 3:
                    r.g_qkv[which] = value
                else:
                    r.g_out[...] = value

    put_copies = []

    def put(source, target):
        copy = pltpu.make_async_copy(source, target, r.outs.at[len(put_copies)])
        copy.start()
        put_copies.append(copy)

    def grad_tile(k, column, size, terms):
        total = None
        for lhs, rhs in terms:
            part = mm(lhs.reshape(chips * rows, row_count), rhs)
            total = part if total is None else total + part
        r.grads[k, :, :, pl.ds(column, size)] = total.reshape(chips, rows, size).astype(BF16)

    chunk = 32

    def row_loop(fn, carry=()):
        def step(i, c):
            return fn(pl.ds(pl.multiple_of(i * chunk, chunk), chunk), i * chunk, c)
        return lax.fori_loop(0, row_count // chunk, step, carry)

    def fold(value):
        return jnp.sum(value.reshape(chunk // 8, 8, value.shape[1]), axis=0)

    def transposed(k, source):
        per = 2 * rows
        for c in range(chips):
            flipped = source[:, c * per : (c + 1) * per].T
            r.xt[k, 0, c] = flipped[:rows]
            r.xt[k, 1, c] = flipped[rows:]
        swap(k, r.xt.at[k, 1 - core], r.xtp.at[k])

    for i in range(4):
        start_item(i)
    ends = []
    for j in range(r.lens.shape[0]):
        ends.append(r.lens[j] if j == 0 else ends[-1] + r.lens[j])
    at_row = lax.broadcasted_iota(jnp.int32, (row_count, row_count), 0)
    at_col = lax.broadcasted_iota(jnp.int32, (row_count, row_count), 1)
    seg_row = sum((at_row >= e).astype(jnp.int32) for e in ends)
    seg_col = sum((at_col >= e).astype(jnp.int32) for e in ends)
    allowed = (seg_row == seg_col) & (at_row >= at_col)
    r.mask[...] = allowed.astype(F32)
    r.vec[...] = jnp.zeros_like(r.vec)
    for copy in staged:
        copy.wait()

    def is_live(first):
        return first + lax.broadcasted_iota(jnp.int32, (chunk, width), 0) < ends[-1]

    def first_norm(at, first, c):
        x = r.tok[at, :].astype(F32)
        x = x - jnp.mean(x, axis=1, keepdims=True)
        inv = lax.rsqrt(jnp.mean(x * x, axis=1, keepdims=True) + NORM_EPS)
        x = x * inv
        r.xh1[at, :] = x
        r.rs1[at, :] = inv
        r.n1[at, :] = (x * r.gain[0:1, :] + r.shift[0:1, :]).astype(BF16)
        g = jnp.where(is_live(first), r.cot[at, :].astype(F32), 0.0)
        r.gy[at, :] = g.astype(BF16)
        return (c[0] + fold(g),)

    (total,) = row_loop(first_norm, (jnp.zeros((8, width), F32),))
    r.vec[8:9, :] = jnp.sum(total, axis=0, keepdims=True)
    for i in range(4):
        hop_item(i, 1)
    transposed(0, r.n1)
    for i in range(4):
        hop_item(i, 2)
    transposed(1, r.gy)
    for i in range(4):
        hop_item(i, 3)
    start_item(4)
    start_item(5)
    start_item(6)

    for i in range(3):
        hop_item(i, 4)
        finish_item(i)
        part = mm(r.n1[...], r.wq[:, i].reshape(width, heads))
        if i != 1:
            part = part + r.b_qv[i // 2 : i // 2 + 1, :]
        r.qkv[i] = part.astype(BF16)
    hop_item(3, 4)
    hop_item(4, 1)
    lane = lax.broadcasted_iota(jnp.int32, (1, 2 * HEAD_DIM), 1)
    picks = [(lane // HEAD_DIM == j).astype(F32).astype(BF16) for j in (0, 1)]
    first_half = lax.broadcasted_iota(jnp.int32, (row_count, 2 * HEAD_DIM), 1) < HEAD_DIM
    pairs = heads // (2 * HEAD_DIM)
    scale = HEAD_DIM ** (-0.5)
    between = [(5, 1), (6, 1), (4, 2), (5, 2)]
    for p in range(pairs):
        at = pl.ds(p * 2 * HEAD_DIM, 2 * HEAD_DIM)
        q, k, v = r.qkv[0, :, at], r.qkv[1, :, at], r.qkv[2, :, at]
        mixed = []
        for j in (0, 1):
            s = mm(q * picks[j], k, ((1,), (1,))) * scale
            s = jnp.where(r.mask[...] > 0.5, s, -1e30)
            e = jnp.exp(s - jnp.max(s, axis=1, keepdims=True))
            e = e / jnp.sum(e, axis=1, keepdims=True)
            r.pf[2 * p + j] = e
            mixed.append(mm(e.astype(BF16), v))
        r.o[:, at] = jnp.where(first_half, mixed[0], mixed[1]).astype(BF16)
        hop_item(*between[p])
    start_item(7)
    finish_item(3)
    for c in range(4):
        w = r.wo[c * group : (c + 1) * group].reshape(quarter, heads)
        r.ysend[0, :, pl.ds(c * quarter, quarter)] = mm(r.o[...], w, ((1,), (1,))).astype(BF16)
        exchange(0, c)
    swap(8, r.o, r.op)
    hop_item(4, 3)
    hop_item(5, 3)
    hop_item(6, 2)
    hop_item(7, 1)
    exchanged(0)

    def second_norm(at, first, c):
        x = r.tok[at, :].astype(F32)
        x = x + (r.ysend[0, at, :].astype(F32) + r.yrecv[0, at, :].astype(F32)) + r.b_out[...]
        r.h1[at, :] = x
        x = x - jnp.mean(x, axis=1, keepdims=True)
        inv = lax.rsqrt(jnp.mean(x * x, axis=1, keepdims=True) + NORM_EPS)
        x = x * inv
        r.xh2[at, :] = x
        r.rs2[at, :] = inv
        r.n2[at, :] = (x * r.gain[1:2, :] + r.shift[1:2, :]).astype(BF16)
        return c

    row_loop(second_norm)
    transposed(2, r.n2)
    hop_item(4, 4)
    hop_item(5, 4)
    finish_item(4)
    finish_item(5)

    tile = hidden // 4
    later = [(), (6, 3), (7, 2), (6, 4)]
    for t in range(4):
        at = pl.ds(t * tile, tile)
        r.u[:, at] = mm(r.n2[...], r.wf1[:, :, at].reshape(width, tile)) + r.b_fc1[:, at]

        def gelu(rows_at, first, c):
            u = r.u[rows_at, at]
            t_ = jnp.tanh(GELU_COEF * (u + GELU_CUBE * u * u * u))
            r.z[rows_at, at] = (0.5 * u * (1.0 + t_)).astype(BF16)
            r.u[rows_at, at] = 0.5 * (1.0 + t_) + 0.5 * u * (1.0 - t_ * t_) * GELU_COEF * (
                1.0 + 3.0 * GELU_CUBE * u * u
            )
            return c

        row_loop(gelu)
        if t % 2 == 1:
            cols = pl.ds((t // 2) * half_hidden, half_hidden)
            swap(4 + t // 2, r.z.at[:, cols], r.zp.at[:, cols])
        if later[t]:
            hop_item(*later[t])
    swapped(1, r.xtp.at[1])
    for h in (0, 1):
        cols = pl.ds(h * half_hidden, half_hidden)
        swapped(4 + h, r.zp.at[:, cols])
        for t in (2 * h, 2 * h + 1):
            at = pl.ds(t * tile, tile)
            grad_tile(0, t * tile, tile, ((r.xt[1, core], r.z[:, at]), (r.xtp[1], r.zp[:, at])))
        scatter_start(h)
        hop_item(7, 3 + h)
    finish_item(6)
    finish_item(7)
    for t in range(4):
        at = pl.ds(t * tile, tile)
        d = mm(r.gy[...], r.wf2[:, :, at].reshape(width, tile)) * r.u[:, at]
        d = d.astype(BF16)
        r.du[:, at] = d
        row, col = (t * tile) // width, (t * tile) % width
        r.vec[6 + row : 7 + row, col : col + tile] = jnp.sum(
            d.astype(F32), axis=0, keepdims=True
        )
        if t % 2 == 1:
            cols = pl.ds((t // 2) * half_hidden, half_hidden)
            swap(6 + t // 2, r.du.at[:, cols], r.dup.at[:, cols])
            scatter_step(t // 2, 1)
    for c in range(4):
        w = r.wf1[c * group : (c + 1) * group].reshape(quarter, hidden)
        r.ysend[1, :, pl.ds(c * quarter, quarter)] = mm(r.du[...], w, ((1,), (1,))).astype(BF16)
        exchange(1, c)
    scatter_step(0, 2)
    swapped(2, r.xtp.at[2])
    for h in (0, 1):
        cols = pl.ds(h * half_hidden, half_hidden)
        swapped(6 + h, r.dup.at[:, cols])
        for t in (2 * h, 2 * h + 1):
            at = pl.ds(t * tile, tile)
            grad_tile(1, t * tile, tile, ((r.xt[2, core], r.du[:, at]), (r.xtp[2], r.dup[:, at])))
        scatter_start(2 + h)
        if h == 0:
            scatter_step(1, 2)
    for j in range(1, count):
        greet(dp=lax.rem(device + j, count))
    for c in range(4):
        w = r.wf2[c * group : (c + 1) * group].reshape(quarter, hidden)
        r.ysend[2, :, pl.ds(c * quarter, quarter)] = mm(r.z[...], w, ((1,), (1,))).astype(BF16)
        exchange(2, c)
    scatter_step(0, 3)
    scatter_step(1, 3)
    scatter_step(2, 1)
    exchanged(1)

    def norm_back(k, gain_row, xh, rs, above, store):
        def step(at, first, c):
            dn = r.ysend[k, at, :].astype(F32) + r.yrecv[k, at, :].astype(F32)
            x = xh[at, :]
            scaled = dn * r.gain[gain_row : gain_row + 1, :]
            m1 = jnp.mean(scaled, axis=1, keepdims=True)
            m2 = jnp.mean(scaled * x, axis=1, keepdims=True)
            g = above[at, :].astype(F32) + rs[at, :] * (scaled - m1 - x * m2)
            store(at, g)
            return (c[0] + fold(dn * x), c[1] + fold(dn), c[2] + fold(g))

        zero = jnp.zeros((8, width), F32)
        return [jnp.sum(s, axis=0, keepdims=True) for s in row_loop(step, (zero, zero, zero))]

    def store_gh1(at, g):
        r.gh1[at, :] = g
        r.ghb[at, :] = g.astype(BF16)

    sums = norm_back(1, 1, r.xh2, r.rs2, r.gy, store_gh1)
    r.vec[1:2, :] = sums[0]
    r.vec[3:4, :] = sums[1]
    r.vec[5:6, :] = sums[2]
    transposed(3, r.ghb)
    scatter_step(3, 1)

    r.dh[...] = mm(r.ghb[...], r.wo[...].reshape(width, heads)).astype(BF16)
    steps = [(), (2, 2), (), (3, 2)]
    for p in range(pairs):
        at = pl.ds(p * 2 * HEAD_DIM, 2 * HEAD_DIM)
        q, k, v = r.qkv[0, :, at], r.qkv[1, :, at], r.qkv[2, :, at]
        d_out, o = r.dh[:, at], r.o[:, at]
        parts = []
        for j in (0, 1):
            mine = d_out * picks[j]
            delta = jnp.sum(mine.astype(F32) * o.astype(F32), axis=1, keepdims=True)
            prob = r.pf[2 * p + j]
            ds = (prob * (mm(mine, v, ((1,), (1,))) - delta) * scale).astype(BF16)
            parts.append((
                mm(ds, k),
                mm(ds, q, ((0,), (0,))),
                mm(prob.astype(BF16), d_out, ((0,), (0,))),
            ))
        for i in range(3):
            r.dqkv[i, :, at] = jnp.where(first_half, parts[0][i], parts[1][i]).astype(BF16)
        if steps[p]:
            scatter_step(*steps[p])
    swap(9, r.dqkv, r.dqkvp)
    for c in range(4):
        total = None
        for i in range(3):
            w = r.wq[c * group : (c + 1) * group, i].reshape(quarter, heads)
            part = mm(r.dqkv[i], w, ((1,), (1,)))
            total = part if total is None else total + part
        r.ysend[3, :, pl.ds(c * quarter, quarter)] = total.astype(BF16)
        exchange(3, c)
    for i in (0, 2):
        r.vec[4:5, pl.ds((i // 2) * heads, heads)] = jnp.sum(
            r.dqkv[i].astype(F32), axis=0, keepdims=True
        )
    swapped(0, r.xtp.at[0])
    swapped(9, r.dqkvp)
    scatter_step(2, 3)
    for i in (0, 1):
        grad_tile(2, i * heads, heads, ((r.xt[0, core], r.dqkv[i]), (r.xtp[0], r.dqkvp[i])))
    scatter_start(4)
    grad_tile(2, 2 * heads, heads, ((r.xt[0, core], r.dqkv[2]), (r.xtp[0], r.dqkvp[2])))
    swapped(3, r.xtp.at[3])
    swapped(8, r.op)
    grad_tile(2, 3 * heads, heads, ((r.xt[3, core], r.o[...]), (r.xtp[3], r.op[...])))
    scatter_start(5)
    scatter_step(3, 3)
    scatter_end(0)
    scatter_end(1)
    put(r.g_fc2, r.far_gfc2)

    exchanged(2)

    def finish_output(at, first, c):
        y = r.h1[at, :] + (r.ysend[2, at, :].astype(F32) + r.yrecv[2, at, :].astype(F32))
        y = jnp.where(is_live(first), y + r.b_fc2[...], 0.0)
        r.n2[at, :] = y.astype(BF16)
        return c

    row_loop(finish_output)
    put(r.n2, r.far_y)
    scatter_step(4, 1)
    scatter_step(5, 1)
    exchanged(3)

    def store_tokens(at, g):
        r.gh1[at, :] = g

    sums = norm_back(3, 0, r.xh1, r.rs1, r.gh1, store_tokens)
    r.vec[0:1, :] = sums[0]
    r.vec[2:3, :] = sums[1]
    put(r.gh1, r.far_gtok)

    def tile_of(ref, dev):
        return ref.at[
            pl.ds(pl.multiple_of(8 * (dev % 2), 8), 8),
            pl.ds(pl.multiple_of(128 * (dev // 2), 128), 128),
        ]

    pl.semaphore_wait(barrier, count - 1)
    for j in range(1, count):
        peer = lax.rem(device + j, count)
        go(remote(
            tile_of(r.vec, peer), r.vslots.at[device], r.vs.at[0, j], r.vr.at[0, j], dp=peer
        ))
    r.vslots[device] = tile_of(r.vec, device)[...]
    scatter_step(4, 2)
    scatter_step(5, 2)
    scatter_end(2)
    scatter_end(3)
    put(r.g_fc1, r.far_gfc1)
    for j in range(1, count):
        spot = r.vslots.at[lax.rem(device + count - j, count)]
        remote(spot, spot, r.vs.at[0, j], r.vr.at[0, j], dp=partner).wait_recv()
    mine = tile_of(r.vres, device)
    mine[...] = jnp.sum(r.vslots[...], axis=0)
    for j in range(1, count):
        go(remote(mine, mine, r.vs.at[1, j], r.vr.at[1, j], dp=lax.rem(device + j, count)))
    scatter_step(4, 3)
    scatter_step(5, 3)
    for j in range(1, count):
        spot = tile_of(r.vres, lax.rem(device + count - j, count))
        remote(spot, spot, r.vs.at[1, j], r.vr.at[1, j], dp=partner).wait_recv()
    put(r.vres, r.far_vec)
    scatter_end(4)
    scatter_end(5)
    put(r.g_qkv, r.far_gqkv)
    put(r.g_out, r.far_gout)
    for copy in put_copies:
        copy.wait()
    for copy in started:
        copy.wait_send()


def one_kernel(tokens, cotangent, seq_lens, gain, shift, w_qkv, b_qv, w_out, b_out, w_fc1, b_fc1, w_fc2, b_fc2):
    chips = lax.axis_size("dp") // 2
    row_count, width = tokens.shape
    rows, heads = w_out.shape
    hidden = w_fc1.shape[1]
    vmem, hbm = pl.BlockSpec(memory_space=pltpu.VMEM), pl.BlockSpec(memory_space=pl.ANY)
    smem = pl.BlockSpec(memory_space=pltpu.SMEM)
    scratch = layer_scratch(chips, rows, row_count, width, heads, hidden)
    names = list(scratch)

    def made(*shape, kind=F32):
        return jax.ShapeDtypeStruct(shape, kind)

    outs = pl.pallas_call(
        lambda *refs: layer_kernel(chips, names, *refs),
        out_shape=(
            made(row_count, width, kind=BF16), made(row_count, width), made(3, rows, heads),
            made(rows, heads), made(rows, hidden), made(rows, hidden), made(16, width),
        ),
        in_specs=[hbm, hbm, smem] + [hbm] * 10,
        out_specs=(hbm,) * 7,
        scratch_shapes=list(scratch.values()),
        compiler_params=pltpu.CompilerParams(
            collective_id=2, has_side_effects=True, vmem_limit_bytes=63 * 2**20
        ),
        name="layer",
    )(
        tokens, cotangent, seq_lens, gain, shift, w_qkv, b_qv, w_out, b_out[None], w_fc1,
        b_fc1[None], w_fc2, b_fc2[None],
    )
    small = ((2, width), (2, width), (2, heads), (1, width), (1, hidden), (1, width))
    outs = pl.pallas_call(
        lambda *refs: results_kernel(heads, *refs),
        out_shape=tuple(made(*o.shape, kind=o.dtype) for o in outs[:6])
        + tuple(made(*o) for o in small),
        in_specs=[hbm] * 6 + [vmem],
        out_specs=(hbm,) * 6 + (vmem,) * 6,
        scratch_shapes=[pltpu.VMEM(o.shape, o.dtype) for o in outs[:6]]
        + [pltpu.SemaphoreType.DMA((2, 6))],
        name="results",
    )(*outs)
    y, g_tok, g_qkv, g_out, g_fc1, g_fc2, g_gain, g_shift, g_bqv, g_bout, g_bfc1, g_bfc2 = outs
    return (
        y, g_tok, g_gain, g_shift, g_qkv, g_bqv, g_out, g_bout.reshape(-1), g_fc1,
        g_bfc1.reshape(-1), g_fc2, g_bfc2.reshape(-1),
    )


def results_kernel(heads, *refs):
    sources, vec, targets, held, sem = refs[:6], refs[6], refs[7:13], refs[19:25], refs[25]
    gain, shift, bqv, bout, bfc1, bfc2 = refs[13:19]
    order = (1, 0, 4, 5, 2, 3)
    reads = {i: pltpu.make_async_copy(sources[i], held[i], sem.at[0, i]) for i in order}
    writes = {i: pltpu.make_async_copy(held[i], targets[i], sem.at[1, i]) for i in order}
    for i in order:
        reads[i].start()
    width = vec.shape[1]
    gain[...] = vec[0:2, :]
    shift[...] = vec[2:4, :]
    bqv[0:1, :] = vec[4:5, :heads]
    bqv[1:2, :] = vec[4:5, heads : 2 * heads]
    bout[...] = vec[5:6, :]
    for j in range(bfc1.shape[1] // width):
        bfc1[:, j * width : (j + 1) * width] = vec[6 + j : 7 + j, :]
    bfc2[...] = vec[8:9, :]
    for i in order:
        reads[i].wait()
        writes[i].start()
    for i in order:
        writes[i].wait()


def fits_one_kernel(tokens, w_out, w_fc1):
    chips = lax.axis_size("dp") // 2
    rows, heads = w_out.shape
    width, hidden = tokens.shape[1], w_fc1.shape[1]
    return (
        lax.axis_size("tensor") == 2
        and chips == 2 * 4
        and width == 128 * chips
        and rows % 16 == 0
        and tokens.shape[0] % 32 == 0
        and 2 * heads == width
        and 4 * heads == hidden
    )


def body(
    tokens,
    cotangent,
    seq_lens,
    layer_norm_gain,
    layer_norm_bias,
    w_qkv,
    b_qv,
    w_out,
    b_out,
    w_fc1,
    b_fc1,
    w_fc2,
    b_fc2,
):
    if fits_one_kernel(tokens, w_out, w_fc1):
        return one_kernel(
            tokens, cotangent, seq_lens, layer_norm_gain, layer_norm_bias, w_qkv, b_qv, w_out,
            b_out, w_fc1, b_fc1, w_fc2, b_fc2,
        )
    heads_width, hidden_width = w_out.shape[1], w_fc1.shape[1]
    attn_shards = jnp.concatenate([w_qkv[0], w_qkv[1], w_qkv[2], w_out], axis=1)
    mlp_shards = jnp.concatenate([w_fc1, w_fc2], axis=1)
    mlp_full = lax.all_gather(mlp_shards, "dp", axis=0, tiled=True)
    attn_full = gather_rows(attn_shards)
    qkv_full, out_full = attn_full[:, : 3 * heads_width], attn_full[:, 3 * heads_width :]
    fc1_full, fc2_full = mlp_full[:, :hidden_width], mlp_full[:, hidden_width:]
    allowed, live_rows = seq_masks(seq_lens, tokens.shape[0])
    input_tokens = tokens.astype(jnp.float32)
    first_normalized, first_centered_scaled, first_inverse_deviation = layer_norm_forward(
        input_tokens, layer_norm_gain[0], layer_norm_bias[0]
    )
    low1 = first_normalized.astype(jnp.bfloat16)
    proj = product("td,dc->tc", low1, qkv_full)
    query = (proj[:, :heads_width] + b_qv[0]).astype(jnp.bfloat16)
    key_rows = proj[:, heads_width : 2 * heads_width].astype(jnp.bfloat16)
    value = (proj[:, 2 * heads_width :] + b_qv[1]).astype(jnp.bfloat16)
    heads_out, logsum = attend(query, key_rows, value, allowed)
    attn_part = product("tc,dc->td", heads_out, out_full)
    attn_mix = sum_tensor(attn_part)
    first_hidden_state = input_tokens + attn_mix + b_out
    second_normalized, second_centered_scaled, second_inverse_deviation = layer_norm_forward(
        first_hidden_state, layer_norm_gain[1], layer_norm_bias[1]
    )
    low2 = second_normalized.astype(jnp.bfloat16)
    pre_act = jnp.dot(low2, fc1_full, preferred_element_type=jnp.float32) + b_fc1
    act, slope = gelu_parts(pre_act)
    act_low = act.astype(jnp.bfloat16)
    mlp_part = product("tf,df->td", act_low, fc2_full)
    mlp_mix = sum_tensor(mlp_part)
    result = first_hidden_state + mlp_mix + b_fc2
    output = jnp.where(live_rows[:, None], result, 0.0).astype(jnp.bfloat16)
    qkv_back, out_back, fc1_back, fc2_back = (qkv_full, out_full, fc1_full, fc2_full)
    grad_y = jnp.where(live_rows[:, None], cotangent, jnp.zeros_like(cotangent))
    flat_output_gradient = grad_y.astype(jnp.float32)
    d_pre = (jnp.dot(grad_y, fc2_back, preferred_element_type=jnp.float32) * slope).astype(
        jnp.bfloat16
    )
    g_fc2 = product("td,tf->df", grad_y, act_low)
    g_bfc2 = jnp.sum(flat_output_gradient, axis=0)
    g_fc1 = product("td,tf->df", low2, d_pre)
    g_mlp = jnp.concatenate([g_fc1.astype(jnp.bfloat16), g_fc2.astype(jnp.bfloat16)], axis=1)
    shard_mlp = lax.psum_scatter(g_mlp, "dp", scatter_dimension=0, tiled=True)
    g_bfc1 = jnp.sum(d_pre.astype(jnp.float32), axis=0)
    d_norm2_part = product("tf,df->td", d_pre, fc1_back)
    second_norm_delta = sum_tensor(d_norm2_part)
    second_gain_gradient = jnp.sum(second_norm_delta * second_centered_scaled, axis=0)
    g_shift2 = jnp.sum(second_norm_delta, axis=0)
    hidden_first_gradient = flat_output_gradient + layer_norm_backward(
        second_norm_delta, layer_norm_gain[1], second_centered_scaled, second_inverse_deviation
    )
    grad_low = hidden_first_gradient.astype(jnp.bfloat16)
    g_out = product("td,tc->dc", grad_low, heads_out)
    g_bout = jnp.sum(hidden_first_gradient, axis=0)
    d_heads = jnp.dot(grad_low, out_back, preferred_element_type=jnp.float32).astype(jnp.bfloat16)
    d_query, d_key, d_value = attend_back(
        query, key_rows, value, heads_out, d_heads, logsum, allowed
    )
    stacked = jnp.concatenate([d_query, d_key, d_value], axis=1)
    g_qkv = product("td,tc->dc", low1, stacked)
    g_attn = jnp.concatenate([g_qkv.astype(jnp.bfloat16), g_out.astype(jnp.bfloat16)], axis=1)
    g_bqv = jnp.stack(
        [jnp.sum(d_query.astype(jnp.float32), axis=0), jnp.sum(d_value.astype(jnp.float32), axis=0)]
    )
    d_norm1_part = product("tc,dc->td", stacked, qkv_back)
    first_norm_delta = sum_tensor(d_norm1_part)
    first_gain_gradient = jnp.sum(first_norm_delta * first_centered_scaled, axis=0)
    g_shift1 = jnp.sum(first_norm_delta, axis=0)
    input_gradient = hidden_first_gradient + layer_norm_backward(
        first_norm_delta, layer_norm_gain[0], first_centered_scaled, first_inverse_deviation
    )
    shard_mlp = shard_mlp.astype(jnp.float32)
    shard_fc1, shard_fc2 = shard_mlp[:, :hidden_width], shard_mlp[:, hidden_width:]
    vectors = jnp.concatenate(
        [
            first_gain_gradient,
            second_gain_gradient,
            g_shift1,
            g_shift2,
            g_bqv.reshape(-1),
            g_bout,
            g_bfc1,
            g_bfc2,
        ]
    )
    shard_attn, vectors = scatter_rows(g_attn, vectors)
    shard_qkv = jnp.stack([shard_attn[:, i * heads_width : (i + 1) * heads_width] for i in range(3)])
    shard_out = shard_attn[:, 3 * heads_width :]
    width = tokens.shape[1]
    cuts = [2 * width, 4 * width, 4 * width + 2 * heads_width]
    cuts += [cuts[-1] + width, cuts[-1] + width + hidden_width]
    gain_sum, shift_sum, bqv_sum, bout_sum, bfc1_sum, bfc2_sum = jnp.split(vectors, cuts)
    gain_sum, shift_sum = gain_sum.reshape(2, width), shift_sum.reshape(2, width)
    bqv_sum = bqv_sum.reshape(2, heads_width)
    return (
        output,
        input_gradient,
        gain_sum,
        shift_sum,
        shard_qkv,
        bqv_sum,
        shard_out,
        bout_sum,
        shard_fc1,
        bfc1_sum,
        shard_fc2,
        bfc2_sum,
    )


def solution(mesh):
    in_specs = (
        P("dp", None),
        P("dp", None),
        P("dp"),
        P(),
        P(),
        P(None, "dp", "tensor"),
        P(None, "tensor"),
        P("dp", "tensor"),
        P(),
        P("dp", "tensor"),
        P("tensor"),
        P("dp", "tensor"),
        P(),
    )
    out_specs = (
        P("dp", None),
        P("dp", None),
        P(),
        P(),
        P(None, "dp", "tensor"),
        P(None, "tensor"),
        P("dp", "tensor"),
        P(),
        P("dp", "tensor"),
        P("tensor"),
        P("dp", "tensor"),
        P(),
    )
    return jax.shard_map(body, mesh=mesh, in_specs=in_specs, out_specs=out_specs, check_vma=False)
```

```python
import jax
import jax.numpy as jnp
from jax import lax
from jax.experimental import pallas as pl
from jax.experimental.pallas import tpu as pltpu
from jax.sharding import PartitionSpec as P

HEAD_DIM = 64


NORM_EPS = 1e-05
GELU_COEF = 0.7978845608028654


def product(spec, left, right):
    return jnp.einsum(spec, left, right, preferred_element_type=jnp.float32)


def seq_masks(lengths, row_count):
    slots = jnp.arange(lengths.shape[0])
    ends = jnp.sum(jnp.where(slots[:, None] <= slots[None, :], lengths[:, None], 0), axis=0)
    places = jnp.arange(row_count, dtype=jnp.int32)
    segment = jnp.sum((places[:, None] >= ends[None, :]).astype(jnp.int32), axis=1)
    allowed = (segment[:, None] == segment[None, :]) & (places[:, None] >= places[None, :])
    live_rows = places < ends[-1]
    return (allowed, live_rows)


def layer_norm_forward(hidden, gain, shift):
    center = hidden - jnp.mean(hidden, axis=-1, keepdims=True)
    inv_std = lax.rsqrt(jnp.mean(center * center, axis=-1, keepdims=True) + NORM_EPS)
    normal_x = center * inv_std
    return (normal_x * gain + shift, normal_x, inv_std)


def layer_norm_backward(grad_out, gain, normal_x, inv_std):
    scaled = grad_out * gain
    return inv_std * (
        scaled
        - jnp.mean(scaled, axis=-1, keepdims=True)
        - normal_x * jnp.mean(scaled * normal_x, axis=-1, keepdims=True)
    )


def gelu_parts(pre_act):
    inner = GELU_COEF * (pre_act + 0.044715 * pre_act * pre_act * pre_act)
    tanh_val = jnp.tanh(inner)
    value = 0.5 * pre_act * (1.0 + tanh_val)
    slope = 0.5 * (1.0 + tanh_val) + 0.5 * pre_act * (1.0 - tanh_val * tanh_val) * GELU_COEF * (
        1.0 + 3.0 * 0.044715 * pre_act * pre_act
    )
    return (value, slope)


def split_heads(matrix):
    return matrix.reshape(matrix.shape[0], matrix.shape[1] // HEAD_DIM, HEAD_DIM)


def head_scores(query, key_rows, allowed):
    scores = product("qhd,khd->hqk", split_heads(query), split_heads(key_rows)) * HEAD_DIM ** (-0.5)
    return jnp.where(allowed[None], scores, -1e30)


def attend(query, key_rows, value, allowed):
    scores = head_scores(query, key_rows, allowed)
    row_max = jnp.max(scores, axis=-1, keepdims=True)
    logsum = row_max + jnp.log(jnp.sum(jnp.exp(scores - row_max), axis=-1, keepdims=True))
    weights = jnp.exp(scores - logsum).astype(jnp.bfloat16)
    mixed = product("hqk,khd->qhd", weights, split_heads(value)).astype(jnp.bfloat16)
    return (mixed.reshape(query.shape[0], -1), logsum)


def attend_back(query, key_rows, value, heads_out, d_heads, logsum, allowed):
    scores = head_scores(query, key_rows, allowed)
    probs = jnp.exp(scores - logsum)
    probs_low = probs.astype(jnp.bfloat16)
    d_split = split_heads(d_heads)
    d_prob = product("qhd,khd->hqk", d_split, split_heads(value))
    delta = jnp.sum(
        d_split.astype(jnp.float32) * split_heads(heads_out).astype(jnp.float32), axis=-1
    )
    d_score = (probs * (d_prob - jnp.transpose(delta)[:, :, None]) * HEAD_DIM ** (-0.5)).astype(
        jnp.bfloat16
    )
    d_query = product("hqk,khd->qhd", d_score, split_heads(key_rows)).astype(jnp.bfloat16)
    d_key = product("hqk,qhd->khd", d_score, split_heads(query)).astype(jnp.bfloat16)
    d_value = product("hqk,qhd->khd", probs_low, d_split).astype(jnp.bfloat16)
    row_count = query.shape[0]
    return (
        d_query.reshape(row_count, -1),
        d_key.reshape(row_count, -1),
        d_value.reshape(row_count, -1),
    )


def sum_tensor(part):
    low = lax.optimization_barrier(part.astype(jnp.bfloat16))
    count = lax.axis_size("tensor")
    if count != 2:
        return lax.psum(low, "tensor").astype(jnp.float32)
    other = lax.ppermute(low, "tensor", [(0, 1), (1, 0)])
    return low.astype(jnp.float32) + other.astype(jnp.float32)


def chip_at(place, chips):
    place = (place + chips) % chips
    back = place // (chips // 2)
    return 2 * (place * (1 - back) + (chips - 1 - place) * back) + back


def ring_place(chips):
    device = lax.axis_index("dp")
    core, chip = device % 2, device // 2
    column, row = chip % 2, chip // 2
    place = row * (1 - column) + (chips - 1 - row) * column
    return device, chip, core, place


def send(source, target, send_sem, recv_sem, device):
    return pltpu.make_async_remote_copy(
        src_ref=source,
        dst_ref=target,
        send_sem=send_sem,
        recv_sem=recv_sem,
        device_id={"dp": device},
        device_id_type=pl.DeviceIdType.MESH,
    )


def meet(devices):
    barrier = pltpu.get_barrier_semaphore()
    for device in devices:
        pl.semaphore_signal(
            barrier, inc=1, device_id={"dp": device}, device_id_type=pl.DeviceIdType.MESH
        )
    pl.semaphore_wait(barrier, len(devices))


def gather_kernel(chips, own, out, rs, rr, ls, lr, ps, pr, own_sem):
    device, chip, core, place = ring_place(chips)
    right = 2 * chip_at(place + 1, chips) + core
    left = 2 * chip_at(place - 1, chips) + core
    partner = 2 * chip + 1 - core
    meet((right, left, partner))
    top, width = chips // 2, own.shape[1]
    half = width // 2

    def block(step, whose, hop, side):
        at = out.at[2 * chip_at(place + step, chips) + whose]
        if hop < top:
            return at
        return at.at[:, pl.ds(side * half, half)]

    started = []

    def go(copy):
        copy.start()
        started.append(copy)

    go(send(own, out.at[device], rs.at[0], rr.at[0], right))
    go(send(own, out.at[device], ls.at[0], lr.at[0], left))
    go(send(own, out.at[device], ps.at[0], pr.at[0], partner))
    keep = pltpu.make_async_copy(own, out.at[device], own_sem)
    keep.start()
    passed = [block(0, 1 - core, 0, 0)]
    for hop in range(1, top + 1):
        for side, sign, s_sem, r_sem, onward in ((0, -1, rs, rr, right), (1, 1, ls, lr, left)):
            here = block(sign * hop, core, hop, side)
            send(here, here, s_sem.at[hop - 1], r_sem.at[hop - 1], onward).wait_recv()
            if hop < top:
                part = block(sign * hop, core, hop + 1, side)
                go(send(part, part, s_sem.at[hop], r_sem.at[hop], onward))
            slot = len(passed)
            go(send(here, here, ps.at[slot], pr.at[slot], partner))
            passed.append(block(sign * hop, 1 - core, hop, side))
    for slot, here in enumerate(passed):
        send(here, here, ps.at[slot], pr.at[slot], partner).wait_recv()
    for copy in started:
        copy.wait_send()
    keep.wait()


def gather_rows(shard):
    count = lax.axis_size("dp")
    chips = count // 2
    top = chips // 2
    dma = pltpu.SemaphoreType.DMA
    out = pl.pallas_call(
        lambda *refs: gather_kernel(chips, *refs),
        out_shape=jax.ShapeDtypeStruct((count, *shard.shape), shard.dtype),
        in_specs=[pl.BlockSpec(memory_space=pltpu.VMEM)],
        out_specs=pl.BlockSpec(memory_space=pl.ANY),
        scratch_shapes=[dma((top,))] * 4 + [dma((chips + 1,))] * 2 + [dma],
        compiler_params=pltpu.CompilerParams(collective_id=0, has_side_effects=True),
        name="gather_rows",
    )(shard)
    return out.reshape(count * shard.shape[0], shard.shape[1])


def scatter_kernel(
    chips, grads, vec, out, vec_out,
    pbuf, rbuf, lbuf, rstage, lstage, vpart, vslots,
    ps, pr, rs, rr, ls, lr, vps, vpr, vrs, vrr, vls, vlr,
):
    device, chip, core, place = ring_place(chips)
    right = 2 * chip_at(place + 1, chips) + core
    left = 2 * chip_at(place - 1, chips) + core
    partner = 2 * chip + 1 - core
    meet((right, left, partner))
    top, width = chips // 2, out.shape[1]
    half = width // 2
    low, high = pl.ds(0, half), pl.ds(half, half)
    started = []

    def go(copy):
        copy.start()
        started.append(copy)

    order = [top]
    for step in range(1, top):
        order += [top - step, step - top]
    order.append(0)
    go(send(vec, vpart, vps.at[0], vpr.at[0], partner))
    for slot, step in enumerate(order):
        mine = grads.at[2 * chip_at(place + step, chips) + 1 - core]
        go(send(mine, pbuf.at[slot], ps.at[slot], pr.at[slot], partner))

    def pair_sum(slot):
        spot = pbuf.at[slot]
        send(spot, spot, ps.at[slot], pr.at[slot], partner).wait_recv()
        mine = grads[2 * chip_at(place + order[slot], chips) + core]
        return mine.astype(jnp.float32) + pbuf[slot].astype(jnp.float32)

    def arrived(spot, s_sem, r_sem):
        send(spot, spot, s_sem, r_sem, partner).wait_recv()

    first = pair_sum(0).astype(jnp.bfloat16)
    rstage[0, :, :half] = first[:, :half]
    go(send(rstage.at[0, :, low], rbuf.at[0, :, low], rs.at[0], rr.at[0], right))
    lstage[0, :, half:] = first[:, half:]
    go(send(lstage.at[0, :, high], lbuf.at[0, :, high], ls.at[0], lr.at[0], left))
    arrived(vpart, vps.at[0], vpr.at[0])
    vslots[chip] = vec[...] + vpart[...]
    go(send(vslots.at[chip], vslots.at[chip], vrs.at[0], vrr.at[0], right))
    go(send(vslots.at[chip], vslots.at[chip], vls.at[0], vlr.at[0], left))
    for step in range(1, top):
        for side, buf, stage, s_sem, r_sem, onward in (
            (0, rbuf, rstage, rs, rr, right),
            (1, lbuf, lstage, ls, lr, left),
        ):
            total = pair_sum(2 * step - 1 + side)
            if step == 1:
                cols = (low, high)[side]
                arrived(buf.at[0, :, cols], s_sem.at[0], r_sem.at[0])
                more = buf[0, :, side * half : (side + 1) * half].astype(jnp.float32)
                if side == 0:
                    stage[step, :, :half] = (total[:, :half] + more).astype(jnp.bfloat16)
                    stage[step, :, half:] = total[:, half:].astype(jnp.bfloat16)
                else:
                    stage[step, :, :half] = total[:, :half].astype(jnp.bfloat16)
                    stage[step, :, half:] = (total[:, half:] + more).astype(jnp.bfloat16)
            else:
                arrived(buf.at[step - 1], s_sem.at[step - 1], r_sem.at[step - 1])
                stage[step] = (total + buf[step - 1].astype(jnp.float32)).astype(jnp.bfloat16)
            go(send(stage.at[step], buf.at[step], s_sem.at[step], r_sem.at[step], onward))
        spot = vslots.at[chip_at(place - step, chips)]
        arrived(spot, vrs.at[step - 1], vrr.at[step - 1])
        go(send(spot, spot, vrs.at[step], vrr.at[step], right))
        spot = vslots.at[chip_at(place + step, chips)]
        arrived(spot, vls.at[step - 1], vlr.at[step - 1])
        if step < top - 1:
            go(send(spot, spot, vls.at[step], vlr.at[step], left))
    spot = vslots.at[chip_at(place - top, chips)]
    arrived(spot, vrs.at[top - 1], vrr.at[top - 1])
    vec_out[...] = jnp.sum(vslots[...], axis=0)
    total = pair_sum(len(order) - 1)
    arrived(rbuf.at[top - 1], rs.at[top - 1], rr.at[top - 1])
    arrived(lbuf.at[top - 1], ls.at[top - 1], lr.at[top - 1])
    out[...] = total + rbuf[top - 1].astype(jnp.float32) + lbuf[top - 1].astype(jnp.float32)
    for copy in started:
        copy.wait_send()


def scatter_rows(grads, vectors):
    count = lax.axis_size("dp")
    chips = count // 2
    top = chips // 2
    rows, width = grads.shape[0] // count, grads.shape[1]
    lines = vectors.shape[0] // 128
    dma, vmem = pltpu.SemaphoreType.DMA, pl.BlockSpec(memory_space=pltpu.VMEM)
    block = (rows, width)
    shard, sums = pl.pallas_call(
        lambda *refs: scatter_kernel(chips, *refs),
        out_shape=(
            jax.ShapeDtypeStruct(block, jnp.float32),
            jax.ShapeDtypeStruct((lines, 128), jnp.float32),
        ),
        in_specs=[vmem, vmem],
        out_specs=(vmem, vmem),
        scratch_shapes=[pltpu.VMEM((chips, *block), jnp.bfloat16)]
        + [pltpu.VMEM((top, *block), jnp.bfloat16)] * 4
        + [pltpu.VMEM((lines, 128), jnp.float32), pltpu.VMEM((chips, lines, 128), jnp.float32)]
        + [dma((chips,))] * 2
        + [dma((top,))] * 4
        + [dma((1,))] * 2
        + [dma((top,))] * 4,
        compiler_params=pltpu.CompilerParams(collective_id=1, has_side_effects=True),
        name="scatter_rows",
    )(grads.reshape(count, rows, width), vectors.reshape(lines, 128))
    return shard, sums.reshape(-1)


GELU_CUBE = 0.044715
F32, BF16 = jnp.float32, jnp.bfloat16


def mm(left, right, dims=((1,), (0,))):
    return lax.dot_general(left, right, (dims, ((), ())), preferred_element_type=F32)


class Names:
    def __init__(self, names, refs):
        for name, ref in zip(names, refs):
            setattr(self, name, ref)


STAGED = ("lens", "tok", "cot", "gain", "shift", "b_qv", "b_out", "b_fc1", "b_fc2")
IN_NAMES = [
    "far_tok", "far_cot", "far_lens", "far_gain", "far_shift", "w_qkv", "far_b_qv", "w_out",
    "far_b_out", "w_fc1", "far_b_fc1", "w_fc2", "far_b_fc2",
]
OUT_NAMES = ["far_y", "far_gtok", "far_gqkv", "far_gout", "far_gfc1", "far_gfc2", "far_vec"]


def layer_scratch(chips, rows, row_count, width, heads, hidden, slots):
    count, top = 2 * chips, chips // 2
    dma = pltpu.SemaphoreType.DMA
    tall = (row_count, width)
    low = dict(
        wq=(count, 3, rows, heads), wo=(count, rows, heads),
        wf1=(count, rows, hidden), wf2=(count, rows, hidden),
        n1=tall, n2=tall, gy=tall, ghb=tall,
        z=(row_count, hidden), zp=(row_count, hidden),
        du=(row_count, hidden), dup=(row_count, hidden),
        qkv=(3, row_count, heads), o=(row_count, heads), op=(row_count, heads),
        dh=(row_count, heads),
        dqkv=(3, row_count, heads), dqkvp=(3, row_count, heads),
        xt=(4, 2, chips, rows, row_count), xtp=(4, chips, rows, row_count),
        grads=(3, chips, rows, hidden), rbuf=(3, 2, top, rows, hidden),
        ysend=(4, *tall), yrecv=(4, *tall), tok=tall, cot=tall,
    )
    full = dict(
        xh1=tall, xh2=tall, h1=tall, gh1=tall, rs1=(row_count, 1), rs2=(row_count, 1),
        u=(row_count, hidden), pf=(heads // HEAD_DIM, row_count, row_count),
        mask=(row_count, row_count), vec=(16, width), vecp=(16, width), vslots=(chips, 8, 128), vres=(16, width), vsum=(16, width),
        gain=(2, width), shift=(2, width), b_qv=(2, heads), b_out=(1, width),
        b_fc1=(1, hidden), b_fc2=(1, width),
        g_qkv=(3, rows, heads), g_out=(rows, heads), g_fc1=(rows, hidden), g_fc2=(rows, hidden),
    )
    sems = dict(
        gs=(8, 2, top), gr=(8, 2, top), ps=(8, chips + 1), pr=(8, chips + 1),
        ss=(12, 2, top), sr=(12, 2, top), as_=(12,), ar=(12,), ys=(4, 4), yr=(4, 4),
        vs=(2, chips), vr=(2, chips), loc=(8,), ins=(9,), outs=(9,),
    )
    shapes = {k: pltpu.VMEM(s, BF16) for k, s in low.items()}
    shapes |= {k: pltpu.VMEM(s, F32) for k, s in full.items()}
    shapes |= {k: dma(s) for k, s in sems.items()}
    shapes["lens"] = pltpu.SMEM((slots,), jnp.int32)
    return shapes


def layer_kernel(chips, scratch_names, *refs):
    r = Names(IN_NAMES + OUT_NAMES + scratch_names, refs)
    device, chip, core, place = ring_place(chips)
    side_y = lax.axis_index("tensor")
    count, top = 2 * chips, chips // 2
    right = 2 * chip_at(place + 1, chips) + core
    left = 2 * chip_at(place - 1, chips) + core
    partner = 2 * chip + 1 - core
    onward = (right, left)
    row_count, width = r.far_tok.shape
    rows, heads = r.w_out.shape
    hidden = r.w_fc1.shape[1]
    half_hidden = hidden // 2
    started = []

    def remote(source, target, send_sem, recv_sem, **where):
        return pltpu.make_async_remote_copy(
            src_ref=source, dst_ref=target, send_sem=send_sem, recv_sem=recv_sem,
            device_id=where, device_id_type=pl.DeviceIdType.MESH,
        )

    def drain(n):
        for copy in started[:n]:
            copy.wait_send()
        del started[:n]

    def go(copy):
        copy.start()
        started.append(copy)

    barrier = pltpu.get_barrier_semaphore()

    def greet(**where):
        pl.semaphore_signal(
            barrier, inc=1, device_id=where, device_id_type=pl.DeviceIdType.MESH
        )

    for other in (right, left, partner):
        greet(dp=other)
    greet(tensor=1 - side_y)
    staged = []
    for j, name in enumerate(STAGED):
        copy = pltpu.make_async_copy(getattr(r, "far_" + name), getattr(r, name), r.ins.at[j])
        copy.start()
        staged.append(copy)
    pl.semaphore_wait(barrier, 4)

    base = (0, 0, 0, 0, 0, half_hidden, 0, half_hidden)
    span = (heads,) * 4 + (half_hidden,) * 4

    def cut(i, ref, side=None):
        start, size = base[i], span[i]
        if side is not None:
            size = size // 2
            start = start + side * size
        if start == 0 and size == ref.shape[-1]:
            return ref
        return ref.at[:, pl.ds(start, size)]

    def own(i):
        if i < 3:
            return r.w_qkv.at[i]
        return cut(i, (r.w_out, r.w_fc1, r.w_fc1, r.w_fc2, r.w_fc2)[i - 3])

    def spot_of(i, dev, side=None):
        if i < 3:
            return cut(i, r.wq.at[dev, i], side)
        return cut(i, (r.wo, r.wf1, r.wf1, r.wf2, r.wf2)[i - 3].at[dev], side)

    def block(i, step, whose, hop, side):
        dev = 2 * chip_at(place + step, chips) + whose
        return spot_of(i, dev, side if hop == top else None)

    def keep(i):
        return pltpu.make_async_copy(own(i), spot_of(i, device), r.loc.at[i])

    def start_item(i):
        mine, there = own(i), spot_of(i, device)
        for side in (0, 1):
            go(remote(mine, there, r.gs.at[i, side, 0], r.gr.at[i, side, 0], dp=onward[side]))
        go(remote(mine, there, r.ps.at[i, 0], r.pr.at[i, 0], dp=partner))
        keep(i).start()

    def hop_item(i, hop):
        for side, sign in ((0, -1), (1, 1)):
            here = block(i, sign * hop, core, hop, side)
            remote(
                here, here, r.gs.at[i, side, hop - 1], r.gr.at[i, side, hop - 1], dp=onward[side]
            ).wait_recv()
            if hop < top:
                part = block(i, sign * hop, core, hop + 1, side)
                go(remote(
                    part, part, r.gs.at[i, side, hop], r.gr.at[i, side, hop], dp=onward[side]
                ))
            slot = 2 * hop - 1 + side
            go(remote(here, here, r.ps.at[i, slot], r.pr.at[i, slot], dp=partner))

    def finish_item(i):
        keep(i).wait()
        for slot in range(chips + 1):
            hop, side = (slot + 1) // 2, (slot + 1) % 2
            here = block(i, (-1, 1)[side] * hop, 1 - core, hop, side)
            remote(here, here, r.ps.at[i, slot], r.pr.at[i, slot], dp=partner).wait_recv()

    def swap(k, source, target):
        go(remote(source, target, r.as_.at[k], r.ar.at[k], dp=partner))

    def swapped(k, target):
        remote(target, target, r.as_.at[k], r.ar.at[k], dp=partner).wait_recv()

    quarter = width // 4
    group = count // 4

    def exchange(k, c):
        at = pl.ds(c * quarter, quarter)
        go(remote(
            r.ysend.at[k, :, at], r.yrecv.at[k, :, at], r.ys.at[k, c], r.yr.at[k, c],
            tensor=1 - side_y,
        ))

    def exchanged(k):
        for c in range(4):
            spot = r.yrecv.at[k, :, pl.ds(c * quarter, quarter)]
            remote(spot, spot, r.ys.at[k, c], r.yr.at[k, c], tensor=1 - side_y).wait_recv()

    scatter_span = hidden // 4
    half = scatter_span // 2

    def scatter_start(i):
        k, col = i // 4, (i % 4) * scatter_span
        far = r.grads.at[k, chip_at(place + top, chips)]
        for side in (0, 1):
            at = pl.ds(col + side * half, half)
            go(remote(
                far.at[:, at], r.rbuf.at[k, side, 0, :, at], r.ss.at[i, side, 0],
                r.sr.at[i, side, 0], dp=onward[side],
            ))

    def scatter_step(i, s):
        k, col = i // 4, (i % 4) * scatter_span
        for side, sign in ((0, 1), (1, -1)):
            target = chip_at(place + sign * (top - s), chips)
            at = pl.ds(col + side * half, half) if s == 1 else pl.ds(col, scatter_span)
            spot = r.rbuf.at[k, side, s - 1, :, at]
            remote(
                spot, spot, r.ss.at[i, side, s - 1], r.sr.at[i, side, s - 1], dp=onward[side]
            ).wait_recv()
            total = r.grads[k, target, :, at].astype(F32) + spot[...].astype(F32)
            r.grads[k, target, :, at] = total.astype(BF16)
            at = pl.ds(col, scatter_span)
            go(remote(
                r.grads.at[k, target, :, at], r.rbuf.at[k, side, s, :, at],
                r.ss.at[i, side, s], r.sr.at[i, side, s], dp=onward[side],
            ))

    def scatter_end(i):
        k, col = i // 4, (i % 4) * scatter_span
        at = pl.ds(col, scatter_span)
        total = r.grads[k, chip, :, at].astype(F32)
        for side in (0, 1):
            spot = r.rbuf.at[k, side, top - 1, :, at]
            remote(
                spot, spot, r.ss.at[i, side, top - 1], r.sr.at[i, side, top - 1], dp=onward[side]
            ).wait_recv()
            total = total + spot[...].astype(F32)
        if k == 0:
            r.g_fc2[:, at] = total
        elif k == 1:
            r.g_fc1[:, at] = total
        elif i < 11:
            r.g_qkv[i - 8] = total
            put(r.g_qkv.at[i - 8], r.far_gqkv.at[i - 8])
        else:
            r.g_out[...] = total
            put(r.g_out, r.far_gout)

    order = [(i, s) for s in range(1, top) for i in range(4)]
    order += [(4 + i, s) for s in range(1, top) for i in range(4)]
    order += [(i, s) for s in range(1, top) for i in (11, 8, 9, 10)]
    steps = iter(order)

    def advance(n):
        for _ in range(n):
            scatter_step(*next(steps))

    put_copies = []

    def put(source, target):
        copy = pltpu.make_async_copy(source, target, r.outs.at[len(put_copies)])
        copy.start()
        put_copies.append(copy)

    def grad_tile(k, column, size, terms):
        total = None
        for lhs, rhs in terms:
            part = mm(lhs.reshape(chips * rows, row_count), rhs)
            total = part if total is None else total + part
        r.grads[k, :, :, pl.ds(column, size)] = total.reshape(chips, rows, size).astype(BF16)

    chunk = 32

    def row_loop(fn, carry=()):
        def step(i, c):
            return fn(pl.ds(pl.multiple_of(i * chunk, chunk), chunk), i * chunk, c)
        return lax.fori_loop(0, row_count // chunk, step, carry)

    def fold(value):
        return jnp.sum(value.reshape(chunk // 8, 8, value.shape[1]), axis=0)

    def transposed(k, source):
        per = 2 * rows
        for c in range(chips):
            flipped = source[:, c * per : (c + 1) * per].T
            r.xt[k, 0, c] = flipped[:rows]
            r.xt[k, 1, c] = flipped[rows:]
        swap(k, r.xt.at[k, 1 - core], r.xtp.at[k])

    for i in range(4):
        start_item(i)
    for copy in staged:
        copy.wait()
    ends = []
    for j in range(r.lens.shape[0]):
        ends.append(r.lens[j] if j == 0 else ends[-1] + r.lens[j])
    at_row = lax.broadcasted_iota(jnp.int32, (row_count, row_count), 0)
    at_col = lax.broadcasted_iota(jnp.int32, (row_count, row_count), 1)
    seg_row = sum((at_row >= e).astype(jnp.int32) for e in ends)
    seg_col = sum((at_col >= e).astype(jnp.int32) for e in ends)
    allowed = (seg_row == seg_col) & (at_row >= at_col)
    r.mask[...] = allowed.astype(F32)
    r.vec[...] = jnp.zeros_like(r.vec)

    def is_live(first):
        return first + lax.broadcasted_iota(jnp.int32, (chunk, width), 0) < ends[-1]

    def first_norm(at, first, c):
        x = r.tok[at, :].astype(F32)
        x = x - jnp.mean(x, axis=1, keepdims=True)
        inv = lax.rsqrt(jnp.mean(x * x, axis=1, keepdims=True) + NORM_EPS)
        x = x * inv
        r.xh1[at, :] = x
        r.rs1[at, :] = inv
        r.n1[at, :] = (x * r.gain[0:1, :] + r.shift[0:1, :]).astype(BF16)
        g = jnp.where(is_live(first), r.cot[at, :].astype(F32), 0.0)
        r.gy[at, :] = g.astype(BF16)
        return (c[0] + fold(g),)

    (total,) = row_loop(first_norm, (jnp.zeros((8, width), F32),))
    r.vec[8:9, :] = jnp.sum(total, axis=0, keepdims=True)
    for i in range(4):
        hop_item(i, 1)
    transposed(0, r.n1)
    for i in range(4):
        hop_item(i, 2)
    transposed(1, r.gy)
    for i in range(4):
        hop_item(i, 3)
    start_item(4)
    start_item(5)
    start_item(6)

    for i in range(3):
        hop_item(i, 4)
        finish_item(i)
        part = mm(r.n1[...], r.wq[:, i].reshape(width, heads))
        if i != 1:
            part = part + r.b_qv[i // 2 : i // 2 + 1, :]
        r.qkv[i] = part.astype(BF16)
    hop_item(3, 4)
    hop_item(4, 1)
    lane = lax.broadcasted_iota(jnp.int32, (1, 2 * HEAD_DIM), 1)
    picks = [(lane // HEAD_DIM == j).astype(F32).astype(BF16) for j in (0, 1)]
    first_half = lax.broadcasted_iota(jnp.int32, (row_count, 2 * HEAD_DIM), 1) < HEAD_DIM
    pairs = heads // (2 * HEAD_DIM)
    scale = HEAD_DIM ** (-0.5)
    between = [(5, 1), (6, 1), (4, 2), (5, 2)]
    for p in range(pairs):
        at = pl.ds(p * 2 * HEAD_DIM, 2 * HEAD_DIM)
        q, k, v = r.qkv[0, :, at], r.qkv[1, :, at], r.qkv[2, :, at]
        mixed = []
        for j in (0, 1):
            s = mm(q * picks[j], k, ((1,), (1,))) * scale
            s = jnp.where(r.mask[...] > 0.5, s, -1e30)
            e = jnp.exp(s - jnp.max(s, axis=1, keepdims=True))
            e = e / jnp.sum(e, axis=1, keepdims=True)
            r.pf[2 * p + j] = e
            mixed.append(mm(e.astype(BF16), v))
        r.o[:, at] = jnp.where(first_half, mixed[0], mixed[1]).astype(BF16)
        hop_item(*between[p])
    start_item(7)
    finish_item(3)
    for c in range(4):
        w = r.wo[c * group : (c + 1) * group].reshape(quarter, heads)
        r.ysend[0, :, pl.ds(c * quarter, quarter)] = mm(r.o[...], w, ((1,), (1,))).astype(BF16)
        exchange(0, c)
    swap(8, r.o, r.op)
    hop_item(4, 3)
    hop_item(5, 3)
    hop_item(6, 2)
    hop_item(7, 1)
    exchanged(0)

    def second_norm(at, first, c):
        x = r.tok[at, :].astype(F32)
        x = x + (r.ysend[0, at, :].astype(F32) + r.yrecv[0, at, :].astype(F32)) + r.b_out[...]
        r.h1[at, :] = x
        x = x - jnp.mean(x, axis=1, keepdims=True)
        inv = lax.rsqrt(jnp.mean(x * x, axis=1, keepdims=True) + NORM_EPS)
        x = x * inv
        r.xh2[at, :] = x
        r.rs2[at, :] = inv
        r.n2[at, :] = (x * r.gain[1:2, :] + r.shift[1:2, :]).astype(BF16)
        return c

    row_loop(second_norm)
    transposed(2, r.n2)
    hop_item(4, 4)
    hop_item(5, 4)
    finish_item(4)
    finish_item(5)

    tile = hidden // 4
    later = [(), (6, 3), (7, 2), (6, 4)]
    for t in range(4):
        at = pl.ds(t * tile, tile)
        r.u[:, at] = mm(r.n2[...], r.wf1[:, :, at].reshape(width, tile)) + r.b_fc1[:, at]

        def gelu(rows_at, first, c):
            u = r.u[rows_at, at]
            t_ = jnp.tanh(GELU_COEF * (u + GELU_CUBE * u * u * u))
            r.z[rows_at, at] = (0.5 * u * (1.0 + t_)).astype(BF16)
            r.u[rows_at, at] = 0.5 * (1.0 + t_) + 0.5 * u * (1.0 - t_ * t_) * GELU_COEF * (
                1.0 + 3.0 * GELU_CUBE * u * u
            )
            return c

        row_loop(gelu)
        if t % 2 == 1:
            cols = pl.ds((t // 2) * half_hidden, half_hidden)
            swap(4 + t // 2, r.z.at[:, cols], r.zp.at[:, cols])
        if later[t]:
            hop_item(*later[t])
    swapped(1, r.xtp.at[1])
    for h in (0, 1):
        cols = pl.ds(h * half_hidden, half_hidden)
        swapped(4 + h, r.zp.at[:, cols])
        for t in (2 * h, 2 * h + 1):
            at = pl.ds(t * tile, tile)
            grad_tile(0, t * tile, tile, ((r.xt[1, core], r.z[:, at]), (r.xtp[1], r.zp[:, at])))
            scatter_start(t)
        hop_item(7, 3 + h)
    finish_item(6)
    finish_item(7)
    for t in range(4):
        at = pl.ds(t * tile, tile)
        d = mm(r.gy[...], r.wf2[:, :, at].reshape(width, tile)) * r.u[:, at]
        d = d.astype(BF16)
        r.du[:, at] = d
        row, col = (t * tile) // width, (t * tile) % width
        r.vec[6 + row : 7 + row, col : col + tile] = jnp.sum(
            d.astype(F32), axis=0, keepdims=True
        )
        if t % 2 == 1:
            cols = pl.ds((t // 2) * half_hidden, half_hidden)
            swap(6 + t // 2, r.du.at[:, cols], r.dup.at[:, cols])
        advance(1)
    for c in range(4):
        w = r.wf1[c * group : (c + 1) * group].reshape(quarter, hidden)
        r.ysend[1, :, pl.ds(c * quarter, quarter)] = mm(r.du[...], w, ((1,), (1,))).astype(BF16)
        exchange(1, c)
        advance(1)
    swapped(2, r.xtp.at[2])
    for h in (0, 1):
        cols = pl.ds(h * half_hidden, half_hidden)
        swapped(6 + h, r.dup.at[:, cols])
        for t in (2 * h, 2 * h + 1):
            at = pl.ds(t * tile, tile)
            grad_tile(1, t * tile, tile, ((r.xt[2, core], r.du[:, at]), (r.xtp[2], r.dup[:, at])))
            scatter_start(4 + t)
            advance(1)
    for j in range(1, chips):
        greet(dp=2 * lax.rem(chip + j, chips) + core)
    for c in range(4):
        w = r.wf2[c * group : (c + 1) * group].reshape(quarter, hidden)
        r.ysend[2, :, pl.ds(c * quarter, quarter)] = mm(r.z[...], w, ((1,), (1,))).astype(BF16)
        exchange(2, c)
    advance(2)
    exchanged(1)

    def norm_back(k, gain_row, xh, rs, above, store):
        def step(at, first, c):
            dn = r.ysend[k, at, :].astype(F32) + r.yrecv[k, at, :].astype(F32)
            x = xh[at, :]
            scaled = dn * r.gain[gain_row : gain_row + 1, :]
            m1 = jnp.mean(scaled, axis=1, keepdims=True)
            m2 = jnp.mean(scaled * x, axis=1, keepdims=True)
            g = above[at, :].astype(F32) + rs[at, :] * (scaled - m1 - x * m2)
            store(at, g)
            return (c[0] + fold(dn * x), c[1] + fold(dn), c[2] + fold(g))

        zero = jnp.zeros((8, width), F32)
        return [jnp.sum(s, axis=0, keepdims=True) for s in row_loop(step, (zero, zero, zero))]

    def store_gh1(at, g):
        r.gh1[at, :] = g
        r.ghb[at, :] = g.astype(BF16)

    sums = norm_back(1, 1, r.xh2, r.rs2, r.gy, store_gh1)
    r.vec[1:2, :] = sums[0]
    r.vec[3:4, :] = sums[1]
    r.vec[5:6, :] = sums[2]
    transposed(3, r.ghb)
    advance(1)

    r.dh[...] = mm(r.ghb[...], r.wo[...].reshape(width, heads)).astype(BF16)
    for p in range(pairs):
        at = pl.ds(p * 2 * HEAD_DIM, 2 * HEAD_DIM)
        q, k, v = r.qkv[0, :, at], r.qkv[1, :, at], r.qkv[2, :, at]
        d_out, o = r.dh[:, at], r.o[:, at]
        parts = []
        for j in (0, 1):
            mine = d_out * picks[j]
            delta = jnp.sum(mine.astype(F32) * o.astype(F32), axis=1, keepdims=True)
            prob = r.pf[2 * p + j]
            ds = (prob * (mm(mine, v, ((1,), (1,))) - delta) * scale).astype(BF16)
            parts.append((
                mm(ds, k),
                mm(ds, q, ((0,), (0,))),
                mm(prob.astype(BF16), d_out, ((0,), (0,))),
            ))
        for i in range(3):
            r.dqkv[i, :, at] = jnp.where(first_half, parts[0][i], parts[1][i]).astype(BF16)
        advance((1, 1, 2, 1)[p])
    swap(9, r.dqkv, r.dqkvp)
    swapped(3, r.xtp.at[3])
    swapped(8, r.op)
    grad_tile(2, 3 * heads, heads, ((r.xt[3, core], r.o[...]), (r.xtp[3], r.op[...])))
    scatter_start(11)
    for c in range(4):
        total = None
        for i in range(3):
            w = r.wq[c * group : (c + 1) * group, i].reshape(quarter, heads)
            part = mm(r.dqkv[i], w, ((1,), (1,)))
            total = part if total is None else total + part
        r.ysend[3, :, pl.ds(c * quarter, quarter)] = total.astype(BF16)
        exchange(3, c)
        if c % 2 == 1:
            advance(1)
    for i in (0, 2):
        r.vec[4:5, pl.ds((i // 2) * heads, heads)] = jnp.sum(
            r.dqkv[i].astype(F32), axis=0, keepdims=True
        )
    swapped(0, r.xtp.at[0])
    swapped(9, r.dqkvp)
    for i in range(3):
        grad_tile(
            2, i * heads, heads, ((r.xt[0, core], r.dqkv[i]), (r.xtp[0], r.dqkvp[i]))
        )
        scatter_start(8 + i)
    advance(1)
    for i in range(4):
        scatter_end(i)
    put(r.g_fc2, r.far_gfc2)
    advance(1)
    exchanged(2)

    def finish_output(at, first, c):
        y = r.h1[at, :] + (r.ysend[2, at, :].astype(F32) + r.yrecv[2, at, :].astype(F32))
        y = jnp.where(is_live(first), y + r.b_fc2[...], 0.0)
        r.n2[at, :] = y.astype(BF16)
        return c

    row_loop(finish_output)
    put(r.n2, r.far_y)
    advance(4)
    exchanged(3)

    def store_tokens(at, g):
        r.gh1[at, :] = g

    sums = norm_back(3, 0, r.xh1, r.rs1, r.gh1, store_tokens)
    r.vec[0:1, :] = sums[0]
    r.vec[2:3, :] = sums[1]
    put(r.gh1, r.far_gtok)

    swap(10, r.vec, r.vecp)
    top_row = pl.multiple_of(8 * core, 8)

    def tile_of(ref, which):
        return ref.at[pl.ds(top_row, 8), pl.ds(pl.multiple_of(128 * which, 128), 128)]

    def tile_copy(stage, j, source, target):
        other = lax.rem(chip + j, chips)
        return remote(
            source, target, r.vs.at[stage, j], r.vr.at[stage, j], dp=2 * other + core
        )

    advance(1)
    swapped(10, r.vecp)
    r.vres[...] = r.vec[...] + r.vecp[...]
    pl.semaphore_wait(barrier, chips - 1)
    for j in range(1, chips):
        go(tile_copy(0, j, tile_of(r.vres, lax.rem(chip + j, chips)), r.vslots.at[chip]))
    r.vslots[chip] = tile_of(r.vres, chip)[...]
    advance(3)
    for i in range(4, 8):
        scatter_end(i)
    put(r.g_fc1, r.far_gfc1)
    drain(len(started) - 12)
    for j in range(1, chips):
        spot = r.vslots.at[lax.rem(chip + chips - j, chips)]
        tile_copy(0, j, spot, spot).wait_recv()
    mine = tile_of(r.vsum, chip)
    mine[...] = jnp.sum(r.vslots[...], axis=0)
    for j in range(1, chips):
        go(tile_copy(1, j, mine, mine))
    advance(4)
    assert next(steps, None) is None
    for j in range(1, chips):
        spot = tile_of(r.vsum, lax.rem(chip + chips - j, chips))
        tile_copy(1, j, spot, spot).wait_recv()
    rows_here = r.vsum.at[pl.ds(top_row, 8), :]
    swap(11, rows_here, rows_here)
    drain(len(started) - 18)
    swapped(11, r.vsum.at[pl.ds(pl.multiple_of(8 * (1 - core), 8), 8), :])
    put(r.vsum, r.far_vec)
    for i in (11, 8, 9, 10):
        scatter_end(i)
    for copy in put_copies:
        copy.wait()
    drain(len(started))


def one_kernel(tokens, cotangent, seq_lens, gain, shift, w_qkv, b_qv, w_out, b_out, w_fc1, b_fc1, w_fc2, b_fc2):
    chips = lax.axis_size("dp") // 2
    row_count, width = tokens.shape
    rows, heads = w_out.shape
    hidden = w_fc1.shape[1]
    vmem, hbm = pl.BlockSpec(memory_space=pltpu.VMEM), pl.BlockSpec(memory_space=pl.ANY)
    scratch = layer_scratch(chips, rows, row_count, width, heads, hidden, seq_lens.shape[0])
    names = list(scratch)

    def made(*shape, kind=F32):
        return jax.ShapeDtypeStruct(shape, kind)

    outs = pl.pallas_call(
        lambda *refs: layer_kernel(chips, names, *refs),
        out_shape=(
            made(row_count, width, kind=BF16), made(row_count, width), made(3, rows, heads),
            made(rows, heads), made(rows, hidden), made(rows, hidden), made(16, width),
        ),
        in_specs=[hbm] * 13,
        out_specs=(hbm,) * 7,
        scratch_shapes=list(scratch.values()),
        compiler_params=pltpu.CompilerParams(
            collective_id=2, has_side_effects=True, vmem_limit_bytes=63 * 2**20
        ),
        name="layer",
    )(
        tokens, cotangent, seq_lens, gain, shift, w_qkv, b_qv, w_out, b_out[None], w_fc1,
        b_fc1[None], w_fc2, b_fc2[None],
    )
    small = ((2, width), (2, width), (2, heads), (1, width), (1, hidden), (1, width))
    outs = pl.pallas_call(
        lambda *refs: results_kernel(heads, *refs),
        out_shape=tuple(made(*o.shape, kind=o.dtype) for o in outs[:6])
        + tuple(made(*o) for o in small),
        in_specs=[vmem] * 7,
        out_specs=(hbm,) * 6 + (vmem,) * 6,
        scratch_shapes=[pltpu.SemaphoreType.DMA((6,))],
        name="results",
    )(*outs)
    y, g_tok, g_qkv, g_out, g_fc1, g_fc2, g_gain, g_shift, g_bqv, g_bout, g_bfc1, g_bfc2 = outs
    return (
        y, g_tok, g_gain, g_shift, g_qkv, g_bqv, g_out, g_bout.reshape(-1), g_fc1,
        g_bfc1.reshape(-1), g_fc2, g_bfc2.reshape(-1),
    )


def results_kernel(heads, *refs):
    sources, vec, targets, sem = refs[:6], refs[6], refs[7:13], refs[19]
    gain, shift, bqv, bout, bfc1, bfc2 = refs[13:19]
    copies = [
        pltpu.make_async_copy(source, target, sem.at[i])
        for i, (source, target) in enumerate(zip(sources, targets))
    ]
    for copy in copies:
        copy.start()
    width = vec.shape[1]
    gain[...] = vec[0:2, :]
    shift[...] = vec[2:4, :]
    bqv[0:1, :] = vec[4:5, :heads]
    bqv[1:2, :] = vec[4:5, heads : 2 * heads]
    bout[...] = vec[5:6, :]
    for j in range(bfc1.shape[1] // width):
        bfc1[:, j * width : (j + 1) * width] = vec[6 + j : 7 + j, :]
    bfc2[...] = vec[8:9, :]
    for copy in copies:
        copy.wait()


def fits_one_kernel(tokens, w_out, w_fc1):
    chips = lax.axis_size("dp") // 2
    rows, heads = w_out.shape
    width, hidden = tokens.shape[1], w_fc1.shape[1]
    return (
        lax.axis_size("tensor") == 2
        and chips == 2 * 4
        and width == 128 * chips
        and rows % 16 == 0
        and tokens.shape[0] % 32 == 0
        and 2 * heads == width
        and 4 * heads == hidden
    )


def body(
    tokens,
    cotangent,
    seq_lens,
    layer_norm_gain,
    layer_norm_bias,
    w_qkv,
    b_qv,
    w_out,
    b_out,
    w_fc1,
    b_fc1,
    w_fc2,
    b_fc2,
):
    if fits_one_kernel(tokens, w_out, w_fc1):
        return one_kernel(
            tokens, cotangent, seq_lens, layer_norm_gain, layer_norm_bias, w_qkv, b_qv, w_out,
            b_out, w_fc1, b_fc1, w_fc2, b_fc2,
        )
    heads_width, hidden_width = w_out.shape[1], w_fc1.shape[1]
    attn_shards = jnp.concatenate([w_qkv[0], w_qkv[1], w_qkv[2], w_out], axis=1)
    mlp_shards = jnp.concatenate([w_fc1, w_fc2], axis=1)
    mlp_full = lax.all_gather(mlp_shards, "dp", axis=0, tiled=True)
    attn_full = gather_rows(attn_shards)
    qkv_full, out_full = attn_full[:, : 3 * heads_width], attn_full[:, 3 * heads_width :]
    fc1_full, fc2_full = mlp_full[:, :hidden_width], mlp_full[:, hidden_width:]
    allowed, live_rows = seq_masks(seq_lens, tokens.shape[0])
    input_tokens = tokens.astype(jnp.float32)
    first_normalized, first_centered_scaled, first_inverse_deviation = layer_norm_forward(
        input_tokens, layer_norm_gain[0], layer_norm_bias[0]
    )
    low1 = first_normalized.astype(jnp.bfloat16)
    proj = product("td,dc->tc", low1, qkv_full)
    query = (proj[:, :heads_width] + b_qv[0]).astype(jnp.bfloat16)
    key_rows = proj[:, heads_width : 2 * heads_width].astype(jnp.bfloat16)
    value = (proj[:, 2 * heads_width :] + b_qv[1]).astype(jnp.bfloat16)
    heads_out, logsum = attend(query, key_rows, value, allowed)
    attn_part = product("tc,dc->td", heads_out, out_full)
    attn_mix = sum_tensor(attn_part)
    first_hidden_state = input_tokens + attn_mix + b_out
    second_normalized, second_centered_scaled, second_inverse_deviation = layer_norm_forward(
        first_hidden_state, layer_norm_gain[1], layer_norm_bias[1]
    )
    low2 = second_normalized.astype(jnp.bfloat16)
    pre_act = jnp.dot(low2, fc1_full, preferred_element_type=jnp.float32) + b_fc1
    act, slope = gelu_parts(pre_act)
    act_low = act.astype(jnp.bfloat16)
    mlp_part = product("tf,df->td", act_low, fc2_full)
    mlp_mix = sum_tensor(mlp_part)
    result = first_hidden_state + mlp_mix + b_fc2
    output = jnp.where(live_rows[:, None], result, 0.0).astype(jnp.bfloat16)
    qkv_back, out_back, fc1_back, fc2_back = (qkv_full, out_full, fc1_full, fc2_full)
    grad_y = jnp.where(live_rows[:, None], cotangent, jnp.zeros_like(cotangent))
    flat_output_gradient = grad_y.astype(jnp.float32)
    d_pre = (jnp.dot(grad_y, fc2_back, preferred_element_type=jnp.float32) * slope).astype(
        jnp.bfloat16
    )
    g_fc2 = product("td,tf->df", grad_y, act_low)
    g_bfc2 = jnp.sum(flat_output_gradient, axis=0)
    g_fc1 = product("td,tf->df", low2, d_pre)
    g_mlp = jnp.concatenate([g_fc1.astype(jnp.bfloat16), g_fc2.astype(jnp.bfloat16)], axis=1)
    shard_mlp = lax.psum_scatter(g_mlp, "dp", scatter_dimension=0, tiled=True)
    g_bfc1 = jnp.sum(d_pre.astype(jnp.float32), axis=0)
    d_norm2_part = product("tf,df->td", d_pre, fc1_back)
    second_norm_delta = sum_tensor(d_norm2_part)
    second_gain_gradient = jnp.sum(second_norm_delta * second_centered_scaled, axis=0)
    g_shift2 = jnp.sum(second_norm_delta, axis=0)
    hidden_first_gradient = flat_output_gradient + layer_norm_backward(
        second_norm_delta, layer_norm_gain[1], second_centered_scaled, second_inverse_deviation
    )
    grad_low = hidden_first_gradient.astype(jnp.bfloat16)
    g_out = product("td,tc->dc", grad_low, heads_out)
    g_bout = jnp.sum(hidden_first_gradient, axis=0)
    d_heads = jnp.dot(grad_low, out_back, preferred_element_type=jnp.float32).astype(jnp.bfloat16)
    d_query, d_key, d_value = attend_back(
        query, key_rows, value, heads_out, d_heads, logsum, allowed
    )
    stacked = jnp.concatenate([d_query, d_key, d_value], axis=1)
    g_qkv = product("td,tc->dc", low1, stacked)
    g_attn = jnp.concatenate([g_qkv.astype(jnp.bfloat16), g_out.astype(jnp.bfloat16)], axis=1)
    g_bqv = jnp.stack(
        [jnp.sum(d_query.astype(jnp.float32), axis=0), jnp.sum(d_value.astype(jnp.float32), axis=0)]
    )
    d_norm1_part = product("tc,dc->td", stacked, qkv_back)
    first_norm_delta = sum_tensor(d_norm1_part)
    first_gain_gradient = jnp.sum(first_norm_delta * first_centered_scaled, axis=0)
    g_shift1 = jnp.sum(first_norm_delta, axis=0)
    input_gradient = hidden_first_gradient + layer_norm_backward(
        first_norm_delta, layer_norm_gain[0], first_centered_scaled, first_inverse_deviation
    )
    shard_mlp = shard_mlp.astype(jnp.float32)
    shard_fc1, shard_fc2 = shard_mlp[:, :hidden_width], shard_mlp[:, hidden_width:]
    vectors = jnp.concatenate(
        [
            first_gain_gradient,
            second_gain_gradient,
            g_shift1,
            g_shift2,
            g_bqv.reshape(-1),
            g_bout,
            g_bfc1,
            g_bfc2,
        ]
    )
    shard_attn, vectors = scatter_rows(g_attn, vectors)
    shard_qkv = jnp.stack([shard_attn[:, i * heads_width : (i + 1) * heads_width] for i in range(3)])
    shard_out = shard_attn[:, 3 * heads_width :]
    width = tokens.shape[1]
    cuts = [2 * width, 4 * width, 4 * width + 2 * heads_width]
    cuts += [cuts[-1] + width, cuts[-1] + width + hidden_width]
    gain_sum, shift_sum, bqv_sum, bout_sum, bfc1_sum, bfc2_sum = jnp.split(vectors, cuts)
    gain_sum, shift_sum = gain_sum.reshape(2, width), shift_sum.reshape(2, width)
    bqv_sum = bqv_sum.reshape(2, heads_width)
    return (
        output,
        input_gradient,
        gain_sum,
        shift_sum,
        shard_qkv,
        bqv_sum,
        shard_out,
        bout_sum,
        shard_fc1,
        bfc1_sum,
        shard_fc2,
        bfc2_sum,
    )


def solution(mesh):
    in_specs = (
        P("dp", None),
        P("dp", None),
        P("dp"),
        P(),
        P(),
        P(None, "dp", "tensor"),
        P(None, "tensor"),
        P("dp", "tensor"),
        P(),
        P("dp", "tensor"),
        P("tensor"),
        P("dp", "tensor"),
        P(),
    )
    out_specs = (
        P("dp", None),
        P("dp", None),
        P(),
        P(),
        P(None, "dp", "tensor"),
        P(None, "tensor"),
        P("dp", "tensor"),
        P(),
        P("dp", "tensor"),
        P("tensor"),
        P("dp", "tensor"),
        P(),
    )
    return jax.shard_map(body, mesh=mesh, in_specs=in_specs, out_specs=out_specs, check_vma=False)
```

```python
import jax
import jax.numpy as jnp
from jax import lax
from jax.experimental import pallas as pl
from jax.experimental.pallas import tpu as pltpu
from jax.sharding import PartitionSpec as P

HEAD_DIM = 64


NORM_EPS = 1e-05
GELU_COEF = 0.7978845608028654


def product(spec, left, right):
    return jnp.einsum(spec, left, right, preferred_element_type=jnp.float32)


def seq_masks(lengths, row_count):
    slots = jnp.arange(lengths.shape[0])
    ends = jnp.sum(jnp.where(slots[:, None] <= slots[None, :], lengths[:, None], 0), axis=0)
    places = jnp.arange(row_count, dtype=jnp.int32)
    segment = jnp.sum((places[:, None] >= ends[None, :]).astype(jnp.int32), axis=1)
    allowed = (segment[:, None] == segment[None, :]) & (places[:, None] >= places[None, :])
    live_rows = places < ends[-1]
    return (allowed, live_rows)


def layer_norm_forward(hidden, gain, shift):
    center = hidden - jnp.mean(hidden, axis=-1, keepdims=True)
    inv_std = lax.rsqrt(jnp.mean(center * center, axis=-1, keepdims=True) + NORM_EPS)
    normal_x = center * inv_std
    return (normal_x * gain + shift, normal_x, inv_std)


def layer_norm_backward(grad_out, gain, normal_x, inv_std):
    scaled = grad_out * gain
    return inv_std * (
        scaled
        - jnp.mean(scaled, axis=-1, keepdims=True)
        - normal_x * jnp.mean(scaled * normal_x, axis=-1, keepdims=True)
    )


def gelu_parts(pre_act):
    inner = GELU_COEF * (pre_act + 0.044715 * pre_act * pre_act * pre_act)
    tanh_val = jnp.tanh(inner)
    value = 0.5 * pre_act * (1.0 + tanh_val)
    slope = 0.5 * (1.0 + tanh_val) + 0.5 * pre_act * (1.0 - tanh_val * tanh_val) * GELU_COEF * (
        1.0 + 3.0 * 0.044715 * pre_act * pre_act
    )
    return (value, slope)


def split_heads(matrix):
    return matrix.reshape(matrix.shape[0], matrix.shape[1] // HEAD_DIM, HEAD_DIM)


def head_scores(query, key_rows, allowed):
    scores = product("qhd,khd->hqk", split_heads(query), split_heads(key_rows)) * HEAD_DIM ** (-0.5)
    return jnp.where(allowed[None], scores, -1e30)


def attend(query, key_rows, value, allowed):
    scores = head_scores(query, key_rows, allowed)
    row_max = jnp.max(scores, axis=-1, keepdims=True)
    logsum = row_max + jnp.log(jnp.sum(jnp.exp(scores - row_max), axis=-1, keepdims=True))
    weights = jnp.exp(scores - logsum).astype(jnp.bfloat16)
    mixed = product("hqk,khd->qhd", weights, split_heads(value)).astype(jnp.bfloat16)
    return (mixed.reshape(query.shape[0], -1), logsum)


def attend_back(query, key_rows, value, heads_out, d_heads, logsum, allowed):
    scores = head_scores(query, key_rows, allowed)
    probs = jnp.exp(scores - logsum)
    probs_low = probs.astype(jnp.bfloat16)
    d_split = split_heads(d_heads)
    d_prob = product("qhd,khd->hqk", d_split, split_heads(value))
    delta = jnp.sum(
        d_split.astype(jnp.float32) * split_heads(heads_out).astype(jnp.float32), axis=-1
    )
    d_score = (probs * (d_prob - jnp.transpose(delta)[:, :, None]) * HEAD_DIM ** (-0.5)).astype(
        jnp.bfloat16
    )
    d_query = product("hqk,khd->qhd", d_score, split_heads(key_rows)).astype(jnp.bfloat16)
    d_key = product("hqk,qhd->khd", d_score, split_heads(query)).astype(jnp.bfloat16)
    d_value = product("hqk,qhd->khd", probs_low, d_split).astype(jnp.bfloat16)
    row_count = query.shape[0]
    return (
        d_query.reshape(row_count, -1),
        d_key.reshape(row_count, -1),
        d_value.reshape(row_count, -1),
    )


def sum_tensor(part):
    low = lax.optimization_barrier(part.astype(jnp.bfloat16))
    count = lax.axis_size("tensor")
    if count != 2:
        return lax.psum(low, "tensor").astype(jnp.float32)
    other = lax.ppermute(low, "tensor", [(0, 1), (1, 0)])
    return low.astype(jnp.float32) + other.astype(jnp.float32)


def chip_at(place, chips):
    place = (place + chips) % chips
    back = place // (chips // 2)
    return 2 * (place * (1 - back) + (chips - 1 - place) * back) + back


def ring_place(chips):
    device = lax.axis_index("dp")
    core, chip = device % 2, device // 2
    column, row = chip % 2, chip // 2
    place = row * (1 - column) + (chips - 1 - row) * column
    return device, chip, core, place


def send(source, target, send_sem, recv_sem, device):
    return pltpu.make_async_remote_copy(
        src_ref=source,
        dst_ref=target,
        send_sem=send_sem,
        recv_sem=recv_sem,
        device_id={"dp": device},
        device_id_type=pl.DeviceIdType.MESH,
    )


def meet(devices):
    barrier = pltpu.get_barrier_semaphore()
    for device in devices:
        pl.semaphore_signal(
            barrier, inc=1, device_id={"dp": device}, device_id_type=pl.DeviceIdType.MESH
        )
    pl.semaphore_wait(barrier, len(devices))


def gather_kernel(chips, own, out, rs, rr, ls, lr, ps, pr, own_sem):
    device, chip, core, place = ring_place(chips)
    right = 2 * chip_at(place + 1, chips) + core
    left = 2 * chip_at(place - 1, chips) + core
    partner = 2 * chip + 1 - core
    meet((right, left, partner))
    top, width = chips // 2, own.shape[1]
    half = width // 2

    def block(step, whose, hop, side):
        at = out.at[2 * chip_at(place + step, chips) + whose]
        if hop < top:
            return at
        return at.at[:, pl.ds(side * half, half)]

    started = []

    def go(copy):
        copy.start()
        started.append(copy)

    go(send(own, out.at[device], rs.at[0], rr.at[0], right))
    go(send(own, out.at[device], ls.at[0], lr.at[0], left))
    go(send(own, out.at[device], ps.at[0], pr.at[0], partner))
    keep = pltpu.make_async_copy(own, out.at[device], own_sem)
    keep.start()
    passed = [block(0, 1 - core, 0, 0)]
    for hop in range(1, top + 1):
        for side, sign, s_sem, r_sem, onward in ((0, -1, rs, rr, right), (1, 1, ls, lr, left)):
            here = block(sign * hop, core, hop, side)
            send(here, here, s_sem.at[hop - 1], r_sem.at[hop - 1], onward).wait_recv()
            if hop < top:
                part = block(sign * hop, core, hop + 1, side)
                go(send(part, part, s_sem.at[hop], r_sem.at[hop], onward))
            slot = len(passed)
            go(send(here, here, ps.at[slot], pr.at[slot], partner))
            passed.append(block(sign * hop, 1 - core, hop, side))
    for slot, here in enumerate(passed):
        send(here, here, ps.at[slot], pr.at[slot], partner).wait_recv()
    for copy in started:
        copy.wait_send()
    keep.wait()


def gather_rows(shard):
    count = lax.axis_size("dp")
    chips = count // 2
    top = chips // 2
    dma = pltpu.SemaphoreType.DMA
    out = pl.pallas_call(
        lambda *refs: gather_kernel(chips, *refs),
        out_shape=jax.ShapeDtypeStruct((count, *shard.shape), shard.dtype),
        in_specs=[pl.BlockSpec(memory_space=pltpu.VMEM)],
        out_specs=pl.BlockSpec(memory_space=pl.ANY),
        scratch_shapes=[dma((top,))] * 4 + [dma((chips + 1,))] * 2 + [dma],
        compiler_params=pltpu.CompilerParams(collective_id=0, has_side_effects=True),
        name="gather_rows",
    )(shard)
    return out.reshape(count * shard.shape[0], shard.shape[1])


def scatter_kernel(
    chips, grads, vec, out, vec_out,
    pbuf, rbuf, lbuf, rstage, lstage, vpart, vslots,
    ps, pr, rs, rr, ls, lr, vps, vpr, vrs, vrr, vls, vlr,
):
    device, chip, core, place = ring_place(chips)
    right = 2 * chip_at(place + 1, chips) + core
    left = 2 * chip_at(place - 1, chips) + core
    partner = 2 * chip + 1 - core
    meet((right, left, partner))
    top, width = chips // 2, out.shape[1]
    half = width // 2
    low, high = pl.ds(0, half), pl.ds(half, half)
    started = []

    def go(copy):
        copy.start()
        started.append(copy)

    order = [top]
    for step in range(1, top):
        order += [top - step, step - top]
    order.append(0)
    go(send(vec, vpart, vps.at[0], vpr.at[0], partner))
    for slot, step in enumerate(order):
        mine = grads.at[2 * chip_at(place + step, chips) + 1 - core]
        go(send(mine, pbuf.at[slot], ps.at[slot], pr.at[slot], partner))

    def pair_sum(slot):
        spot = pbuf.at[slot]
        send(spot, spot, ps.at[slot], pr.at[slot], partner).wait_recv()
        mine = grads[2 * chip_at(place + order[slot], chips) + core]
        return mine.astype(jnp.float32) + pbuf[slot].astype(jnp.float32)

    def arrived(spot, s_sem, r_sem):
        send(spot, spot, s_sem, r_sem, partner).wait_recv()

    first = pair_sum(0).astype(jnp.bfloat16)
    rstage[0, :, :half] = first[:, :half]
    go(send(rstage.at[0, :, low], rbuf.at[0, :, low], rs.at[0], rr.at[0], right))
    lstage[0, :, half:] = first[:, half:]
    go(send(lstage.at[0, :, high], lbuf.at[0, :, high], ls.at[0], lr.at[0], left))
    arrived(vpart, vps.at[0], vpr.at[0])
    vslots[chip] = vec[...] + vpart[...]
    go(send(vslots.at[chip], vslots.at[chip], vrs.at[0], vrr.at[0], right))
    go(send(vslots.at[chip], vslots.at[chip], vls.at[0], vlr.at[0], left))
    for step in range(1, top):
        for side, buf, stage, s_sem, r_sem, onward in (
            (0, rbuf, rstage, rs, rr, right),
            (1, lbuf, lstage, ls, lr, left),
        ):
            total = pair_sum(2 * step - 1 + side)
            if step == 1:
                cols = (low, high)[side]
                arrived(buf.at[0, :, cols], s_sem.at[0], r_sem.at[0])
                more = buf[0, :, side * half : (side + 1) * half].astype(jnp.float32)
                if side == 0:
                    stage[step, :, :half] = (total[:, :half] + more).astype(jnp.bfloat16)
                    stage[step, :, half:] = total[:, half:].astype(jnp.bfloat16)
                else:
                    stage[step, :, :half] = total[:, :half].astype(jnp.bfloat16)
                    stage[step, :, half:] = (total[:, half:] + more).astype(jnp.bfloat16)
            else:
                arrived(buf.at[step - 1], s_sem.at[step - 1], r_sem.at[step - 1])
                stage[step] = (total + buf[step - 1].astype(jnp.float32)).astype(jnp.bfloat16)
            go(send(stage.at[step], buf.at[step], s_sem.at[step], r_sem.at[step], onward))
        spot = vslots.at[chip_at(place - step, chips)]
        arrived(spot, vrs.at[step - 1], vrr.at[step - 1])
        go(send(spot, spot, vrs.at[step], vrr.at[step], right))
        spot = vslots.at[chip_at(place + step, chips)]
        arrived(spot, vls.at[step - 1], vlr.at[step - 1])
        if step < top - 1:
            go(send(spot, spot, vls.at[step], vlr.at[step], left))
    spot = vslots.at[chip_at(place - top, chips)]
    arrived(spot, vrs.at[top - 1], vrr.at[top - 1])
    vec_out[...] = jnp.sum(vslots[...], axis=0)
    total = pair_sum(len(order) - 1)
    arrived(rbuf.at[top - 1], rs.at[top - 1], rr.at[top - 1])
    arrived(lbuf.at[top - 1], ls.at[top - 1], lr.at[top - 1])
    out[...] = total + rbuf[top - 1].astype(jnp.float32) + lbuf[top - 1].astype(jnp.float32)
    for copy in started:
        copy.wait_send()


def scatter_rows(grads, vectors):
    count = lax.axis_size("dp")
    chips = count // 2
    top = chips // 2
    rows, width = grads.shape[0] // count, grads.shape[1]
    lines = vectors.shape[0] // 128
    dma, vmem = pltpu.SemaphoreType.DMA, pl.BlockSpec(memory_space=pltpu.VMEM)
    block = (rows, width)
    shard, sums = pl.pallas_call(
        lambda *refs: scatter_kernel(chips, *refs),
        out_shape=(
            jax.ShapeDtypeStruct(block, jnp.float32),
            jax.ShapeDtypeStruct((lines, 128), jnp.float32),
        ),
        in_specs=[vmem, vmem],
        out_specs=(vmem, vmem),
        scratch_shapes=[pltpu.VMEM((chips, *block), jnp.bfloat16)]
        + [pltpu.VMEM((top, *block), jnp.bfloat16)] * 4
        + [pltpu.VMEM((lines, 128), jnp.float32), pltpu.VMEM((chips, lines, 128), jnp.float32)]
        + [dma((chips,))] * 2
        + [dma((top,))] * 4
        + [dma((1,))] * 2
        + [dma((top,))] * 4,
        compiler_params=pltpu.CompilerParams(collective_id=1, has_side_effects=True),
        name="scatter_rows",
    )(grads.reshape(count, rows, width), vectors.reshape(lines, 128))
    return shard, sums.reshape(-1)


GELU_CUBE = 0.044715
POOL = 48
F32, BF16 = jnp.float32, jnp.bfloat16


def mm(left, right, dims=((1,), (0,))):
    return lax.dot_general(left, right, (dims, ((), ())), preferred_element_type=F32)


class Names:
    def __init__(self, names, refs):
        for name, ref in zip(names, refs):
            setattr(self, name, ref)


STAGED = ("lens", "tok", "cot", "gain", "shift", "b_qv", "b_out", "b_fc1", "b_fc2")
IN_NAMES = [
    "far_tok", "far_cot", "far_lens", "far_gain", "far_shift", "w_qkv", "far_b_qv", "w_out",
    "far_b_out", "w_fc1", "far_b_fc1", "w_fc2", "far_b_fc2",
]
OUT_NAMES = ["far_y", "far_gtok", "far_gqkv", "far_gout", "far_gfc1", "far_gfc2", "far_vec"]


def layer_scratch(chips, rows, row_count, width, heads, hidden, slots):
    count, top = 2 * chips, chips // 2
    dma = pltpu.SemaphoreType.DMA
    tall = (row_count, width)
    low = dict(
        wq=(count, 3, rows, heads), wo=(count, rows, heads),
        wf1=(count, rows, hidden), wf2=(count, rows, hidden),
        n1=tall, n2=tall, gy=tall, ghb=tall,
        z=(row_count, hidden), zp=(row_count, hidden),
        du=(row_count, hidden), dup=(row_count, hidden),
        qkv=(3, row_count, heads), o=(row_count, heads), op=(row_count, heads),
        dh=(row_count, heads),
        dqkv=(3, row_count, heads), dqkvp=(3, row_count, heads),
        xt=(4, 2, chips, rows, row_count), xtp=(4, chips, rows, row_count),
        grads=(3, chips, rows, hidden), rbuf=(3, 2, top, rows, hidden),
        ysend=(4, *tall), yrecv=(4, *tall), tok=tall, cot=tall,
    )
    full = dict(
        xh1=tall, xh2=tall, h1=tall, gh1=tall, rs1=(row_count, 1), rs2=(row_count, 1),
        u=(row_count, hidden), pf=(heads // HEAD_DIM, row_count, row_count),
        mask=(row_count, row_count), vec=(16, width), vecp=(16, width), vslots=(chips, 8, 128), vres=(16, width), vsum=(16, width),
        gain=(2, width), shift=(2, width), b_qv=(2, heads), b_out=(1, width),
        b_fc1=(1, hidden), b_fc2=(1, width),
        g_qkv=(3, rows, heads), g_out=(rows, heads), g_fc1=(rows, hidden), g_fc2=(rows, hidden),
    )
    sems = dict(
        pool=(POOL,), gr=(8, 2, top), pr=(8, chips + 1), sr=(12, 2, top), ar=(12,),
        yr=(4, 4), vr=(2, chips), loc=(8,), ins=(9,), outs=(9,),
    )
    shapes = {k: pltpu.VMEM(s, BF16) for k, s in low.items()}
    shapes |= {k: pltpu.VMEM(s, F32) for k, s in full.items()}
    shapes |= {k: dma(s) for k, s in sems.items()}
    shapes["lens"] = pltpu.SMEM((slots,), jnp.int32)
    return shapes


def layer_kernel(chips, scratch_names, *refs):
    r = Names(IN_NAMES + OUT_NAMES + scratch_names, refs)
    device, chip, core, place = ring_place(chips)
    side_y = lax.axis_index("tensor")
    count, top = 2 * chips, chips // 2
    right = 2 * chip_at(place + 1, chips) + core
    left = 2 * chip_at(place - 1, chips) + core
    partner = 2 * chip + 1 - core
    onward = (right, left)
    row_count, width = r.far_tok.shape
    rows, heads = r.w_out.shape
    hidden = r.w_fc1.shape[1]
    half_hidden = hidden // 2
    slots, issued = [None] * POOL, []

    class remote:
        def __init__(self, source, target, recv_sem, **where):
            self.parts = (source, target, recv_sem, where)

        def build(self, slot):
            source, target, recv_sem, where = self.parts
            return pltpu.make_async_remote_copy(
                src_ref=source, dst_ref=target, send_sem=r.pool.at[slot], recv_sem=recv_sem,
                device_id=where, device_id_type=pl.DeviceIdType.MESH,
            )

        def wait_recv(self):
            self.build(0).wait_recv()

    def go(send):
        slot = len(issued) % POOL
        issued.append(slot)
        if slots[slot] is not None:
            slots[slot].wait_send()
        slots[slot] = send.build(slot)
        slots[slot].start()

    barrier = pltpu.get_barrier_semaphore()

    def greet(**where):
        pl.semaphore_signal(
            barrier, inc=1, device_id=where, device_id_type=pl.DeviceIdType.MESH
        )

    for other in (right, left, partner):
        greet(dp=other)
    greet(tensor=1 - side_y)
    staged = []
    for j, name in enumerate(STAGED):
        copy = pltpu.make_async_copy(getattr(r, "far_" + name), getattr(r, name), r.ins.at[j])
        copy.start()
        staged.append(copy)
    pl.semaphore_wait(barrier, 4)

    base = (0, 0, 0, 0, 0, half_hidden, 0, half_hidden)
    span = (heads,) * 4 + (half_hidden,) * 4

    def cut(i, ref, side=None):
        start, size = base[i], span[i]
        if side is not None:
            size = size // 2
            start = start + side * size
        if start == 0 and size == ref.shape[-1]:
            return ref
        return ref.at[:, pl.ds(start, size)]

    def own(i):
        if i < 3:
            return r.w_qkv.at[i]
        return cut(i, (r.w_out, r.w_fc1, r.w_fc1, r.w_fc2, r.w_fc2)[i - 3])

    def spot_of(i, dev, side=None):
        if i < 3:
            return cut(i, r.wq.at[dev, i], side)
        return cut(i, (r.wo, r.wf1, r.wf1, r.wf2, r.wf2)[i - 3].at[dev], side)

    def block(i, step, whose, hop, side):
        dev = 2 * chip_at(place + step, chips) + whose
        return spot_of(i, dev, side if hop == top else None)

    def keep(i):
        return pltpu.make_async_copy(own(i), spot_of(i, device), r.loc.at[i])

    def start_item(i):
        mine, there = own(i), spot_of(i, device)
        for side in (0, 1):
            go(remote(mine, there, r.gr.at[i, side, 0], dp=onward[side]))
        go(remote(mine, there, r.pr.at[i, 0], dp=partner))
        keep(i).start()

    def hop_item(i, hop):
        for side, sign in ((0, -1), (1, 1)):
            here = block(i, sign * hop, core, hop, side)
            remote(
                here, here, r.gr.at[i, side, hop - 1], dp=onward[side]
            ).wait_recv()
            if hop < top:
                part = block(i, sign * hop, core, hop + 1, side)
                go(remote(
                    part, part, r.gr.at[i, side, hop], dp=onward[side]
                ))
            slot = 2 * hop - 1 + side
            go(remote(here, here, r.pr.at[i, slot], dp=partner))

    def finish_item(i):
        keep(i).wait()
        for slot in range(chips + 1):
            hop, side = (slot + 1) // 2, (slot + 1) % 2
            here = block(i, (-1, 1)[side] * hop, 1 - core, hop, side)
            remote(here, here, r.pr.at[i, slot], dp=partner).wait_recv()

    def swap(k, source, target):
        go(remote(source, target, r.ar.at[k], dp=partner))

    def swapped(k, target):
        remote(target, target, r.ar.at[k], dp=partner).wait_recv()

    quarter = width // 4
    group = count // 4

    def exchange(k, c):
        at = pl.ds(c * quarter, quarter)
        go(remote(
            r.ysend.at[k, :, at], r.yrecv.at[k, :, at], r.yr.at[k, c],
            tensor=1 - side_y,
        ))

    def exchanged(k):
        for c in range(4):
            spot = r.yrecv.at[k, :, pl.ds(c * quarter, quarter)]
            remote(spot, spot, r.yr.at[k, c], tensor=1 - side_y).wait_recv()

    scatter_span = hidden // 4
    half = scatter_span // 2

    def scatter_start(i):
        k, col = i // 4, (i % 4) * scatter_span
        far = r.grads.at[k, chip_at(place + top, chips)]
        for side in (0, 1):
            at = pl.ds(col + side * half, half)
            go(remote(
                far.at[:, at], r.rbuf.at[k, side, 0, :, at], r.sr.at[i, side, 0], dp=onward[side],
            ))

    def scatter_step(i, s):
        k, col = i // 4, (i % 4) * scatter_span
        for side, sign in ((0, 1), (1, -1)):
            target = chip_at(place + sign * (top - s), chips)
            at = pl.ds(col + side * half, half) if s == 1 else pl.ds(col, scatter_span)
            spot = r.rbuf.at[k, side, s - 1, :, at]
            remote(
                spot, spot, r.sr.at[i, side, s - 1], dp=onward[side]
            ).wait_recv()
            total = r.grads[k, target, :, at].astype(F32) + spot[...].astype(F32)
            r.grads[k, target, :, at] = total.astype(BF16)
            at = pl.ds(col, scatter_span)
            go(remote(
                r.grads.at[k, target, :, at], r.rbuf.at[k, side, s, :, at],
                r.sr.at[i, side, s], dp=onward[side],
            ))

    def scatter_end(i):
        k, col = i // 4, (i % 4) * scatter_span
        at = pl.ds(col, scatter_span)
        total = r.grads[k, chip, :, at].astype(F32)
        for side in (0, 1):
            spot = r.rbuf.at[k, side, top - 1, :, at]
            remote(
                spot, spot, r.sr.at[i, side, top - 1], dp=onward[side]
            ).wait_recv()
            total = total + spot[...].astype(F32)
        if k == 0:
            r.g_fc2[:, at] = total
        elif k == 1:
            r.g_fc1[:, at] = total
        elif i < 11:
            r.g_qkv[i - 8] = total
            put(r.g_qkv.at[i - 8], r.far_gqkv.at[i - 8])
        else:
            r.g_out[...] = total
            put(r.g_out, r.far_gout)

    order = [(i, s) for s in range(1, top) for i in range(4)]
    order += [(4 + i, s) for s in range(1, top) for i in range(4)]
    order += [(i, s) for s in range(1, top) for i in (11, 8, 9, 10)]
    steps = iter(order)

    def advance(n):
        for _ in range(n):
            scatter_step(*next(steps))

    put_copies = []

    def put(source, target):
        copy = pltpu.make_async_copy(source, target, r.outs.at[len(put_copies)])
        copy.start()
        put_copies.append(copy)

    def grad_tile(k, column, size, terms):
        total = None
        for lhs, rhs in terms:
            part = mm(lhs.reshape(chips * rows, row_count), rhs)
            total = part if total is None else total + part
        r.grads[k, :, :, pl.ds(column, size)] = total.reshape(chips, rows, size).astype(BF16)

    chunk = 32

    def row_loop(fn, carry=()):
        def step(i, c):
            return fn(pl.ds(pl.multiple_of(i * chunk, chunk), chunk), i * chunk, c)
        return lax.fori_loop(0, row_count // chunk, step, carry)

    def fold(value):
        return jnp.sum(value.reshape(chunk // 8, 8, value.shape[1]), axis=0)

    def transposed(k, source):
        per = 2 * rows
        for c in range(chips):
            flipped = source[:, c * per : (c + 1) * per].T
            r.xt[k, 0, c] = flipped[:rows]
            r.xt[k, 1, c] = flipped[rows:]
        swap(k, r.xt.at[k, 1 - core], r.xtp.at[k])

    for i in range(4):
        start_item(i)
    for copy in staged:
        copy.wait()
    ends = []
    for j in range(r.lens.shape[0]):
        ends.append(r.lens[j] if j == 0 else ends[-1] + r.lens[j])
    at_row = lax.broadcasted_iota(jnp.int32, (row_count, row_count), 0)
    at_col = lax.broadcasted_iota(jnp.int32, (row_count, row_count), 1)
    seg_row = sum((at_row >= e).astype(jnp.int32) for e in ends)
    seg_col = sum((at_col >= e).astype(jnp.int32) for e in ends)
    allowed = (seg_row == seg_col) & (at_row >= at_col)
    r.mask[...] = allowed.astype(F32)
    r.vec[...] = jnp.zeros_like(r.vec)

    def is_live(first):
        return first + lax.broadcasted_iota(jnp.int32, (chunk, width), 0) < ends[-1]

    def first_norm(at, first, c):
        x = r.tok[at, :].astype(F32)
        x = x - jnp.mean(x, axis=1, keepdims=True)
        inv = lax.rsqrt(jnp.mean(x * x, axis=1, keepdims=True) + NORM_EPS)
        x = x * inv
        r.xh1[at, :] = x
        r.rs1[at, :] = inv
        r.n1[at, :] = (x * r.gain[0:1, :] + r.shift[0:1, :]).astype(BF16)
        g = jnp.where(is_live(first), r.cot[at, :].astype(F32), 0.0)
        r.gy[at, :] = g.astype(BF16)
        return (c[0] + fold(g),)

    (total,) = row_loop(first_norm, (jnp.zeros((8, width), F32),))
    r.vec[8:9, :] = jnp.sum(total, axis=0, keepdims=True)
    for i in range(4):
        hop_item(i, 1)
    transposed(0, r.n1)
    for i in range(4):
        hop_item(i, 2)
    transposed(1, r.gy)
    for i in range(4):
        hop_item(i, 3)
    start_item(4)
    start_item(5)
    start_item(6)

    for i in range(3):
        hop_item(i, 4)
        finish_item(i)
        part = mm(r.n1[...], r.wq[:, i].reshape(width, heads))
        if i != 1:
            part = part + r.b_qv[i // 2 : i // 2 + 1, :]
        r.qkv[i] = part.astype(BF16)
    hop_item(3, 4)
    hop_item(4, 1)
    lane = lax.broadcasted_iota(jnp.int32, (1, 2 * HEAD_DIM), 1)
    picks = [(lane // HEAD_DIM == j).astype(F32).astype(BF16) for j in (0, 1)]
    first_half = lax.broadcasted_iota(jnp.int32, (row_count, 2 * HEAD_DIM), 1) < HEAD_DIM
    pairs = heads // (2 * HEAD_DIM)
    scale = HEAD_DIM ** (-0.5)
    between = [(5, 1), (6, 1), (4, 2), (5, 2)]
    for p in range(pairs):
        at = pl.ds(p * 2 * HEAD_DIM, 2 * HEAD_DIM)
        q, k, v = r.qkv[0, :, at], r.qkv[1, :, at], r.qkv[2, :, at]
        mixed = []
        for j in (0, 1):
            s = mm(q * picks[j], k, ((1,), (1,))) * scale
            s = jnp.where(r.mask[...] > 0.5, s, -1e30)
            e = jnp.exp(s - jnp.max(s, axis=1, keepdims=True))
            e = e / jnp.sum(e, axis=1, keepdims=True)
            r.pf[2 * p + j] = e
            mixed.append(mm(e.astype(BF16), v))
        r.o[:, at] = jnp.where(first_half, mixed[0], mixed[1]).astype(BF16)
        hop_item(*between[p])
    start_item(7)
    finish_item(3)
    for c in range(4):
        w = r.wo[c * group : (c + 1) * group].reshape(quarter, heads)
        r.ysend[0, :, pl.ds(c * quarter, quarter)] = mm(r.o[...], w, ((1,), (1,))).astype(BF16)
        exchange(0, c)
    swap(8, r.o, r.op)
    hop_item(4, 3)
    hop_item(5, 3)
    hop_item(6, 2)
    hop_item(7, 1)
    exchanged(0)

    def second_norm(at, first, c):
        x = r.tok[at, :].astype(F32)
        x = x + (r.ysend[0, at, :].astype(F32) + r.yrecv[0, at, :].astype(F32)) + r.b_out[...]
        r.h1[at, :] = x
        x = x - jnp.mean(x, axis=1, keepdims=True)
        inv = lax.rsqrt(jnp.mean(x * x, axis=1, keepdims=True) + NORM_EPS)
        x = x * inv
        r.xh2[at, :] = x
        r.rs2[at, :] = inv
        r.n2[at, :] = (x * r.gain[1:2, :] + r.shift[1:2, :]).astype(BF16)
        return c

    row_loop(second_norm)
    transposed(2, r.n2)
    hop_item(4, 4)
    hop_item(5, 4)
    finish_item(4)
    finish_item(5)

    tile = hidden // 4
    later = [(), (6, 3), (7, 2), (6, 4)]
    for t in range(4):
        at = pl.ds(t * tile, tile)
        r.u[:, at] = mm(r.n2[...], r.wf1[:, :, at].reshape(width, tile)) + r.b_fc1[:, at]

        def gelu(rows_at, first, c):
            u = r.u[rows_at, at]
            t_ = jnp.tanh(GELU_COEF * (u + GELU_CUBE * u * u * u))
            r.z[rows_at, at] = (0.5 * u * (1.0 + t_)).astype(BF16)
            r.u[rows_at, at] = 0.5 * (1.0 + t_) + 0.5 * u * (1.0 - t_ * t_) * GELU_COEF * (
                1.0 + 3.0 * GELU_CUBE * u * u
            )
            return c

        row_loop(gelu)
        if t % 2 == 1:
            cols = pl.ds((t // 2) * half_hidden, half_hidden)
            swap(4 + t // 2, r.z.at[:, cols], r.zp.at[:, cols])
        if later[t]:
            hop_item(*later[t])
    swapped(1, r.xtp.at[1])
    for h in (0, 1):
        cols = pl.ds(h * half_hidden, half_hidden)
        swapped(4 + h, r.zp.at[:, cols])
        for t in (2 * h, 2 * h + 1):
            at = pl.ds(t * tile, tile)
            grad_tile(0, t * tile, tile, ((r.xt[1, core], r.z[:, at]), (r.xtp[1], r.zp[:, at])))
            scatter_start(t)
        hop_item(7, 3 + h)
    finish_item(6)
    finish_item(7)
    for t in range(4):
        at = pl.ds(t * tile, tile)
        d = mm(r.gy[...], r.wf2[:, :, at].reshape(width, tile)) * r.u[:, at]
        d = d.astype(BF16)
        r.du[:, at] = d
        row, col = (t * tile) // width, (t * tile) % width
        r.vec[6 + row : 7 + row, col : col + tile] = jnp.sum(
            d.astype(F32), axis=0, keepdims=True
        )
        if t % 2 == 1:
            cols = pl.ds((t // 2) * half_hidden, half_hidden)
            swap(6 + t // 2, r.du.at[:, cols], r.dup.at[:, cols])
        advance(1)
    for c in range(4):
        w = r.wf1[c * group : (c + 1) * group].reshape(quarter, hidden)
        r.ysend[1, :, pl.ds(c * quarter, quarter)] = mm(r.du[...], w, ((1,), (1,))).astype(BF16)
        exchange(1, c)
        advance(1)
    swapped(2, r.xtp.at[2])
    for h in (0, 1):
        cols = pl.ds(h * half_hidden, half_hidden)
        swapped(6 + h, r.dup.at[:, cols])
        for t in (2 * h, 2 * h + 1):
            at = pl.ds(t * tile, tile)
            grad_tile(1, t * tile, tile, ((r.xt[2, core], r.du[:, at]), (r.xtp[2], r.dup[:, at])))
            scatter_start(4 + t)
            advance(1)
    for j in range(1, chips):
        greet(dp=2 * lax.rem(chip + j, chips) + core)
    for c in range(4):
        w = r.wf2[c * group : (c + 1) * group].reshape(quarter, hidden)
        r.ysend[2, :, pl.ds(c * quarter, quarter)] = mm(r.z[...], w, ((1,), (1,))).astype(BF16)
        exchange(2, c)
    advance(2)
    exchanged(1)

    def norm_back(k, gain_row, xh, rs, above, store):
        def step(at, first, c):
            dn = r.ysend[k, at, :].astype(F32) + r.yrecv[k, at, :].astype(F32)
            x = xh[at, :]
            scaled = dn * r.gain[gain_row : gain_row + 1, :]
            m1 = jnp.mean(scaled, axis=1, keepdims=True)
            m2 = jnp.mean(scaled * x, axis=1, keepdims=True)
            g = above[at, :].astype(F32) + rs[at, :] * (scaled - m1 - x * m2)
            store(at, g)
            return (c[0] + fold(dn * x), c[1] + fold(dn), c[2] + fold(g))

        zero = jnp.zeros((8, width), F32)
        return [jnp.sum(s, axis=0, keepdims=True) for s in row_loop(step, (zero, zero, zero))]

    def store_gh1(at, g):
        r.gh1[at, :] = g
        r.ghb[at, :] = g.astype(BF16)

    sums = norm_back(1, 1, r.xh2, r.rs2, r.gy, store_gh1)
    r.vec[1:2, :] = sums[0]
    r.vec[3:4, :] = sums[1]
    r.vec[5:6, :] = sums[2]
    transposed(3, r.ghb)
    advance(1)

    r.dh[...] = mm(r.ghb[...], r.wo[...].reshape(width, heads)).astype(BF16)
    for p in range(pairs):
        at = pl.ds(p * 2 * HEAD_DIM, 2 * HEAD_DIM)
        q, k, v = r.qkv[0, :, at], r.qkv[1, :, at], r.qkv[2, :, at]
        d_out, o = r.dh[:, at], r.o[:, at]
        parts = []
        for j in (0, 1):
            mine = d_out * picks[j]
            delta = jnp.sum(mine.astype(F32) * o.astype(F32), axis=1, keepdims=True)
            prob = r.pf[2 * p + j]
            ds = (prob * (mm(mine, v, ((1,), (1,))) - delta) * scale).astype(BF16)
            parts.append((
                mm(ds, k),
                mm(ds, q, ((0,), (0,))),
                mm(prob.astype(BF16), d_out, ((0,), (0,))),
            ))
        for i in range(3):
            r.dqkv[i, :, at] = jnp.where(first_half, parts[0][i], parts[1][i]).astype(BF16)
        advance((1, 1, 2, 1)[p])
    swap(9, r.dqkv, r.dqkvp)
    swapped(3, r.xtp.at[3])
    swapped(8, r.op)
    grad_tile(2, 3 * heads, heads, ((r.xt[3, core], r.o[...]), (r.xtp[3], r.op[...])))
    scatter_start(11)
    for c in range(4):
        total = None
        for i in range(3):
            w = r.wq[c * group : (c + 1) * group, i].reshape(quarter, heads)
            part = mm(r.dqkv[i], w, ((1,), (1,)))
            total = part if total is None else total + part
        r.ysend[3, :, pl.ds(c * quarter, quarter)] = total.astype(BF16)
        exchange(3, c)
        if c % 2 == 1:
            advance(1)
    for i in (0, 2):
        r.vec[4:5, pl.ds((i // 2) * heads, heads)] = jnp.sum(
            r.dqkv[i].astype(F32), axis=0, keepdims=True
        )
    swapped(0, r.xtp.at[0])
    swapped(9, r.dqkvp)
    for i in range(3):
        grad_tile(
            2, i * heads, heads, ((r.xt[0, core], r.dqkv[i]), (r.xtp[0], r.dqkvp[i]))
        )
        scatter_start(8 + i)
    advance(1)
    for i in range(4):
        scatter_end(i)
    put(r.g_fc2, r.far_gfc2)
    advance(1)
    exchanged(2)

    def finish_output(at, first, c):
        y = r.h1[at, :] + (r.ysend[2, at, :].astype(F32) + r.yrecv[2, at, :].astype(F32))
        y = jnp.where(is_live(first), y + r.b_fc2[...], 0.0)
        r.n2[at, :] = y.astype(BF16)
        return c

    row_loop(finish_output)
    put(r.n2, r.far_y)
    advance(4)
    exchanged(3)

    def store_tokens(at, g):
        r.gh1[at, :] = g

    sums = norm_back(3, 0, r.xh1, r.rs1, r.gh1, store_tokens)
    r.vec[0:1, :] = sums[0]
    r.vec[2:3, :] = sums[1]
    put(r.gh1, r.far_gtok)

    swap(10, r.vec, r.vecp)
    top_row = pl.multiple_of(8 * core, 8)

    def tile_of(ref, which):
        return ref.at[pl.ds(top_row, 8), pl.ds(pl.multiple_of(128 * which, 128), 128)]

    def tile_copy(stage, j, source, target):
        other = lax.rem(chip + j, chips)
        return remote(
            source, target, r.vr.at[stage, j], dp=2 * other + core
        )

    advance(1)
    swapped(10, r.vecp)
    r.vres[...] = r.vec[...] + r.vecp[...]
    pl.semaphore_wait(barrier, chips - 1)
    for j in range(1, chips):
        go(tile_copy(0, j, tile_of(r.vres, lax.rem(chip + j, chips)), r.vslots.at[chip]))
    r.vslots[chip] = tile_of(r.vres, chip)[...]
    advance(3)
    for i in range(4, 8):
        scatter_end(i)
    put(r.g_fc1, r.far_gfc1)
    for j in range(1, chips):
        spot = r.vslots.at[lax.rem(chip + chips - j, chips)]
        tile_copy(0, j, spot, spot).wait_recv()
    mine = tile_of(r.vsum, chip)
    mine[...] = jnp.sum(r.vslots[...], axis=0)
    for j in range(1, chips):
        go(tile_copy(1, j, mine, mine))
    advance(4)
    assert next(steps, None) is None
    for j in range(1, chips):
        spot = tile_of(r.vsum, lax.rem(chip + chips - j, chips))
        tile_copy(1, j, spot, spot).wait_recv()
    rows_here = r.vsum.at[pl.ds(top_row, 8), :]
    swap(11, rows_here, rows_here)
    swapped(11, r.vsum.at[pl.ds(pl.multiple_of(8 * (1 - core), 8), 8), :])
    put(r.vsum, r.far_vec)
    for i in (11, 8, 9, 10):
        scatter_end(i)
    for copy in put_copies:
        copy.wait()
    for copy in slots:
        copy.wait_send()


def one_kernel(tokens, cotangent, seq_lens, gain, shift, w_qkv, b_qv, w_out, b_out, w_fc1, b_fc1, w_fc2, b_fc2):
    chips = lax.axis_size("dp") // 2
    row_count, width = tokens.shape
    rows, heads = w_out.shape
    hidden = w_fc1.shape[1]
    vmem, hbm = pl.BlockSpec(memory_space=pltpu.VMEM), pl.BlockSpec(memory_space=pl.ANY)
    scratch = layer_scratch(chips, rows, row_count, width, heads, hidden, seq_lens.shape[0])
    names = list(scratch)

    def made(*shape, kind=F32):
        return jax.ShapeDtypeStruct(shape, kind)

    outs = pl.pallas_call(
        lambda *refs: layer_kernel(chips, names, *refs),
        out_shape=(
            made(row_count, width, kind=BF16), made(row_count, width), made(3, rows, heads),
            made(rows, heads), made(rows, hidden), made(rows, hidden), made(16, width),
        ),
        in_specs=[hbm] * 13,
        out_specs=(hbm,) * 7,
        scratch_shapes=list(scratch.values()),
        compiler_params=pltpu.CompilerParams(
            collective_id=2, has_side_effects=True, vmem_limit_bytes=63 * 2**20
        ),
        name="layer",
    )(
        tokens, cotangent, seq_lens, gain, shift, w_qkv, b_qv, w_out, b_out[None], w_fc1,
        b_fc1[None], w_fc2, b_fc2[None],
    )
    small = ((2, width), (2, width), (2, heads), (1, width), (1, hidden), (1, width))
    outs = pl.pallas_call(
        lambda *refs: results_kernel(heads, *refs),
        out_shape=tuple(made(*o.shape, kind=o.dtype) for o in outs[:6])
        + tuple(made(*o) for o in small),
        in_specs=[vmem] * 7,
        out_specs=(hbm,) * 6 + (vmem,) * 6,
        scratch_shapes=[pltpu.SemaphoreType.DMA((6,))],
        name="results",
    )(*outs)
    y, g_tok, g_qkv, g_out, g_fc1, g_fc2, g_gain, g_shift, g_bqv, g_bout, g_bfc1, g_bfc2 = outs
    return (
        y, g_tok, g_gain, g_shift, g_qkv, g_bqv, g_out, g_bout.reshape(-1), g_fc1,
        g_bfc1.reshape(-1), g_fc2, g_bfc2.reshape(-1),
    )


def results_kernel(heads, *refs):
    sources, vec, targets, sem = refs[:6], refs[6], refs[7:13], refs[19]
    gain, shift, bqv, bout, bfc1, bfc2 = refs[13:19]
    copies = [
        pltpu.make_async_copy(source, target, sem.at[i])
        for i, (source, target) in enumerate(zip(sources, targets))
    ]
    for copy in copies:
        copy.start()
    width = vec.shape[1]
    gain[...] = vec[0:2, :]
    shift[...] = vec[2:4, :]
    bqv[0:1, :] = vec[4:5, :heads]
    bqv[1:2, :] = vec[4:5, heads : 2 * heads]
    bout[...] = vec[5:6, :]
    for j in range(bfc1.shape[1] // width):
        bfc1[:, j * width : (j + 1) * width] = vec[6 + j : 7 + j, :]
    bfc2[...] = vec[8:9, :]
    for copy in copies:
        copy.wait()


def fits_one_kernel(tokens, w_out, w_fc1):
    chips = lax.axis_size("dp") // 2
    rows, heads = w_out.shape
    width, hidden = tokens.shape[1], w_fc1.shape[1]
    return (
        lax.axis_size("tensor") == 2
        and chips == 2 * 4
        and width == 128 * chips
        and rows % 16 == 0
        and tokens.shape[0] % 32 == 0
        and 2 * heads == width
        and 4 * heads == hidden
    )


def body(
    tokens,
    cotangent,
    seq_lens,
    layer_norm_gain,
    layer_norm_bias,
    w_qkv,
    b_qv,
    w_out,
    b_out,
    w_fc1,
    b_fc1,
    w_fc2,
    b_fc2,
):
    if fits_one_kernel(tokens, w_out, w_fc1):
        return one_kernel(
            tokens, cotangent, seq_lens, layer_norm_gain, layer_norm_bias, w_qkv, b_qv, w_out,
            b_out, w_fc1, b_fc1, w_fc2, b_fc2,
        )
    heads_width, hidden_width = w_out.shape[1], w_fc1.shape[1]
    attn_shards = jnp.concatenate([w_qkv[0], w_qkv[1], w_qkv[2], w_out], axis=1)
    mlp_shards = jnp.concatenate([w_fc1, w_fc2], axis=1)
    mlp_full = lax.all_gather(mlp_shards, "dp", axis=0, tiled=True)
    attn_full = gather_rows(attn_shards)
    qkv_full, out_full = attn_full[:, : 3 * heads_width], attn_full[:, 3 * heads_width :]
    fc1_full, fc2_full = mlp_full[:, :hidden_width], mlp_full[:, hidden_width:]
    allowed, live_rows = seq_masks(seq_lens, tokens.shape[0])
    input_tokens = tokens.astype(jnp.float32)
    first_normalized, first_centered_scaled, first_inverse_deviation = layer_norm_forward(
        input_tokens, layer_norm_gain[0], layer_norm_bias[0]
    )
    low1 = first_normalized.astype(jnp.bfloat16)
    proj = product("td,dc->tc", low1, qkv_full)
    query = (proj[:, :heads_width] + b_qv[0]).astype(jnp.bfloat16)
    key_rows = proj[:, heads_width : 2 * heads_width].astype(jnp.bfloat16)
    value = (proj[:, 2 * heads_width :] + b_qv[1]).astype(jnp.bfloat16)
    heads_out, logsum = attend(query, key_rows, value, allowed)
    attn_part = product("tc,dc->td", heads_out, out_full)
    attn_mix = sum_tensor(attn_part)
    first_hidden_state = input_tokens + attn_mix + b_out
    second_normalized, second_centered_scaled, second_inverse_deviation = layer_norm_forward(
        first_hidden_state, layer_norm_gain[1], layer_norm_bias[1]
    )
    low2 = second_normalized.astype(jnp.bfloat16)
    pre_act = jnp.dot(low2, fc1_full, preferred_element_type=jnp.float32) + b_fc1
    act, slope = gelu_parts(pre_act)
    act_low = act.astype(jnp.bfloat16)
    mlp_part = product("tf,df->td", act_low, fc2_full)
    mlp_mix = sum_tensor(mlp_part)
    result = first_hidden_state + mlp_mix + b_fc2
    output = jnp.where(live_rows[:, None], result, 0.0).astype(jnp.bfloat16)
    qkv_back, out_back, fc1_back, fc2_back = (qkv_full, out_full, fc1_full, fc2_full)
    grad_y = jnp.where(live_rows[:, None], cotangent, jnp.zeros_like(cotangent))
    flat_output_gradient = grad_y.astype(jnp.float32)
    d_pre = (jnp.dot(grad_y, fc2_back, preferred_element_type=jnp.float32) * slope).astype(
        jnp.bfloat16
    )
    g_fc2 = product("td,tf->df", grad_y, act_low)
    g_bfc2 = jnp.sum(flat_output_gradient, axis=0)
    g_fc1 = product("td,tf->df", low2, d_pre)
    g_mlp = jnp.concatenate([g_fc1.astype(jnp.bfloat16), g_fc2.astype(jnp.bfloat16)], axis=1)
    shard_mlp = lax.psum_scatter(g_mlp, "dp", scatter_dimension=0, tiled=True)
    g_bfc1 = jnp.sum(d_pre.astype(jnp.float32), axis=0)
    d_norm2_part = product("tf,df->td", d_pre, fc1_back)
    second_norm_delta = sum_tensor(d_norm2_part)
    second_gain_gradient = jnp.sum(second_norm_delta * second_centered_scaled, axis=0)
    g_shift2 = jnp.sum(second_norm_delta, axis=0)
    hidden_first_gradient = flat_output_gradient + layer_norm_backward(
        second_norm_delta, layer_norm_gain[1], second_centered_scaled, second_inverse_deviation
    )
    grad_low = hidden_first_gradient.astype(jnp.bfloat16)
    g_out = product("td,tc->dc", grad_low, heads_out)
    g_bout = jnp.sum(hidden_first_gradient, axis=0)
    d_heads = jnp.dot(grad_low, out_back, preferred_element_type=jnp.float32).astype(jnp.bfloat16)
    d_query, d_key, d_value = attend_back(
        query, key_rows, value, heads_out, d_heads, logsum, allowed
    )
    stacked = jnp.concatenate([d_query, d_key, d_value], axis=1)
    g_qkv = product("td,tc->dc", low1, stacked)
    g_attn = jnp.concatenate([g_qkv.astype(jnp.bfloat16), g_out.astype(jnp.bfloat16)], axis=1)
    g_bqv = jnp.stack(
        [jnp.sum(d_query.astype(jnp.float32), axis=0), jnp.sum(d_value.astype(jnp.float32), axis=0)]
    )
    d_norm1_part = product("tc,dc->td", stacked, qkv_back)
    first_norm_delta = sum_tensor(d_norm1_part)
    first_gain_gradient = jnp.sum(first_norm_delta * first_centered_scaled, axis=0)
    g_shift1 = jnp.sum(first_norm_delta, axis=0)
    input_gradient = hidden_first_gradient + layer_norm_backward(
        first_norm_delta, layer_norm_gain[0], first_centered_scaled, first_inverse_deviation
    )
    shard_mlp = shard_mlp.astype(jnp.float32)
    shard_fc1, shard_fc2 = shard_mlp[:, :hidden_width], shard_mlp[:, hidden_width:]
    vectors = jnp.concatenate(
        [
            first_gain_gradient,
            second_gain_gradient,
            g_shift1,
            g_shift2,
            g_bqv.reshape(-1),
            g_bout,
            g_bfc1,
            g_bfc2,
        ]
    )
    shard_attn, vectors = scatter_rows(g_attn, vectors)
    shard_qkv = jnp.stack([shard_attn[:, i * heads_width : (i + 1) * heads_width] for i in range(3)])
    shard_out = shard_attn[:, 3 * heads_width :]
    width = tokens.shape[1]
    cuts = [2 * width, 4 * width, 4 * width + 2 * heads_width]
    cuts += [cuts[-1] + width, cuts[-1] + width + hidden_width]
    gain_sum, shift_sum, bqv_sum, bout_sum, bfc1_sum, bfc2_sum = jnp.split(vectors, cuts)
    gain_sum, shift_sum = gain_sum.reshape(2, width), shift_sum.reshape(2, width)
    bqv_sum = bqv_sum.reshape(2, heads_width)
    return (
        output,
        input_gradient,
        gain_sum,
        shift_sum,
        shard_qkv,
        bqv_sum,
        shard_out,
        bout_sum,
        shard_fc1,
        bfc1_sum,
        shard_fc2,
        bfc2_sum,
    )


def solution(mesh):
    in_specs = (
        P("dp", None),
        P("dp", None),
        P("dp"),
        P(),
        P(),
        P(None, "dp", "tensor"),
        P(None, "tensor"),
        P("dp", "tensor"),
        P(),
        P("dp", "tensor"),
        P("tensor"),
        P("dp", "tensor"),
        P(),
    )
    out_specs = (
        P("dp", None),
        P("dp", None),
        P(),
        P(),
        P(None, "dp", "tensor"),
        P(None, "tensor"),
        P("dp", "tensor"),
        P(),
        P("dp", "tensor"),
        P("tensor"),
        P("dp", "tensor"),
        P(),
    )
    return jax.shard_map(body, mesh=mesh, in_specs=in_specs, out_specs=out_specs, check_vma=False)
```

```python
import jax
import jax.numpy as jnp
from jax import lax
from jax.experimental import pallas as pl
from jax.experimental.pallas import tpu as pltpu
from jax.sharding import PartitionSpec as P

HEAD_DIM = 64


NORM_EPS = 1e-05
GELU_COEF = 0.7978845608028654


def product(spec, left, right):
    return jnp.einsum(spec, left, right, preferred_element_type=jnp.float32)


def seq_masks(lengths, row_count):
    slots = jnp.arange(lengths.shape[0])
    ends = jnp.sum(jnp.where(slots[:, None] <= slots[None, :], lengths[:, None], 0), axis=0)
    places = jnp.arange(row_count, dtype=jnp.int32)
    segment = jnp.sum((places[:, None] >= ends[None, :]).astype(jnp.int32), axis=1)
    allowed = (segment[:, None] == segment[None, :]) & (places[:, None] >= places[None, :])
    live_rows = places < ends[-1]
    return (allowed, live_rows)


def layer_norm_forward(hidden, gain, shift):
    center = hidden - jnp.mean(hidden, axis=-1, keepdims=True)
    inv_std = lax.rsqrt(jnp.mean(center * center, axis=-1, keepdims=True) + NORM_EPS)
    normal_x = center * inv_std
    return (normal_x * gain + shift, normal_x, inv_std)


def layer_norm_backward(grad_out, gain, normal_x, inv_std):
    scaled = grad_out * gain
    return inv_std * (
        scaled
        - jnp.mean(scaled, axis=-1, keepdims=True)
        - normal_x * jnp.mean(scaled * normal_x, axis=-1, keepdims=True)
    )


def gelu_parts(pre_act):
    inner = GELU_COEF * (pre_act + 0.044715 * pre_act * pre_act * pre_act)
    tanh_val = jnp.tanh(inner)
    value = 0.5 * pre_act * (1.0 + tanh_val)
    slope = 0.5 * (1.0 + tanh_val) + 0.5 * pre_act * (1.0 - tanh_val * tanh_val) * GELU_COEF * (
        1.0 + 3.0 * 0.044715 * pre_act * pre_act
    )
    return (value, slope)


def split_heads(matrix):
    return matrix.reshape(matrix.shape[0], matrix.shape[1] // HEAD_DIM, HEAD_DIM)


def head_scores(query, key_rows, allowed):
    scores = product("qhd,khd->hqk", split_heads(query), split_heads(key_rows)) * HEAD_DIM ** (-0.5)
    return jnp.where(allowed[None], scores, -1e30)


def attend(query, key_rows, value, allowed):
    scores = head_scores(query, key_rows, allowed)
    row_max = jnp.max(scores, axis=-1, keepdims=True)
    logsum = row_max + jnp.log(jnp.sum(jnp.exp(scores - row_max), axis=-1, keepdims=True))
    weights = jnp.exp(scores - logsum).astype(jnp.bfloat16)
    mixed = product("hqk,khd->qhd", weights, split_heads(value)).astype(jnp.bfloat16)
    return (mixed.reshape(query.shape[0], -1), logsum)


def attend_back(query, key_rows, value, heads_out, d_heads, logsum, allowed):
    scores = head_scores(query, key_rows, allowed)
    probs = jnp.exp(scores - logsum)
    probs_low = probs.astype(jnp.bfloat16)
    d_split = split_heads(d_heads)
    d_prob = product("qhd,khd->hqk", d_split, split_heads(value))
    delta = jnp.sum(
        d_split.astype(jnp.float32) * split_heads(heads_out).astype(jnp.float32), axis=-1
    )
    d_score = (probs * (d_prob - jnp.transpose(delta)[:, :, None]) * HEAD_DIM ** (-0.5)).astype(
        jnp.bfloat16
    )
    d_query = product("hqk,khd->qhd", d_score, split_heads(key_rows)).astype(jnp.bfloat16)
    d_key = product("hqk,qhd->khd", d_score, split_heads(query)).astype(jnp.bfloat16)
    d_value = product("hqk,qhd->khd", probs_low, d_split).astype(jnp.bfloat16)
    row_count = query.shape[0]
    return (
        d_query.reshape(row_count, -1),
        d_key.reshape(row_count, -1),
        d_value.reshape(row_count, -1),
    )


def sum_tensor(part):
    low = lax.optimization_barrier(part.astype(jnp.bfloat16))
    count = lax.axis_size("tensor")
    if count != 2:
        return lax.psum(low, "tensor").astype(jnp.float32)
    other = lax.ppermute(low, "tensor", [(0, 1), (1, 0)])
    return low.astype(jnp.float32) + other.astype(jnp.float32)


def chip_at(place, chips):
    place = (place + chips) % chips
    back = place // (chips // 2)
    return 2 * (place * (1 - back) + (chips - 1 - place) * back) + back


def ring_place(chips):
    device = lax.axis_index("dp")
    core, chip = device % 2, device // 2
    column, row = chip % 2, chip // 2
    place = row * (1 - column) + (chips - 1 - row) * column
    return device, chip, core, place


def send(source, target, send_sem, recv_sem, device):
    return pltpu.make_async_remote_copy(
        src_ref=source,
        dst_ref=target,
        send_sem=send_sem,
        recv_sem=recv_sem,
        device_id={"dp": device},
        device_id_type=pl.DeviceIdType.MESH,
    )


def meet(devices):
    barrier = pltpu.get_barrier_semaphore()
    for device in devices:
        pl.semaphore_signal(
            barrier, inc=1, device_id={"dp": device}, device_id_type=pl.DeviceIdType.MESH
        )
    pl.semaphore_wait(barrier, len(devices))


def gather_kernel(chips, own, out, rs, rr, ls, lr, ps, pr, own_sem):
    device, chip, core, place = ring_place(chips)
    right = 2 * chip_at(place + 1, chips) + core
    left = 2 * chip_at(place - 1, chips) + core
    partner = 2 * chip + 1 - core
    meet((right, left, partner))
    top, width = chips // 2, own.shape[1]
    half = width // 2

    def block(step, whose, hop, side):
        at = out.at[2 * chip_at(place + step, chips) + whose]
        if hop < top:
            return at
        return at.at[:, pl.ds(side * half, half)]

    started = []

    def go(copy):
        copy.start()
        started.append(copy)

    go(send(own, out.at[device], rs.at[0], rr.at[0], right))
    go(send(own, out.at[device], ls.at[0], lr.at[0], left))
    go(send(own, out.at[device], ps.at[0], pr.at[0], partner))
    keep = pltpu.make_async_copy(own, out.at[device], own_sem)
    keep.start()
    passed = [block(0, 1 - core, 0, 0)]
    for hop in range(1, top + 1):
        for side, sign, s_sem, r_sem, onward in ((0, -1, rs, rr, right), (1, 1, ls, lr, left)):
            here = block(sign * hop, core, hop, side)
            send(here, here, s_sem.at[hop - 1], r_sem.at[hop - 1], onward).wait_recv()
            if hop < top:
                part = block(sign * hop, core, hop + 1, side)
                go(send(part, part, s_sem.at[hop], r_sem.at[hop], onward))
            slot = len(passed)
            go(send(here, here, ps.at[slot], pr.at[slot], partner))
            passed.append(block(sign * hop, 1 - core, hop, side))
    for slot, here in enumerate(passed):
        send(here, here, ps.at[slot], pr.at[slot], partner).wait_recv()
    for copy in started:
        copy.wait_send()
    keep.wait()


def gather_rows(shard):
    count = lax.axis_size("dp")
    chips = count // 2
    top = chips // 2
    dma = pltpu.SemaphoreType.DMA
    out = pl.pallas_call(
        lambda *refs: gather_kernel(chips, *refs),
        out_shape=jax.ShapeDtypeStruct((count, *shard.shape), shard.dtype),
        in_specs=[pl.BlockSpec(memory_space=pltpu.VMEM)],
        out_specs=pl.BlockSpec(memory_space=pl.ANY),
        scratch_shapes=[dma((top,))] * 4 + [dma((chips + 1,))] * 2 + [dma],
        compiler_params=pltpu.CompilerParams(collective_id=0, has_side_effects=True),
        name="gather_rows",
    )(shard)
    return out.reshape(count * shard.shape[0], shard.shape[1])


def scatter_kernel(
    chips, grads, vec, out, vec_out,
    pbuf, rbuf, lbuf, rstage, lstage, vpart, vslots,
    ps, pr, rs, rr, ls, lr, vps, vpr, vrs, vrr, vls, vlr,
):
    device, chip, core, place = ring_place(chips)
    right = 2 * chip_at(place + 1, chips) + core
    left = 2 * chip_at(place - 1, chips) + core
    partner = 2 * chip + 1 - core
    meet((right, left, partner))
    top, width = chips // 2, out.shape[1]
    half = width // 2
    low, high = pl.ds(0, half), pl.ds(half, half)
    started = []

    def go(copy):
        copy.start()
        started.append(copy)

    order = [top]
    for step in range(1, top):
        order += [top - step, step - top]
    order.append(0)
    go(send(vec, vpart, vps.at[0], vpr.at[0], partner))
    for slot, step in enumerate(order):
        mine = grads.at[2 * chip_at(place + step, chips) + 1 - core]
        go(send(mine, pbuf.at[slot], ps.at[slot], pr.at[slot], partner))

    def pair_sum(slot):
        spot = pbuf.at[slot]
        send(spot, spot, ps.at[slot], pr.at[slot], partner).wait_recv()
        mine = grads[2 * chip_at(place + order[slot], chips) + core]
        return mine.astype(jnp.float32) + pbuf[slot].astype(jnp.float32)

    def arrived(spot, s_sem, r_sem):
        send(spot, spot, s_sem, r_sem, partner).wait_recv()

    first = pair_sum(0).astype(jnp.bfloat16)
    rstage[0, :, :half] = first[:, :half]
    go(send(rstage.at[0, :, low], rbuf.at[0, :, low], rs.at[0], rr.at[0], right))
    lstage[0, :, half:] = first[:, half:]
    go(send(lstage.at[0, :, high], lbuf.at[0, :, high], ls.at[0], lr.at[0], left))
    arrived(vpart, vps.at[0], vpr.at[0])
    vslots[chip] = vec[...] + vpart[...]
    go(send(vslots.at[chip], vslots.at[chip], vrs.at[0], vrr.at[0], right))
    go(send(vslots.at[chip], vslots.at[chip], vls.at[0], vlr.at[0], left))
    for step in range(1, top):
        for side, buf, stage, s_sem, r_sem, onward in (
            (0, rbuf, rstage, rs, rr, right),
            (1, lbuf, lstage, ls, lr, left),
        ):
            total = pair_sum(2 * step - 1 + side)
            if step == 1:
                cols = (low, high)[side]
                arrived(buf.at[0, :, cols], s_sem.at[0], r_sem.at[0])
                more = buf[0, :, side * half : (side + 1) * half].astype(jnp.float32)
                if side == 0:
                    stage[step, :, :half] = (total[:, :half] + more).astype(jnp.bfloat16)
                    stage[step, :, half:] = total[:, half:].astype(jnp.bfloat16)
                else:
                    stage[step, :, :half] = total[:, :half].astype(jnp.bfloat16)
                    stage[step, :, half:] = (total[:, half:] + more).astype(jnp.bfloat16)
            else:
                arrived(buf.at[step - 1], s_sem.at[step - 1], r_sem.at[step - 1])
                stage[step] = (total + buf[step - 1].astype(jnp.float32)).astype(jnp.bfloat16)
            go(send(stage.at[step], buf.at[step], s_sem.at[step], r_sem.at[step], onward))
        spot = vslots.at[chip_at(place - step, chips)]
        arrived(spot, vrs.at[step - 1], vrr.at[step - 1])
        go(send(spot, spot, vrs.at[step], vrr.at[step], right))
        spot = vslots.at[chip_at(place + step, chips)]
        arrived(spot, vls.at[step - 1], vlr.at[step - 1])
        if step < top - 1:
            go(send(spot, spot, vls.at[step], vlr.at[step], left))
    spot = vslots.at[chip_at(place - top, chips)]
    arrived(spot, vrs.at[top - 1], vrr.at[top - 1])
    vec_out[...] = jnp.sum(vslots[...], axis=0)
    total = pair_sum(len(order) - 1)
    arrived(rbuf.at[top - 1], rs.at[top - 1], rr.at[top - 1])
    arrived(lbuf.at[top - 1], ls.at[top - 1], lr.at[top - 1])
    out[...] = total + rbuf[top - 1].astype(jnp.float32) + lbuf[top - 1].astype(jnp.float32)
    for copy in started:
        copy.wait_send()


def scatter_rows(grads, vectors):
    count = lax.axis_size("dp")
    chips = count // 2
    top = chips // 2
    rows, width = grads.shape[0] // count, grads.shape[1]
    lines = vectors.shape[0] // 128
    dma, vmem = pltpu.SemaphoreType.DMA, pl.BlockSpec(memory_space=pltpu.VMEM)
    block = (rows, width)
    shard, sums = pl.pallas_call(
        lambda *refs: scatter_kernel(chips, *refs),
        out_shape=(
            jax.ShapeDtypeStruct(block, jnp.float32),
            jax.ShapeDtypeStruct((lines, 128), jnp.float32),
        ),
        in_specs=[vmem, vmem],
        out_specs=(vmem, vmem),
        scratch_shapes=[pltpu.VMEM((chips, *block), jnp.bfloat16)]
        + [pltpu.VMEM((top, *block), jnp.bfloat16)] * 4
        + [pltpu.VMEM((lines, 128), jnp.float32), pltpu.VMEM((chips, lines, 128), jnp.float32)]
        + [dma((chips,))] * 2
        + [dma((top,))] * 4
        + [dma((1,))] * 2
        + [dma((top,))] * 4,
        compiler_params=pltpu.CompilerParams(collective_id=1, has_side_effects=True),
        name="scatter_rows",
    )(grads.reshape(count, rows, width), vectors.reshape(lines, 128))
    return shard, sums.reshape(-1)


GELU_CUBE = 0.044715
POOL = 48
F32, BF16 = jnp.float32, jnp.bfloat16


def mm(left, right, dims=((1,), (0,))):
    return lax.dot_general(left, right, (dims, ((), ())), preferred_element_type=F32)


class Names:
    def __init__(self, names, refs):
        for name, ref in zip(names, refs):
            setattr(self, name, ref)


STAGED = ("lens", "tok", "cot", "gain", "shift", "b_qv", "b_out", "b_fc1", "b_fc2")
IN_NAMES = [
    "far_tok", "far_cot", "far_lens", "far_gain", "far_shift", "w_qkv", "far_b_qv", "w_out",
    "far_b_out", "w_fc1", "far_b_fc1", "w_fc2", "far_b_fc2",
]
OUT_NAMES = ["far_y", "far_gtok", "far_gqkv", "far_gout", "far_gfc1", "far_gfc2", "far_vec"]


def layer_scratch(chips, rows, row_count, width, heads, hidden, slots):
    count, top = 2 * chips, chips // 2
    dma = pltpu.SemaphoreType.DMA
    tall = (row_count, width)
    low = dict(
        wq=(chips, 2, 3, rows, heads), wo=(chips, 2, rows, heads),
        wf1=(chips, 2, rows, hidden), wf2=(chips, 2, rows, hidden),
        n1=tall, n2=tall, gy=tall, ghb=tall,
        z=(row_count, hidden), zp=(row_count, hidden),
        du=(row_count, hidden), dup=(row_count, hidden),
        qkv=(3, row_count, heads), o=(row_count, heads), op=(row_count, heads),
        dh=(row_count, heads),
        dqkv=(3, row_count, heads), dqkvp=(3, row_count, heads),
        xt=(4, 2, chips, rows, row_count), xtp=(4, chips, rows, row_count),
        grads=(3, chips, rows, hidden), rbuf=(3, 2, top, rows, hidden),
        ysend=(4, *tall), yrecv=(4, *tall), tok=tall, cot=tall,
    )
    full = dict(
        xh1=tall, xh2=tall, h1=tall, gh1=tall, rs1=(row_count, 1), rs2=(row_count, 1),
        u=(row_count, hidden), pf=(heads // HEAD_DIM, row_count, row_count),
        mask=(row_count, row_count), vec=(16, width), vecp=(16, width), vslots=(chips, 8, 128), vres=(16, width), vsum=(16, width),
        gain=(2, width), shift=(2, width), b_qv=(2, heads), b_out=(1, width),
        b_fc1=(1, hidden), b_fc2=(1, width),
        g_qkv=(3, rows, heads), g_out=(rows, heads), g_fc1=(rows, hidden), g_fc2=(rows, hidden),
    )
    sems = dict(
        pool=(POOL,), gr=(8, 2, top), pr=(8,), sr=(12, 2, top), ar=(12,),
        yr=(4,), vr=(2, chips), loc=(8,), ins=(9,), outs=(9,),
    )
    shapes = {k: pltpu.VMEM(s, BF16) for k, s in low.items()}
    shapes |= {k: pltpu.VMEM(s, F32) for k, s in full.items()}
    shapes |= {k: dma(s) for k, s in sems.items()}
    shapes["lens"] = pltpu.SMEM((slots,), jnp.int32)
    return shapes


def layer_kernel(chips, scratch_names, *refs):
    r = Names(IN_NAMES + OUT_NAMES + scratch_names, refs)
    device, chip, core, place = ring_place(chips)
    side_y = lax.axis_index("tensor")
    count, top = 2 * chips, chips // 2
    right = 2 * chip_at(place + 1, chips) + core
    left = 2 * chip_at(place - 1, chips) + core
    partner = 2 * chip + 1 - core
    onward = (right, left)
    row_count, width = r.far_tok.shape
    rows, heads = r.w_out.shape
    hidden = r.w_fc1.shape[1]
    half_hidden = hidden // 2
    slots, issued = [None] * POOL, []

    class remote:
        def __init__(self, source, target, recv_sem, **where):
            self.parts = (source, target, recv_sem, where)

        def build(self, slot):
            source, target, recv_sem, where = self.parts
            return pltpu.make_async_remote_copy(
                src_ref=source, dst_ref=target, send_sem=r.pool.at[slot], recv_sem=recv_sem,
                device_id=where, device_id_type=pl.DeviceIdType.MESH,
            )

        def wait_recv(self):
            self.build(0).wait_recv()

    def go(send):
        slot = len(issued) % POOL
        issued.append(slot)
        if slots[slot] is not None:
            slots[slot].wait_send()
        slots[slot] = send.build(slot)
        slots[slot].start()

    barrier = pltpu.get_barrier_semaphore()

    def greet(**where):
        pl.semaphore_signal(
            barrier, inc=1, device_id=where, device_id_type=pl.DeviceIdType.MESH
        )

    for other in (right, left, partner):
        greet(dp=other)
    greet(tensor=1 - side_y)
    staged = []
    for j, name in enumerate(STAGED):
        copy = pltpu.make_async_copy(getattr(r, "far_" + name), getattr(r, name), r.ins.at[j])
        copy.start()
        staged.append(copy)
    pl.semaphore_wait(barrier, 4)

    base = (0, 0, 0, 0, 0, half_hidden, 0, half_hidden)
    span = (heads,) * 4 + (half_hidden,) * 4

    def cut(i, ref, side=None):
        start, size = base[i], span[i]
        if side is not None:
            size = size // 2
            start = start + side * size
        if start == 0 and size == ref.shape[-1]:
            return ref
        return ref.at[:, pl.ds(start, size)]

    def own(i):
        if i < 3:
            return r.w_qkv.at[i]
        return cut(i, (r.w_out, r.w_fc1, r.w_fc1, r.w_fc2, r.w_fc2)[i - 3])

    def spot_of(i, at_chip, whose, side=None):
        if i < 3:
            return cut(i, r.wq.at[at_chip, whose, i], side)
        return cut(i, (r.wo, r.wf1, r.wf1, r.wf2, r.wf2)[i - 3].at[at_chip, whose], side)

    def all_of(i, whose):
        if i < 3:
            return r.wq.at[:, whose, i]
        if i == 3:
            return r.wo.at[:, whose]
        return (r.wf1, r.wf1, r.wf2, r.wf2)[i - 4].at[:, whose, :, pl.ds(base[i], span[i])]

    def block(i, step, whose, hop, side):
        return spot_of(i, chip_at(place + step, chips), whose, side if hop == top else None)

    def keep(i):
        return pltpu.make_async_copy(own(i), spot_of(i, chip, core), r.loc.at[i])

    def start_item(i):
        mine, there = own(i), spot_of(i, chip, core)
        for side in (0, 1):
            go(remote(mine, there, r.gr.at[i, side, 0], dp=onward[side]))
        go(remote(mine, there, r.pr.at[i], dp=partner))
        keep(i).start()

    def hop_item(i, hop):
        for side, sign in ((0, -1), (1, 1)):
            here = block(i, sign * hop, core, hop, side)
            remote(
                here, here, r.gr.at[i, side, hop - 1], dp=onward[side]
            ).wait_recv()
            if hop < top:
                part = block(i, sign * hop, core, hop + 1, side)
                go(remote(
                    part, part, r.gr.at[i, side, hop], dp=onward[side]
                ))
            go(remote(here, here, r.pr.at[i], dp=partner))

    def finish_item(i):
        keep(i).wait()
        theirs = all_of(i, 1 - core)
        remote(theirs, theirs, r.pr.at[i], dp=partner).wait_recv()

    def swap(k, source, target):
        go(remote(source, target, r.ar.at[k], dp=partner))

    def swapped(k, target):
        remote(target, target, r.ar.at[k], dp=partner).wait_recv()

    quarter = width // 4
    group = chips // 4

    def exchange(k, c):
        at = pl.ds(c * quarter, quarter)
        go(remote(
            r.ysend.at[k, :, at], r.yrecv.at[k, :, at], r.yr.at[k], tensor=1 - side_y
        ))

    def exchanged(k):
        spot = r.yrecv.at[k]
        remote(spot, spot, r.yr.at[k], tensor=1 - side_y).wait_recv()

    scatter_span = hidden // 4
    half = scatter_span // 2

    def scatter_start(i):
        k, col = i // 4, (i % 4) * scatter_span
        far = r.grads.at[k, chip_at(place + top, chips)]
        for side in (0, 1):
            at = pl.ds(col + side * half, half)
            go(remote(
                far.at[:, at], r.rbuf.at[k, side, 0, :, at], r.sr.at[i, side, 0], dp=onward[side],
            ))

    def scatter_step(i, s):
        k, col = i // 4, (i % 4) * scatter_span
        for side, sign in ((0, 1), (1, -1)):
            target = chip_at(place + sign * (top - s), chips)
            at = pl.ds(col + side * half, half) if s == 1 else pl.ds(col, scatter_span)
            spot = r.rbuf.at[k, side, s - 1, :, at]
            remote(
                spot, spot, r.sr.at[i, side, s - 1], dp=onward[side]
            ).wait_recv()
            total = r.grads[k, target, :, at].astype(F32) + spot[...].astype(F32)
            r.grads[k, target, :, at] = total.astype(BF16)
            at = pl.ds(col, scatter_span)
            go(remote(
                r.grads.at[k, target, :, at], r.rbuf.at[k, side, s, :, at],
                r.sr.at[i, side, s], dp=onward[side],
            ))

    def scatter_end(i):
        k, col = i // 4, (i % 4) * scatter_span
        at = pl.ds(col, scatter_span)
        total = r.grads[k, chip, :, at].astype(F32)
        for side in (0, 1):
            spot = r.rbuf.at[k, side, top - 1, :, at]
            remote(
                spot, spot, r.sr.at[i, side, top - 1], dp=onward[side]
            ).wait_recv()
            total = total + spot[...].astype(F32)
        if k == 0:
            r.g_fc2[:, at] = total
        elif k == 1:
            r.g_fc1[:, at] = total
        elif i < 11:
            r.g_qkv[i - 8] = total
            put(r.g_qkv.at[i - 8], r.far_gqkv.at[i - 8])
        else:
            r.g_out[...] = total
            put(r.g_out, r.far_gout)

    order = [(i, s) for s in range(1, top) for i in range(4)]
    order += [(4 + i, s) for s in range(1, top) for i in range(4)]
    order += [(i, s) for s in range(1, top) for i in (11, 8, 9, 10)]
    steps = iter(order)

    def advance(n):
        for _ in range(n):
            scatter_step(*next(steps))

    put_copies = []

    def put(source, target):
        copy = pltpu.make_async_copy(source, target, r.outs.at[len(put_copies)])
        copy.start()
        put_copies.append(copy)

    def grad_tile(k, column, size, terms):
        total = None
        for lhs, rhs in terms:
            part = mm(lhs.reshape(chips * rows, row_count), rhs)
            total = part if total is None else total + part
        r.grads[k, :, :, pl.ds(column, size)] = total.reshape(chips, rows, size).astype(BF16)

    chunk = 32

    def row_loop(fn, carry=()):
        def step(i, c):
            return fn(pl.ds(pl.multiple_of(i * chunk, chunk), chunk), i * chunk, c)
        return lax.fori_loop(0, row_count // chunk, step, carry)

    def fold(value):
        return jnp.sum(value.reshape(chunk // 8, 8, value.shape[1]), axis=0)

    def transposed(k, source):
        per = 2 * rows
        for c in range(chips):
            flipped = source[:, c * per : (c + 1) * per].T
            r.xt[k, 0, c] = flipped[:rows]
            r.xt[k, 1, c] = flipped[rows:]
        swap(k, r.xt.at[k, 1 - core], r.xtp.at[k])

    for i in range(4):
        start_item(i)
    for copy in staged:
        copy.wait()
    ends = []
    for j in range(r.lens.shape[0]):
        ends.append(r.lens[j] if j == 0 else ends[-1] + r.lens[j])
    at_row = lax.broadcasted_iota(jnp.int32, (row_count, row_count), 0)
    at_col = lax.broadcasted_iota(jnp.int32, (row_count, row_count), 1)
    seg_row = sum((at_row >= e).astype(jnp.int32) for e in ends)
    seg_col = sum((at_col >= e).astype(jnp.int32) for e in ends)
    allowed = (seg_row == seg_col) & (at_row >= at_col)
    r.mask[...] = allowed.astype(F32)
    r.vec[...] = jnp.zeros_like(r.vec)

    def is_live(first):
        return first + lax.broadcasted_iota(jnp.int32, (chunk, width), 0) < ends[-1]

    def first_norm(at, first, c):
        x = r.tok[at, :].astype(F32)
        x = x - jnp.mean(x, axis=1, keepdims=True)
        inv = lax.rsqrt(jnp.mean(x * x, axis=1, keepdims=True) + NORM_EPS)
        x = x * inv
        r.xh1[at, :] = x
        r.rs1[at, :] = inv
        r.n1[at, :] = (x * r.gain[0:1, :] + r.shift[0:1, :]).astype(BF16)
        g = jnp.where(is_live(first), r.cot[at, :].astype(F32), 0.0)
        r.gy[at, :] = g.astype(BF16)
        return (c[0] + fold(g),)

    (total,) = row_loop(first_norm, (jnp.zeros((8, width), F32),))
    r.vec[8:9, :] = jnp.sum(total, axis=0, keepdims=True)
    for i in range(4):
        hop_item(i, 1)
    transposed(0, r.n1)
    for i in range(4):
        hop_item(i, 2)
    transposed(1, r.gy)
    for i in range(4):
        hop_item(i, 3)
    start_item(4)
    start_item(5)
    start_item(6)

    for i in range(3):
        hop_item(i, 4)
        finish_item(i)
        part = mm(r.n1[...], r.wq[:, :, i].reshape(width, heads))
        if i != 1:
            part = part + r.b_qv[i // 2 : i // 2 + 1, :]
        r.qkv[i] = part.astype(BF16)
    hop_item(3, 4)
    hop_item(4, 1)
    lane = lax.broadcasted_iota(jnp.int32, (1, 2 * HEAD_DIM), 1)
    picks = [(lane // HEAD_DIM == j).astype(F32).astype(BF16) for j in (0, 1)]
    first_half = lax.broadcasted_iota(jnp.int32, (row_count, 2 * HEAD_DIM), 1) < HEAD_DIM
    pairs = heads // (2 * HEAD_DIM)
    scale = HEAD_DIM ** (-0.5)
    between = [(5, 1), (6, 1), (4, 2), (5, 2)]
    for p in range(pairs):
        at = pl.ds(p * 2 * HEAD_DIM, 2 * HEAD_DIM)
        q, k, v = r.qkv[0, :, at], r.qkv[1, :, at], r.qkv[2, :, at]
        mixed = []
        for j in (0, 1):
            s = mm(q * picks[j], k, ((1,), (1,))) * scale
            s = jnp.where(r.mask[...] > 0.5, s, -1e30)
            e = jnp.exp(s - jnp.max(s, axis=1, keepdims=True))
            e = e / jnp.sum(e, axis=1, keepdims=True)
            r.pf[2 * p + j] = e
            mixed.append(mm(e.astype(BF16), v))
        r.o[:, at] = jnp.where(first_half, mixed[0], mixed[1]).astype(BF16)
        hop_item(*between[p])
    start_item(7)
    finish_item(3)
    for c in range(4):
        w = r.wo[c * group : (c + 1) * group].reshape(quarter, heads)
        r.ysend[0, :, pl.ds(c * quarter, quarter)] = mm(r.o[...], w, ((1,), (1,))).astype(BF16)
        exchange(0, c)
    swap(8, r.o, r.op)
    hop_item(4, 3)
    hop_item(5, 3)
    hop_item(6, 2)
    hop_item(7, 1)
    exchanged(0)

    def second_norm(at, first, c):
        x = r.tok[at, :].astype(F32)
        x = x + (r.ysend[0, at, :].astype(F32) + r.yrecv[0, at, :].astype(F32)) + r.b_out[...]
        r.h1[at, :] = x
        x = x - jnp.mean(x, axis=1, keepdims=True)
        inv = lax.rsqrt(jnp.mean(x * x, axis=1, keepdims=True) + NORM_EPS)
        x = x * inv
        r.xh2[at, :] = x
        r.rs2[at, :] = inv
        r.n2[at, :] = (x * r.gain[1:2, :] + r.shift[1:2, :]).astype(BF16)
        return c

    row_loop(second_norm)
    transposed(2, r.n2)
    hop_item(4, 4)
    hop_item(5, 4)
    finish_item(4)
    finish_item(5)

    tile = hidden // 4
    later = [(), (6, 3), (7, 2), (6, 4)]
    for t in range(4):
        at = pl.ds(t * tile, tile)
        r.u[:, at] = mm(r.n2[...], r.wf1[:, :, :, at].reshape(width, tile)) + r.b_fc1[:, at]

        def gelu(rows_at, first, c):
            u = r.u[rows_at, at]
            t_ = jnp.tanh(GELU_COEF * (u + GELU_CUBE * u * u * u))
            r.z[rows_at, at] = (0.5 * u * (1.0 + t_)).astype(BF16)
            r.u[rows_at, at] = 0.5 * (1.0 + t_) + 0.5 * u * (1.0 - t_ * t_) * GELU_COEF * (
                1.0 + 3.0 * GELU_CUBE * u * u
            )
            return c

        row_loop(gelu)
        if t % 2 == 1:
            cols = pl.ds((t // 2) * half_hidden, half_hidden)
            swap(4 + t // 2, r.z.at[:, cols], r.zp.at[:, cols])
        if later[t]:
            hop_item(*later[t])
    swapped(1, r.xtp.at[1])
    for h in (0, 1):
        cols = pl.ds(h * half_hidden, half_hidden)
        swapped(4 + h, r.zp.at[:, cols])
        for t in (2 * h, 2 * h + 1):
            at = pl.ds(t * tile, tile)
            grad_tile(0, t * tile, tile, ((r.xt[1, core], r.z[:, at]), (r.xtp[1], r.zp[:, at])))
            scatter_start(t)
        hop_item(7, 3 + h)
    finish_item(6)
    finish_item(7)
    for t in range(4):
        at = pl.ds(t * tile, tile)
        d = mm(r.gy[...], r.wf2[:, :, :, at].reshape(width, tile)) * r.u[:, at]
        d = d.astype(BF16)
        r.du[:, at] = d
        row, col = (t * tile) // width, (t * tile) % width
        r.vec[6 + row : 7 + row, col : col + tile] = jnp.sum(
            d.astype(F32), axis=0, keepdims=True
        )
        if t % 2 == 1:
            cols = pl.ds((t // 2) * half_hidden, half_hidden)
            swap(6 + t // 2, r.du.at[:, cols], r.dup.at[:, cols])
        advance(1)
    for c in range(4):
        w = r.wf1[c * group : (c + 1) * group].reshape(quarter, hidden)
        r.ysend[1, :, pl.ds(c * quarter, quarter)] = mm(r.du[...], w, ((1,), (1,))).astype(BF16)
        exchange(1, c)
        advance(1)
    swapped(2, r.xtp.at[2])
    for h in (0, 1):
        cols = pl.ds(h * half_hidden, half_hidden)
        swapped(6 + h, r.dup.at[:, cols])
        for t in (2 * h, 2 * h + 1):
            at = pl.ds(t * tile, tile)
            grad_tile(1, t * tile, tile, ((r.xt[2, core], r.du[:, at]), (r.xtp[2], r.dup[:, at])))
            scatter_start(4 + t)
            advance(1)
    for j in range(1, chips):
        greet(dp=2 * lax.rem(chip + j, chips) + core)
    for c in range(4):
        w = r.wf2[c * group : (c + 1) * group].reshape(quarter, hidden)
        r.ysend[2, :, pl.ds(c * quarter, quarter)] = mm(r.z[...], w, ((1,), (1,))).astype(BF16)
        exchange(2, c)
    advance(2)
    exchanged(1)

    def norm_back(k, gain_row, xh, rs, above, store):
        def step(at, first, c):
            dn = r.ysend[k, at, :].astype(F32) + r.yrecv[k, at, :].astype(F32)
            x = xh[at, :]
            scaled = dn * r.gain[gain_row : gain_row + 1, :]
            m1 = jnp.mean(scaled, axis=1, keepdims=True)
            m2 = jnp.mean(scaled * x, axis=1, keepdims=True)
            g = above[at, :].astype(F32) + rs[at, :] * (scaled - m1 - x * m2)
            store(at, g)
            return (c[0] + fold(dn * x), c[1] + fold(dn), c[2] + fold(g))

        zero = jnp.zeros((8, width), F32)
        return [jnp.sum(s, axis=0, keepdims=True) for s in row_loop(step, (zero, zero, zero))]

    def store_gh1(at, g):
        r.gh1[at, :] = g
        r.ghb[at, :] = g.astype(BF16)

    sums = norm_back(1, 1, r.xh2, r.rs2, r.gy, store_gh1)
    r.vec[1:2, :] = sums[0]
    r.vec[3:4, :] = sums[1]
    r.vec[5:6, :] = sums[2]
    transposed(3, r.ghb)
    advance(1)

    r.dh[...] = mm(r.ghb[...], r.wo[...].reshape(width, heads)).astype(BF16)
    for p in range(pairs):
        at = pl.ds(p * 2 * HEAD_DIM, 2 * HEAD_DIM)
        q, k, v = r.qkv[0, :, at], r.qkv[1, :, at], r.qkv[2, :, at]
        d_out, o = r.dh[:, at], r.o[:, at]
        parts = []
        for j in (0, 1):
            mine = d_out * picks[j]
            delta = jnp.sum(mine.astype(F32) * o.astype(F32), axis=1, keepdims=True)
            prob = r.pf[2 * p + j]
            ds = (prob * (mm(mine, v, ((1,), (1,))) - delta) * scale).astype(BF16)
            parts.append((
                mm(ds, k),
                mm(ds, q, ((0,), (0,))),
                mm(prob.astype(BF16), d_out, ((0,), (0,))),
            ))
        for i in range(3):
            r.dqkv[i, :, at] = jnp.where(first_half, parts[0][i], parts[1][i]).astype(BF16)
        advance((1, 1, 2, 1)[p])
    swap(9, r.dqkv, r.dqkvp)
    swapped(3, r.xtp.at[3])
    swapped(8, r.op)
    grad_tile(2, 3 * heads, heads, ((r.xt[3, core], r.o[...]), (r.xtp[3], r.op[...])))
    scatter_start(11)
    for c in range(4):
        total = None
        for i in range(3):
            w = r.wq[c * group : (c + 1) * group, :, i].reshape(quarter, heads)
            part = mm(r.dqkv[i], w, ((1,), (1,)))
            total = part if total is None else total + part
        r.ysend[3, :, pl.ds(c * quarter, quarter)] = total.astype(BF16)
        exchange(3, c)
        if c % 2 == 1:
            advance(1)
    for i in (0, 2):
        r.vec[4:5, pl.ds((i // 2) * heads, heads)] = jnp.sum(
            r.dqkv[i].astype(F32), axis=0, keepdims=True
        )
    swapped(0, r.xtp.at[0])
    swapped(9, r.dqkvp)
    for i in range(3):
        grad_tile(
            2, i * heads, heads, ((r.xt[0, core], r.dqkv[i]), (r.xtp[0], r.dqkvp[i]))
        )
        scatter_start(8 + i)
    advance(1)
    for i in range(4):
        scatter_end(i)
    put(r.g_fc2, r.far_gfc2)
    advance(1)
    exchanged(2)

    def finish_output(at, first, c):
        y = r.h1[at, :] + (r.ysend[2, at, :].astype(F32) + r.yrecv[2, at, :].astype(F32))
        y = jnp.where(is_live(first), y + r.b_fc2[...], 0.0)
        r.n2[at, :] = y.astype(BF16)
        return c

    row_loop(finish_output)
    put(r.n2, r.far_y)
    advance(4)
    exchanged(3)

    def store_tokens(at, g):
        r.gh1[at, :] = g

    sums = norm_back(3, 0, r.xh1, r.rs1, r.gh1, store_tokens)
    r.vec[0:1, :] = sums[0]
    r.vec[2:3, :] = sums[1]
    put(r.gh1, r.far_gtok)

    swap(10, r.vec, r.vecp)
    top_row = pl.multiple_of(8 * core, 8)

    def tile_of(ref, which):
        return ref.at[pl.ds(top_row, 8), pl.ds(pl.multiple_of(128 * which, 128), 128)]

    def tile_copy(stage, j, source, target):
        other = lax.rem(chip + j, chips)
        return remote(
            source, target, r.vr.at[stage, j], dp=2 * other + core
        )

    advance(1)
    swapped(10, r.vecp)
    r.vres[...] = r.vec[...] + r.vecp[...]
    pl.semaphore_wait(barrier, chips - 1)
    for j in range(1, chips):
        go(tile_copy(0, j, tile_of(r.vres, lax.rem(chip + j, chips)), r.vslots.at[chip]))
    r.vslots[chip] = tile_of(r.vres, chip)[...]
    advance(3)
    for i in range(4, 8):
        scatter_end(i)
    put(r.g_fc1, r.far_gfc1)
    for j in range(1, chips):
        spot = r.vslots.at[lax.rem(chip + chips - j, chips)]
        tile_copy(0, j, spot, spot).wait_recv()
    mine = tile_of(r.vsum, chip)
    mine[...] = jnp.sum(r.vslots[...], axis=0)
    for j in range(1, chips):
        go(tile_copy(1, j, mine, mine))
    advance(4)
    assert next(steps, None) is None
    for j in range(1, chips):
        spot = tile_of(r.vsum, lax.rem(chip + chips - j, chips))
        tile_copy(1, j, spot, spot).wait_recv()
    rows_here = r.vsum.at[pl.ds(top_row, 8), :]
    swap(11, rows_here, rows_here)
    swapped(11, r.vsum.at[pl.ds(pl.multiple_of(8 * (1 - core), 8), 8), :])
    put(r.vsum, r.far_vec)
    for i in (11, 8, 9, 10):
        scatter_end(i)
    for copy in put_copies:
        copy.wait()
    for copy in slots:
        copy.wait_send()


def one_kernel(tokens, cotangent, seq_lens, gain, shift, w_qkv, b_qv, w_out, b_out, w_fc1, b_fc1, w_fc2, b_fc2):
    chips = lax.axis_size("dp") // 2
    row_count, width = tokens.shape
    rows, heads = w_out.shape
    hidden = w_fc1.shape[1]
    vmem, hbm = pl.BlockSpec(memory_space=pltpu.VMEM), pl.BlockSpec(memory_space=pl.ANY)
    scratch = layer_scratch(chips, rows, row_count, width, heads, hidden, seq_lens.shape[0])
    names = list(scratch)

    def made(*shape, kind=F32):
        return jax.ShapeDtypeStruct(shape, kind)

    outs = pl.pallas_call(
        lambda *refs: layer_kernel(chips, names, *refs),
        out_shape=(
            made(row_count, width, kind=BF16), made(row_count, width), made(3, rows, heads),
            made(rows, heads), made(rows, hidden), made(rows, hidden), made(16, width),
        ),
        in_specs=[hbm] * 13,
        out_specs=(hbm,) * 7,
        scratch_shapes=list(scratch.values()),
        compiler_params=pltpu.CompilerParams(
            collective_id=2, has_side_effects=True, vmem_limit_bytes=63 * 2**20
        ),
        name="layer",
    )(
        tokens, cotangent, seq_lens, gain, shift, w_qkv, b_qv, w_out, b_out[None], w_fc1,
        b_fc1[None], w_fc2, b_fc2[None],
    )
    small = ((2, width), (2, width), (2, heads), (1, width), (1, hidden), (1, width))
    outs = pl.pallas_call(
        lambda *refs: results_kernel(heads, *refs),
        out_shape=tuple(made(*o.shape, kind=o.dtype) for o in outs[:6])
        + tuple(made(*o) for o in small),
        in_specs=[vmem] * 7,
        out_specs=(hbm,) * 6 + (vmem,) * 6,
        scratch_shapes=[pltpu.SemaphoreType.DMA((6,))],
        name="results",
    )(*outs)
    y, g_tok, g_qkv, g_out, g_fc1, g_fc2, g_gain, g_shift, g_bqv, g_bout, g_bfc1, g_bfc2 = outs
    return (
        y, g_tok, g_gain, g_shift, g_qkv, g_bqv, g_out, g_bout.reshape(-1), g_fc1,
        g_bfc1.reshape(-1), g_fc2, g_bfc2.reshape(-1),
    )


def results_kernel(heads, *refs):
    sources, vec, targets, sem = refs[:6], refs[6], refs[7:13], refs[19]
    gain, shift, bqv, bout, bfc1, bfc2 = refs[13:19]
    copies = [
        pltpu.make_async_copy(source, target, sem.at[i])
        for i, (source, target) in enumerate(zip(sources, targets))
    ]
    for copy in copies:
        copy.start()
    width = vec.shape[1]
    gain[...] = vec[0:2, :]
    shift[...] = vec[2:4, :]
    bqv[0:1, :] = vec[4:5, :heads]
    bqv[1:2, :] = vec[4:5, heads : 2 * heads]
    bout[...] = vec[5:6, :]
    for j in range(bfc1.shape[1] // width):
        bfc1[:, j * width : (j + 1) * width] = vec[6 + j : 7 + j, :]
    bfc2[...] = vec[8:9, :]
    for copy in copies:
        copy.wait()


def fits_one_kernel(tokens, w_out, w_fc1):
    chips = lax.axis_size("dp") // 2
    rows, heads = w_out.shape
    width, hidden = tokens.shape[1], w_fc1.shape[1]
    return (
        lax.axis_size("tensor") == 2
        and chips == 2 * 4
        and width == 128 * chips
        and rows % 16 == 0
        and tokens.shape[0] % 32 == 0
        and 2 * heads == width
        and 4 * heads == hidden
    )


def body(
    tokens,
    cotangent,
    seq_lens,
    layer_norm_gain,
    layer_norm_bias,
    w_qkv,
    b_qv,
    w_out,
    b_out,
    w_fc1,
    b_fc1,
    w_fc2,
    b_fc2,
):
    if fits_one_kernel(tokens, w_out, w_fc1):
        return one_kernel(
            tokens, cotangent, seq_lens, layer_norm_gain, layer_norm_bias, w_qkv, b_qv, w_out,
            b_out, w_fc1, b_fc1, w_fc2, b_fc2,
        )
    heads_width, hidden_width = w_out.shape[1], w_fc1.shape[1]
    attn_shards = jnp.concatenate([w_qkv[0], w_qkv[1], w_qkv[2], w_out], axis=1)
    mlp_shards = jnp.concatenate([w_fc1, w_fc2], axis=1)
    mlp_full = lax.all_gather(mlp_shards, "dp", axis=0, tiled=True)
    attn_full = gather_rows(attn_shards)
    qkv_full, out_full = attn_full[:, : 3 * heads_width], attn_full[:, 3 * heads_width :]
    fc1_full, fc2_full = mlp_full[:, :hidden_width], mlp_full[:, hidden_width:]
    allowed, live_rows = seq_masks(seq_lens, tokens.shape[0])
    input_tokens = tokens.astype(jnp.float32)
    first_normalized, first_centered_scaled, first_inverse_deviation = layer_norm_forward(
        input_tokens, layer_norm_gain[0], layer_norm_bias[0]
    )
    low1 = first_normalized.astype(jnp.bfloat16)
    proj = product("td,dc->tc", low1, qkv_full)
    query = (proj[:, :heads_width] + b_qv[0]).astype(jnp.bfloat16)
    key_rows = proj[:, heads_width : 2 * heads_width].astype(jnp.bfloat16)
    value = (proj[:, 2 * heads_width :] + b_qv[1]).astype(jnp.bfloat16)
    heads_out, logsum = attend(query, key_rows, value, allowed)
    attn_part = product("tc,dc->td", heads_out, out_full)
    attn_mix = sum_tensor(attn_part)
    first_hidden_state = input_tokens + attn_mix + b_out
    second_normalized, second_centered_scaled, second_inverse_deviation = layer_norm_forward(
        first_hidden_state, layer_norm_gain[1], layer_norm_bias[1]
    )
    low2 = second_normalized.astype(jnp.bfloat16)
    pre_act = jnp.dot(low2, fc1_full, preferred_element_type=jnp.float32) + b_fc1
    act, slope = gelu_parts(pre_act)
    act_low = act.astype(jnp.bfloat16)
    mlp_part = product("tf,df->td", act_low, fc2_full)
    mlp_mix = sum_tensor(mlp_part)
    result = first_hidden_state + mlp_mix + b_fc2
    output = jnp.where(live_rows[:, None], result, 0.0).astype(jnp.bfloat16)
    qkv_back, out_back, fc1_back, fc2_back = (qkv_full, out_full, fc1_full, fc2_full)
    grad_y = jnp.where(live_rows[:, None], cotangent, jnp.zeros_like(cotangent))
    flat_output_gradient = grad_y.astype(jnp.float32)
    d_pre = (jnp.dot(grad_y, fc2_back, preferred_element_type=jnp.float32) * slope).astype(
        jnp.bfloat16
    )
    g_fc2 = product("td,tf->df", grad_y, act_low)
    g_bfc2 = jnp.sum(flat_output_gradient, axis=0)
    g_fc1 = product("td,tf->df", low2, d_pre)
    g_mlp = jnp.concatenate([g_fc1.astype(jnp.bfloat16), g_fc2.astype(jnp.bfloat16)], axis=1)
    shard_mlp = lax.psum_scatter(g_mlp, "dp", scatter_dimension=0, tiled=True)
    g_bfc1 = jnp.sum(d_pre.astype(jnp.float32), axis=0)
    d_norm2_part = product("tf,df->td", d_pre, fc1_back)
    second_norm_delta = sum_tensor(d_norm2_part)
    second_gain_gradient = jnp.sum(second_norm_delta * second_centered_scaled, axis=0)
    g_shift2 = jnp.sum(second_norm_delta, axis=0)
    hidden_first_gradient = flat_output_gradient + layer_norm_backward(
        second_norm_delta, layer_norm_gain[1], second_centered_scaled, second_inverse_deviation
    )
    grad_low = hidden_first_gradient.astype(jnp.bfloat16)
    g_out = product("td,tc->dc", grad_low, heads_out)
    g_bout = jnp.sum(hidden_first_gradient, axis=0)
    d_heads = jnp.dot(grad_low, out_back, preferred_element_type=jnp.float32).astype(jnp.bfloat16)
    d_query, d_key, d_value = attend_back(
        query, key_rows, value, heads_out, d_heads, logsum, allowed
    )
    stacked = jnp.concatenate([d_query, d_key, d_value], axis=1)
    g_qkv = product("td,tc->dc", low1, stacked)
    g_attn = jnp.concatenate([g_qkv.astype(jnp.bfloat16), g_out.astype(jnp.bfloat16)], axis=1)
    g_bqv = jnp.stack(
        [jnp.sum(d_query.astype(jnp.float32), axis=0), jnp.sum(d_value.astype(jnp.float32), axis=0)]
    )
    d_norm1_part = product("tc,dc->td", stacked, qkv_back)
    first_norm_delta = sum_tensor(d_norm1_part)
    first_gain_gradient = jnp.sum(first_norm_delta * first_centered_scaled, axis=0)
    g_shift1 = jnp.sum(first_norm_delta, axis=0)
    input_gradient = hidden_first_gradient + layer_norm_backward(
        first_norm_delta, layer_norm_gain[0], first_centered_scaled, first_inverse_deviation
    )
    shard_mlp = shard_mlp.astype(jnp.float32)
    shard_fc1, shard_fc2 = shard_mlp[:, :hidden_width], shard_mlp[:, hidden_width:]
    vectors = jnp.concatenate(
        [
            first_gain_gradient,
            second_gain_gradient,
            g_shift1,
            g_shift2,
            g_bqv.reshape(-1),
            g_bout,
            g_bfc1,
            g_bfc2,
        ]
    )
    shard_attn, vectors = scatter_rows(g_attn, vectors)
    shard_qkv = jnp.stack([shard_attn[:, i * heads_width : (i + 1) * heads_width] for i in range(3)])
    shard_out = shard_attn[:, 3 * heads_width :]
    width = tokens.shape[1]
    cuts = [2 * width, 4 * width, 4 * width + 2 * heads_width]
    cuts += [cuts[-1] + width, cuts[-1] + width + hidden_width]
    gain_sum, shift_sum, bqv_sum, bout_sum, bfc1_sum, bfc2_sum = jnp.split(vectors, cuts)
    gain_sum, shift_sum = gain_sum.reshape(2, width), shift_sum.reshape(2, width)
    bqv_sum = bqv_sum.reshape(2, heads_width)
    return (
        output,
        input_gradient,
        gain_sum,
        shift_sum,
        shard_qkv,
        bqv_sum,
        shard_out,
        bout_sum,
        shard_fc1,
        bfc1_sum,
        shard_fc2,
        bfc2_sum,
    )


def solution(mesh):
    in_specs = (
        P("dp", None),
        P("dp", None),
        P("dp"),
        P(),
        P(),
        P(None, "dp", "tensor"),
        P(None, "tensor"),
        P("dp", "tensor"),
        P(),
        P("dp", "tensor"),
        P("tensor"),
        P("dp", "tensor"),
        P(),
    )
    out_specs = (
        P("dp", None),
        P("dp", None),
        P(),
        P(),
        P(None, "dp", "tensor"),
        P(None, "tensor"),
        P("dp", "tensor"),
        P(),
        P("dp", "tensor"),
        P("tensor"),
        P("dp", "tensor"),
        P(),
    )
    return jax.shard_map(body, mesh=mesh, in_specs=in_specs, out_specs=out_specs, check_vma=False)
```

```python
import jax
import jax.numpy as jnp
from jax import lax
from jax.experimental import pallas as pl
from jax.experimental.pallas import tpu as pltpu
from jax.sharding import PartitionSpec as P

HEAD_DIM = 64


NORM_EPS = 1e-05
GELU_COEF = 0.7978845608028654


def product(spec, left, right):
    return jnp.einsum(spec, left, right, preferred_element_type=jnp.float32)


def seq_masks(lengths, row_count):
    slots = jnp.arange(lengths.shape[0])
    ends = jnp.sum(jnp.where(slots[:, None] <= slots[None, :], lengths[:, None], 0), axis=0)
    places = jnp.arange(row_count, dtype=jnp.int32)
    segment = jnp.sum((places[:, None] >= ends[None, :]).astype(jnp.int32), axis=1)
    allowed = (segment[:, None] == segment[None, :]) & (places[:, None] >= places[None, :])
    live_rows = places < ends[-1]
    return (allowed, live_rows)


def layer_norm_forward(hidden, gain, shift):
    center = hidden - jnp.mean(hidden, axis=-1, keepdims=True)
    inv_std = lax.rsqrt(jnp.mean(center * center, axis=-1, keepdims=True) + NORM_EPS)
    normal_x = center * inv_std
    return (normal_x * gain + shift, normal_x, inv_std)


def layer_norm_backward(grad_out, gain, normal_x, inv_std):
    scaled = grad_out * gain
    return inv_std * (
        scaled
        - jnp.mean(scaled, axis=-1, keepdims=True)
        - normal_x * jnp.mean(scaled * normal_x, axis=-1, keepdims=True)
    )


def gelu_parts(pre_act):
    inner = GELU_COEF * (pre_act + 0.044715 * pre_act * pre_act * pre_act)
    tanh_val = jnp.tanh(inner)
    value = 0.5 * pre_act * (1.0 + tanh_val)
    slope = 0.5 * (1.0 + tanh_val) + 0.5 * pre_act * (1.0 - tanh_val * tanh_val) * GELU_COEF * (
        1.0 + 3.0 * 0.044715 * pre_act * pre_act
    )
    return (value, slope)


def split_heads(matrix):
    return matrix.reshape(matrix.shape[0], matrix.shape[1] // HEAD_DIM, HEAD_DIM)


def head_scores(query, key_rows, allowed):
    scores = product("qhd,khd->hqk", split_heads(query), split_heads(key_rows)) * HEAD_DIM ** (-0.5)
    return jnp.where(allowed[None], scores, -1e30)


def attend(query, key_rows, value, allowed):
    scores = head_scores(query, key_rows, allowed)
    row_max = jnp.max(scores, axis=-1, keepdims=True)
    logsum = row_max + jnp.log(jnp.sum(jnp.exp(scores - row_max), axis=-1, keepdims=True))
    weights = jnp.exp(scores - logsum).astype(jnp.bfloat16)
    mixed = product("hqk,khd->qhd", weights, split_heads(value)).astype(jnp.bfloat16)
    return (mixed.reshape(query.shape[0], -1), logsum)


def attend_back(query, key_rows, value, heads_out, d_heads, logsum, allowed):
    scores = head_scores(query, key_rows, allowed)
    probs = jnp.exp(scores - logsum)
    probs_low = probs.astype(jnp.bfloat16)
    d_split = split_heads(d_heads)
    d_prob = product("qhd,khd->hqk", d_split, split_heads(value))
    delta = jnp.sum(
        d_split.astype(jnp.float32) * split_heads(heads_out).astype(jnp.float32), axis=-1
    )
    d_score = (probs * (d_prob - jnp.transpose(delta)[:, :, None]) * HEAD_DIM ** (-0.5)).astype(
        jnp.bfloat16
    )
    d_query = product("hqk,khd->qhd", d_score, split_heads(key_rows)).astype(jnp.bfloat16)
    d_key = product("hqk,qhd->khd", d_score, split_heads(query)).astype(jnp.bfloat16)
    d_value = product("hqk,qhd->khd", probs_low, d_split).astype(jnp.bfloat16)
    row_count = query.shape[0]
    return (
        d_query.reshape(row_count, -1),
        d_key.reshape(row_count, -1),
        d_value.reshape(row_count, -1),
    )


def sum_tensor(part):
    low = lax.optimization_barrier(part.astype(jnp.bfloat16))
    count = lax.axis_size("tensor")
    if count != 2:
        return lax.psum(low, "tensor").astype(jnp.float32)
    other = lax.ppermute(low, "tensor", [(0, 1), (1, 0)])
    return low.astype(jnp.float32) + other.astype(jnp.float32)


def chip_at(place, chips):
    place = (place + chips) % chips
    back = place // (chips // 2)
    return 2 * (place * (1 - back) + (chips - 1 - place) * back) + back


def ring_place(chips):
    device = lax.axis_index("dp")
    core, chip = device % 2, device // 2
    column, row = chip % 2, chip // 2
    place = row * (1 - column) + (chips - 1 - row) * column
    return device, chip, core, place


def send(source, target, send_sem, recv_sem, device):
    return pltpu.make_async_remote_copy(
        src_ref=source,
        dst_ref=target,
        send_sem=send_sem,
        recv_sem=recv_sem,
        device_id={"dp": device},
        device_id_type=pl.DeviceIdType.MESH,
    )


def meet(devices):
    barrier = pltpu.get_barrier_semaphore()
    for device in devices:
        pl.semaphore_signal(
            barrier, inc=1, device_id={"dp": device}, device_id_type=pl.DeviceIdType.MESH
        )
    pl.semaphore_wait(barrier, len(devices))


def gather_kernel(chips, own, out, rs, rr, ls, lr, ps, pr, own_sem):
    device, chip, core, place = ring_place(chips)
    right = 2 * chip_at(place + 1, chips) + core
    left = 2 * chip_at(place - 1, chips) + core
    partner = 2 * chip + 1 - core
    meet((right, left, partner))
    top, width = chips // 2, own.shape[1]
    half = width // 2

    def block(step, whose, hop, side):
        at = out.at[2 * chip_at(place + step, chips) + whose]
        if hop < top:
            return at
        return at.at[:, pl.ds(side * half, half)]

    started = []

    def go(copy):
        copy.start()
        started.append(copy)

    go(send(own, out.at[device], rs.at[0], rr.at[0], right))
    go(send(own, out.at[device], ls.at[0], lr.at[0], left))
    go(send(own, out.at[device], ps.at[0], pr.at[0], partner))
    keep = pltpu.make_async_copy(own, out.at[device], own_sem)
    keep.start()
    passed = [block(0, 1 - core, 0, 0)]
    for hop in range(1, top + 1):
        for side, sign, s_sem, r_sem, onward in ((0, -1, rs, rr, right), (1, 1, ls, lr, left)):
            here = block(sign * hop, core, hop, side)
            send(here, here, s_sem.at[hop - 1], r_sem.at[hop - 1], onward).wait_recv()
            if hop < top:
                part = block(sign * hop, core, hop + 1, side)
                go(send(part, part, s_sem.at[hop], r_sem.at[hop], onward))
            slot = len(passed)
            go(send(here, here, ps.at[slot], pr.at[slot], partner))
            passed.append(block(sign * hop, 1 - core, hop, side))
    for slot, here in enumerate(passed):
        send(here, here, ps.at[slot], pr.at[slot], partner).wait_recv()
    for copy in started:
        copy.wait_send()
    keep.wait()


def gather_rows(shard):
    count = lax.axis_size("dp")
    chips = count // 2
    top = chips // 2
    dma = pltpu.SemaphoreType.DMA
    out = pl.pallas_call(
        lambda *refs: gather_kernel(chips, *refs),
        out_shape=jax.ShapeDtypeStruct((count, *shard.shape), shard.dtype),
        in_specs=[pl.BlockSpec(memory_space=pltpu.VMEM)],
        out_specs=pl.BlockSpec(memory_space=pl.ANY),
        scratch_shapes=[dma((top,))] * 4 + [dma((chips + 1,))] * 2 + [dma],
        compiler_params=pltpu.CompilerParams(collective_id=0, has_side_effects=True),
        name="gather_rows",
    )(shard)
    return out.reshape(count * shard.shape[0], shard.shape[1])


def scatter_kernel(
    chips, grads, vec, out, vec_out,
    pbuf, rbuf, lbuf, rstage, lstage, vpart, vslots,
    ps, pr, rs, rr, ls, lr, vps, vpr, vrs, vrr, vls, vlr,
):
    device, chip, core, place = ring_place(chips)
    right = 2 * chip_at(place + 1, chips) + core
    left = 2 * chip_at(place - 1, chips) + core
    partner = 2 * chip + 1 - core
    meet((right, left, partner))
    top, width = chips // 2, out.shape[1]
    half = width // 2
    low, high = pl.ds(0, half), pl.ds(half, half)
    started = []

    def go(copy):
        copy.start()
        started.append(copy)

    order = [top]
    for step in range(1, top):
        order += [top - step, step - top]
    order.append(0)
    go(send(vec, vpart, vps.at[0], vpr.at[0], partner))
    for slot, step in enumerate(order):
        mine = grads.at[2 * chip_at(place + step, chips) + 1 - core]
        go(send(mine, pbuf.at[slot], ps.at[slot], pr.at[slot], partner))

    def pair_sum(slot):
        spot = pbuf.at[slot]
        send(spot, spot, ps.at[slot], pr.at[slot], partner).wait_recv()
        mine = grads[2 * chip_at(place + order[slot], chips) + core]
        return mine.astype(jnp.float32) + pbuf[slot].astype(jnp.float32)

    def arrived(spot, s_sem, r_sem):
        send(spot, spot, s_sem, r_sem, partner).wait_recv()

    first = pair_sum(0).astype(jnp.bfloat16)
    rstage[0, :, :half] = first[:, :half]
    go(send(rstage.at[0, :, low], rbuf.at[0, :, low], rs.at[0], rr.at[0], right))
    lstage[0, :, half:] = first[:, half:]
    go(send(lstage.at[0, :, high], lbuf.at[0, :, high], ls.at[0], lr.at[0], left))
    arrived(vpart, vps.at[0], vpr.at[0])
    vslots[chip] = vec[...] + vpart[...]
    go(send(vslots.at[chip], vslots.at[chip], vrs.at[0], vrr.at[0], right))
    go(send(vslots.at[chip], vslots.at[chip], vls.at[0], vlr.at[0], left))
    for step in range(1, top):
        for side, buf, stage, s_sem, r_sem, onward in (
            (0, rbuf, rstage, rs, rr, right),
            (1, lbuf, lstage, ls, lr, left),
        ):
            total = pair_sum(2 * step - 1 + side)
            if step == 1:
                cols = (low, high)[side]
                arrived(buf.at[0, :, cols], s_sem.at[0], r_sem.at[0])
                more = buf[0, :, side * half : (side + 1) * half].astype(jnp.float32)
                if side == 0:
                    stage[step, :, :half] = (total[:, :half] + more).astype(jnp.bfloat16)
                    stage[step, :, half:] = total[:, half:].astype(jnp.bfloat16)
                else:
                    stage[step, :, :half] = total[:, :half].astype(jnp.bfloat16)
                    stage[step, :, half:] = (total[:, half:] + more).astype(jnp.bfloat16)
            else:
                arrived(buf.at[step - 1], s_sem.at[step - 1], r_sem.at[step - 1])
                stage[step] = (total + buf[step - 1].astype(jnp.float32)).astype(jnp.bfloat16)
            go(send(stage.at[step], buf.at[step], s_sem.at[step], r_sem.at[step], onward))
        spot = vslots.at[chip_at(place - step, chips)]
        arrived(spot, vrs.at[step - 1], vrr.at[step - 1])
        go(send(spot, spot, vrs.at[step], vrr.at[step], right))
        spot = vslots.at[chip_at(place + step, chips)]
        arrived(spot, vls.at[step - 1], vlr.at[step - 1])
        if step < top - 1:
            go(send(spot, spot, vls.at[step], vlr.at[step], left))
    spot = vslots.at[chip_at(place - top, chips)]
    arrived(spot, vrs.at[top - 1], vrr.at[top - 1])
    vec_out[...] = jnp.sum(vslots[...], axis=0)
    total = pair_sum(len(order) - 1)
    arrived(rbuf.at[top - 1], rs.at[top - 1], rr.at[top - 1])
    arrived(lbuf.at[top - 1], ls.at[top - 1], lr.at[top - 1])
    out[...] = total + rbuf[top - 1].astype(jnp.float32) + lbuf[top - 1].astype(jnp.float32)
    for copy in started:
        copy.wait_send()


def scatter_rows(grads, vectors):
    count = lax.axis_size("dp")
    chips = count // 2
    top = chips // 2
    rows, width = grads.shape[0] // count, grads.shape[1]
    lines = vectors.shape[0] // 128
    dma, vmem = pltpu.SemaphoreType.DMA, pl.BlockSpec(memory_space=pltpu.VMEM)
    block = (rows, width)
    shard, sums = pl.pallas_call(
        lambda *refs: scatter_kernel(chips, *refs),
        out_shape=(
            jax.ShapeDtypeStruct(block, jnp.float32),
            jax.ShapeDtypeStruct((lines, 128), jnp.float32),
        ),
        in_specs=[vmem, vmem],
        out_specs=(vmem, vmem),
        scratch_shapes=[pltpu.VMEM((chips, *block), jnp.bfloat16)]
        + [pltpu.VMEM((top, *block), jnp.bfloat16)] * 4
        + [pltpu.VMEM((lines, 128), jnp.float32), pltpu.VMEM((chips, lines, 128), jnp.float32)]
        + [dma((chips,))] * 2
        + [dma((top,))] * 4
        + [dma((1,))] * 2
        + [dma((top,))] * 4,
        compiler_params=pltpu.CompilerParams(collective_id=1, has_side_effects=True),
        name="scatter_rows",
    )(grads.reshape(count, rows, width), vectors.reshape(lines, 128))
    return shard, sums.reshape(-1)


GELU_CUBE = 0.044715
POOL = 24
F32, BF16 = jnp.float32, jnp.bfloat16


def mm(left, right, dims=((1,), (0,))):
    return lax.dot_general(left, right, (dims, ((), ())), preferred_element_type=F32)


class Names:
    def __init__(self, names, refs):
        for name, ref in zip(names, refs):
            setattr(self, name, ref)


STAGED = ("lens", "tok", "cot", "gain", "shift", "b_qv", "b_out", "b_fc1", "b_fc2")
IN_NAMES = [
    "far_tok", "far_cot", "far_lens", "far_gain", "far_shift", "w_qkv", "far_b_qv", "w_out",
    "far_b_out", "w_fc1", "far_b_fc1", "w_fc2", "far_b_fc2",
]
OUT_NAMES = ["far_y", "far_gtok", "far_gqkv", "far_gout", "far_gfc1", "far_gfc2", "far_vec"]


def layer_scratch(chips, rows, row_count, width, heads, hidden, slots):
    count, top = 2 * chips, chips // 2
    dma = pltpu.SemaphoreType.DMA
    tall = (row_count, width)
    low = dict(
        wq=(chips, 2, 3, rows, heads), wo=(chips, 2, rows, heads),
        wf1=(chips, 2, rows, hidden), wf2=(chips, 2, rows, hidden),
        n1=tall, n2=tall, gy=tall, ghb=tall,
        z=(row_count, hidden), zp=(row_count, hidden),
        du=(row_count, hidden), dup=(row_count, hidden),
        qkv=(3, row_count, heads), o=(row_count, heads), op=(row_count, heads),
        dh=(row_count, heads),
        dqkv=(3, row_count, heads), dqkvp=(3, row_count, heads),
        xt=(4, 2, chips, rows, row_count), xtp=(4, chips, rows, row_count),
        grads=(3, chips, rows, hidden), rbuf=(3, 2, top, rows, hidden),
        ysend=(4, *tall), yrecv=(4, *tall), tok=tall, cot=tall,
    )
    full = dict(
        xh1=tall, xh2=tall, h1=tall, gh1=tall, rs1=(row_count, 1), rs2=(row_count, 1),
        u=(row_count, hidden), pf=(heads // HEAD_DIM, row_count, row_count),
        mask=(row_count, row_count), vec=(16, width), vecp=(16, width), vslots=(chips, 8, 128), vres=(16, width), vsum=(16, width),
        gain=(2, width), shift=(2, width), b_qv=(2, heads), b_out=(1, width),
        b_fc1=(1, hidden), b_fc2=(1, width),
        g_qkv=(3, rows, heads), g_out=(rows, heads), g_fc1=(rows, hidden), g_fc2=(rows, hidden),
    )
    sems = dict(
        pool=(POOL,), gr=(8, 2, top), pr=(8,), sr=(12, 2, top), ar=(12,),
        yr=(4,), vr=(2, chips), loc=(8,), ins=(9,), outs=(9,),
    )
    shapes = {k: pltpu.VMEM(s, BF16) for k, s in low.items()}
    shapes |= {k: pltpu.VMEM(s, F32) for k, s in full.items()}
    shapes |= {k: dma(s) for k, s in sems.items()}
    shapes["lens"] = pltpu.SMEM((slots,), jnp.int32)
    return shapes


def layer_kernel(chips, scratch_names, *refs):
    r = Names(IN_NAMES + OUT_NAMES + scratch_names, refs)
    device, chip, core, place = ring_place(chips)
    side_y = lax.axis_index("tensor")
    count, top = 2 * chips, chips // 2
    right = 2 * chip_at(place + 1, chips) + core
    left = 2 * chip_at(place - 1, chips) + core
    partner = 2 * chip + 1 - core
    onward = (right, left)
    row_count, width = r.far_tok.shape
    rows, heads = r.w_out.shape
    hidden = r.w_fc1.shape[1]
    half_hidden = hidden // 2
    slots, issued = [None] * POOL, []

    class remote:
        def __init__(self, source, target, recv_sem, **where):
            self.parts = (source, target, recv_sem, where)

        def build(self, slot):
            source, target, recv_sem, where = self.parts
            return pltpu.make_async_remote_copy(
                src_ref=source, dst_ref=target, send_sem=r.pool.at[slot], recv_sem=recv_sem,
                device_id=where, device_id_type=pl.DeviceIdType.MESH,
            )

        def wait_recv(self):
            self.build(0).wait_recv()

    def go(send):
        slot = len(issued) % POOL
        issued.append(slot)
        if slots[slot] is not None:
            slots[slot].wait_send()
        slots[slot] = send.build(slot)
        slots[slot].start()

    barrier = pltpu.get_barrier_semaphore()

    def greet(**where):
        pl.semaphore_signal(
            barrier, inc=1, device_id=where, device_id_type=pl.DeviceIdType.MESH
        )

    for other in (right, left, partner):
        greet(dp=other)
    greet(tensor=1 - side_y)
    staged = []
    for j, name in enumerate(STAGED):
        copy = pltpu.make_async_copy(getattr(r, "far_" + name), getattr(r, name), r.ins.at[j])
        copy.start()
        staged.append(copy)
    pl.semaphore_wait(barrier, 4)

    base = (0, 0, 0, 0, 0, half_hidden, 0, half_hidden)
    span = (heads,) * 4 + (half_hidden,) * 4

    def cut(i, ref, side=None):
        start, size = base[i], span[i]
        if side is not None:
            size = size // 2
            start = start + side * size
        if start == 0 and size == ref.shape[-1]:
            return ref
        return ref.at[:, pl.ds(start, size)]

    def own(i):
        if i < 3:
            return r.w_qkv.at[i]
        return cut(i, (r.w_out, r.w_fc1, r.w_fc1, r.w_fc2, r.w_fc2)[i - 3])

    def spot_of(i, at_chip, whose, side=None):
        if i < 3:
            return cut(i, r.wq.at[at_chip, whose, i], side)
        return cut(i, (r.wo, r.wf1, r.wf1, r.wf2, r.wf2)[i - 3].at[at_chip, whose], side)

    def all_of(i, whose):
        if i < 3:
            return r.wq.at[:, whose, i]
        if i == 3:
            return r.wo.at[:, whose]
        return (r.wf1, r.wf1, r.wf2, r.wf2)[i - 4].at[:, whose, :, pl.ds(base[i], span[i])]

    def block(i, step, whose, hop, side):
        return spot_of(i, chip_at(place + step, chips), whose, side if hop == top else None)

    def keep(i):
        return pltpu.make_async_copy(own(i), spot_of(i, chip, core), r.loc.at[i])

    def start_item(i):
        mine, there = own(i), spot_of(i, chip, core)
        for side in (0, 1):
            go(remote(mine, there, r.gr.at[i, side, 0], dp=onward[side]))
        go(remote(mine, there, r.pr.at[i], dp=partner))
        keep(i).start()

    def hop_item(i, hop):
        for side, sign in ((0, -1), (1, 1)):
            here = block(i, sign * hop, core, hop, side)
            remote(
                here, here, r.gr.at[i, side, hop - 1], dp=onward[side]
            ).wait_recv()
            if hop < top:
                part = block(i, sign * hop, core, hop + 1, side)
                go(remote(
                    part, part, r.gr.at[i, side, hop], dp=onward[side]
                ))
            go(remote(here, here, r.pr.at[i], dp=partner))

    def finish_item(i):
        keep(i).wait()
        theirs = all_of(i, 1 - core)
        remote(theirs, theirs, r.pr.at[i], dp=partner).wait_recv()

    def swap(k, source, target):
        go(remote(source, target, r.ar.at[k], dp=partner))

    def swapped(k, target):
        remote(target, target, r.ar.at[k], dp=partner).wait_recv()

    quarter = width // 4
    group = chips // 4

    def exchange(k, c):
        at = pl.ds(c * quarter, quarter)
        go(remote(
            r.ysend.at[k, :, at], r.yrecv.at[k, :, at], r.yr.at[k], tensor=1 - side_y
        ))

    def exchanged(k):
        spot = r.yrecv.at[k]
        remote(spot, spot, r.yr.at[k], tensor=1 - side_y).wait_recv()

    scatter_span = hidden // 4
    half = scatter_span // 2

    def scatter_start(i):
        k, col = i // 4, (i % 4) * scatter_span
        far = r.grads.at[k, chip_at(place + top, chips)]
        for side in (0, 1):
            at = pl.ds(col + side * half, half)
            go(remote(
                far.at[:, at], r.rbuf.at[k, side, 0, :, at], r.sr.at[i, side, 0], dp=onward[side],
            ))

    def scatter_step(i, s):
        k, col = i // 4, (i % 4) * scatter_span
        for side, sign in ((0, 1), (1, -1)):
            target = chip_at(place + sign * (top - s), chips)
            at = pl.ds(col + side * half, half) if s == 1 else pl.ds(col, scatter_span)
            spot = r.rbuf.at[k, side, s - 1, :, at]
            remote(
                spot, spot, r.sr.at[i, side, s - 1], dp=onward[side]
            ).wait_recv()
            total = r.grads[k, target, :, at].astype(F32) + spot[...].astype(F32)
            r.grads[k, target, :, at] = total.astype(BF16)
            at = pl.ds(col, scatter_span)
            go(remote(
                r.grads.at[k, target, :, at], r.rbuf.at[k, side, s, :, at],
                r.sr.at[i, side, s], dp=onward[side],
            ))

    def scatter_end(i):
        k, col = i // 4, (i % 4) * scatter_span
        at = pl.ds(col, scatter_span)
        total = r.grads[k, chip, :, at].astype(F32)
        for side in (0, 1):
            spot = r.rbuf.at[k, side, top - 1, :, at]
            remote(
                spot, spot, r.sr.at[i, side, top - 1], dp=onward[side]
            ).wait_recv()
            total = total + spot[...].astype(F32)
        if k == 0:
            r.g_fc2[:, at] = total
        elif k == 1:
            r.g_fc1[:, at] = total
        elif i < 11:
            r.g_qkv[i - 8] = total
            put(r.g_qkv.at[i - 8], r.far_gqkv.at[i - 8])
        else:
            r.g_out[...] = total
            put(r.g_out, r.far_gout)

    order = [(i, s) for s in range(1, top) for i in range(4)]
    order += [(4 + i, s) for s in range(1, top) for i in range(4)]
    order += [(i, s) for s in range(1, top) for i in (11, 8, 9, 10)]
    steps = iter(order)

    def advance(n):
        for _ in range(n):
            scatter_step(*next(steps))

    put_copies = []

    def put(source, target):
        copy = pltpu.make_async_copy(source, target, r.outs.at[len(put_copies)])
        copy.start()
        put_copies.append(copy)

    def grad_tile(k, column, size, terms):
        total = None
        for lhs, rhs in terms:
            part = mm(lhs.reshape(chips * rows, row_count), rhs)
            total = part if total is None else total + part
        r.grads[k, :, :, pl.ds(column, size)] = total.reshape(chips, rows, size).astype(BF16)

    chunk = 32

    def row_loop(fn, carry=()):
        def step(i, c):
            return fn(pl.ds(pl.multiple_of(i * chunk, chunk), chunk), i * chunk, c)
        return lax.fori_loop(0, row_count // chunk, step, carry)

    def fold(value):
        return jnp.sum(value.reshape(chunk // 8, 8, value.shape[1]), axis=0)

    def transposed(k, source):
        per = 2 * rows
        for c in range(chips):
            flipped = source[:, c * per : (c + 1) * per].T
            r.xt[k, 0, c] = flipped[:rows]
            r.xt[k, 1, c] = flipped[rows:]
        swap(k, r.xt.at[k, 1 - core], r.xtp.at[k])

    for i in range(4):
        start_item(i)
    for copy in staged:
        copy.wait()
    ends = []
    for j in range(r.lens.shape[0]):
        ends.append(r.lens[j] if j == 0 else ends[-1] + r.lens[j])
    at_row = lax.broadcasted_iota(jnp.int32, (row_count, row_count), 0)
    at_col = lax.broadcasted_iota(jnp.int32, (row_count, row_count), 1)
    seg_row = sum((at_row >= e).astype(jnp.int32) for e in ends)
    seg_col = sum((at_col >= e).astype(jnp.int32) for e in ends)
    allowed = (seg_row == seg_col) & (at_row >= at_col)
    r.mask[...] = allowed.astype(F32)
    r.vec[...] = jnp.zeros_like(r.vec)

    def is_live(first):
        return first + lax.broadcasted_iota(jnp.int32, (chunk, width), 0) < ends[-1]

    def first_norm(at, first, c):
        x = r.tok[at, :].astype(F32)
        x = x - jnp.mean(x, axis=1, keepdims=True)
        inv = lax.rsqrt(jnp.mean(x * x, axis=1, keepdims=True) + NORM_EPS)
        x = x * inv
        r.xh1[at, :] = x
        r.rs1[at, :] = inv
        r.n1[at, :] = (x * r.gain[0:1, :] + r.shift[0:1, :]).astype(BF16)
        g = jnp.where(is_live(first), r.cot[at, :].astype(F32), 0.0)
        r.gy[at, :] = g.astype(BF16)
        return (c[0] + fold(g),)

    (total,) = row_loop(first_norm, (jnp.zeros((8, width), F32),))
    r.vec[8:9, :] = jnp.sum(total, axis=0, keepdims=True)
    for i in range(4):
        hop_item(i, 1)
    transposed(0, r.n1)
    for i in range(4):
        hop_item(i, 2)
    transposed(1, r.gy)
    for i in range(4):
        hop_item(i, 3)
    start_item(4)
    start_item(5)
    start_item(6)

    for i in range(3):
        hop_item(i, 4)
        finish_item(i)
        part = mm(r.n1[...], r.wq[:, :, i].reshape(width, heads))
        if i != 1:
            part = part + r.b_qv[i // 2 : i // 2 + 1, :]
        r.qkv[i] = part.astype(BF16)
    hop_item(3, 4)
    hop_item(4, 1)
    lane = lax.broadcasted_iota(jnp.int32, (1, 2 * HEAD_DIM), 1)
    picks = [(lane // HEAD_DIM == j).astype(F32).astype(BF16) for j in (0, 1)]
    first_half = lax.broadcasted_iota(jnp.int32, (row_count, 2 * HEAD_DIM), 1) < HEAD_DIM
    pairs = heads // (2 * HEAD_DIM)
    scale = HEAD_DIM ** (-0.5)
    between = [(5, 1), (6, 1), (4, 2), (5, 2)]
    for p in range(pairs):
        at = pl.ds(p * 2 * HEAD_DIM, 2 * HEAD_DIM)
        q, k, v = r.qkv[0, :, at], r.qkv[1, :, at], r.qkv[2, :, at]
        mixed = []
        for j in (0, 1):
            s = mm(q * picks[j], k, ((1,), (1,))) * scale
            s = jnp.where(r.mask[...] > 0.5, s, -1e30)
            e = jnp.exp(s - jnp.max(s, axis=1, keepdims=True))
            e = e / jnp.sum(e, axis=1, keepdims=True)
            r.pf[2 * p + j] = e
            mixed.append(mm(e.astype(BF16), v))
        r.o[:, at] = jnp.where(first_half, mixed[0], mixed[1]).astype(BF16)
        hop_item(*between[p])
    start_item(7)
    finish_item(3)
    for c in range(4):
        w = r.wo[c * group : (c + 1) * group].reshape(quarter, heads)
        r.ysend[0, :, pl.ds(c * quarter, quarter)] = mm(r.o[...], w, ((1,), (1,))).astype(BF16)
        exchange(0, c)
    swap(8, r.o, r.op)
    hop_item(4, 3)
    hop_item(5, 3)
    hop_item(6, 2)
    hop_item(7, 1)
    exchanged(0)

    def second_norm(at, first, c):
        x = r.tok[at, :].astype(F32)
        x = x + (r.ysend[0, at, :].astype(F32) + r.yrecv[0, at, :].astype(F32)) + r.b_out[...]
        r.h1[at, :] = x
        x = x - jnp.mean(x, axis=1, keepdims=True)
        inv = lax.rsqrt(jnp.mean(x * x, axis=1, keepdims=True) + NORM_EPS)
        x = x * inv
        r.xh2[at, :] = x
        r.rs2[at, :] = inv
        r.n2[at, :] = (x * r.gain[1:2, :] + r.shift[1:2, :]).astype(BF16)
        return c

    row_loop(second_norm)
    transposed(2, r.n2)
    hop_item(4, 4)
    hop_item(5, 4)
    finish_item(4)
    finish_item(5)

    tile = hidden // 4
    later = [(), (6, 3), (7, 2), (6, 4)]
    for t in range(4):
        at = pl.ds(t * tile, tile)
        r.u[:, at] = mm(r.n2[...], r.wf1[:, :, :, at].reshape(width, tile)) + r.b_fc1[:, at]

        def gelu(rows_at, first, c):
            u = r.u[rows_at, at]
            t_ = jnp.tanh(GELU_COEF * (u + GELU_CUBE * u * u * u))
            r.z[rows_at, at] = (0.5 * u * (1.0 + t_)).astype(BF16)
            r.u[rows_at, at] = 0.5 * (1.0 + t_) + 0.5 * u * (1.0 - t_ * t_) * GELU_COEF * (
                1.0 + 3.0 * GELU_CUBE * u * u
            )
            return c

        row_loop(gelu)
        if t % 2 == 1:
            cols = pl.ds((t // 2) * half_hidden, half_hidden)
            swap(4 + t // 2, r.z.at[:, cols], r.zp.at[:, cols])
        if later[t]:
            hop_item(*later[t])
    swapped(1, r.xtp.at[1])
    for h in (0, 1):
        cols = pl.ds(h * half_hidden, half_hidden)
        swapped(4 + h, r.zp.at[:, cols])
        for t in (2 * h, 2 * h + 1):
            at = pl.ds(t * tile, tile)
            grad_tile(0, t * tile, tile, ((r.xt[1, core], r.z[:, at]), (r.xtp[1], r.zp[:, at])))
            scatter_start(t)
        hop_item(7, 3 + h)
    finish_item(6)
    finish_item(7)
    for t in range(4):
        at = pl.ds(t * tile, tile)
        d = mm(r.gy[...], r.wf2[:, :, :, at].reshape(width, tile)) * r.u[:, at]
        d = d.astype(BF16)
        r.du[:, at] = d
        row, col = (t * tile) // width, (t * tile) % width
        r.vec[6 + row : 7 + row, col : col + tile] = jnp.sum(
            d.astype(F32), axis=0, keepdims=True
        )
        if t % 2 == 1:
            cols = pl.ds((t // 2) * half_hidden, half_hidden)
            swap(6 + t // 2, r.du.at[:, cols], r.dup.at[:, cols])
        advance(1)
    for c in range(4):
        w = r.wf1[c * group : (c + 1) * group].reshape(quarter, hidden)
        r.ysend[1, :, pl.ds(c * quarter, quarter)] = mm(r.du[...], w, ((1,), (1,))).astype(BF16)
        exchange(1, c)
        advance(1)
    swapped(2, r.xtp.at[2])
    for h in (0, 1):
        cols = pl.ds(h * half_hidden, half_hidden)
        swapped(6 + h, r.dup.at[:, cols])
        for t in (2 * h, 2 * h + 1):
            at = pl.ds(t * tile, tile)
            grad_tile(1, t * tile, tile, ((r.xt[2, core], r.du[:, at]), (r.xtp[2], r.dup[:, at])))
            scatter_start(4 + t)
            advance(1)
    for j in range(1, chips):
        greet(dp=2 * lax.rem(chip + j, chips) + core)
    for c in range(4):
        w = r.wf2[c * group : (c + 1) * group].reshape(quarter, hidden)
        r.ysend[2, :, pl.ds(c * quarter, quarter)] = mm(r.z[...], w, ((1,), (1,))).astype(BF16)
        exchange(2, c)
    advance(2)
    exchanged(1)

    def norm_back(k, gain_row, xh, rs, above, store):
        def step(at, first, c):
            dn = r.ysend[k, at, :].astype(F32) + r.yrecv[k, at, :].astype(F32)
            x = xh[at, :]
            scaled = dn * r.gain[gain_row : gain_row + 1, :]
            m1 = jnp.mean(scaled, axis=1, keepdims=True)
            m2 = jnp.mean(scaled * x, axis=1, keepdims=True)
            g = above[at, :].astype(F32) + rs[at, :] * (scaled - m1 - x * m2)
            store(at, g)
            return (c[0] + fold(dn * x), c[1] + fold(dn), c[2] + fold(g))

        zero = jnp.zeros((8, width), F32)
        return [jnp.sum(s, axis=0, keepdims=True) for s in row_loop(step, (zero, zero, zero))]

    def store_gh1(at, g):
        r.gh1[at, :] = g
        r.ghb[at, :] = g.astype(BF16)

    sums = norm_back(1, 1, r.xh2, r.rs2, r.gy, store_gh1)
    r.vec[1:2, :] = sums[0]
    r.vec[3:4, :] = sums[1]
    r.vec[5:6, :] = sums[2]
    transposed(3, r.ghb)
    advance(1)

    r.dh[...] = mm(r.ghb[...], r.wo[...].reshape(width, heads)).astype(BF16)
    for p in range(pairs):
        at = pl.ds(p * 2 * HEAD_DIM, 2 * HEAD_DIM)
        q, k, v = r.qkv[0, :, at], r.qkv[1, :, at], r.qkv[2, :, at]
        d_out, o = r.dh[:, at], r.o[:, at]
        parts = []
        for j in (0, 1):
            mine = d_out * picks[j]
            delta = jnp.sum(mine.astype(F32) * o.astype(F32), axis=1, keepdims=True)
            prob = r.pf[2 * p + j]
            ds = (prob * (mm(mine, v, ((1,), (1,))) - delta) * scale).astype(BF16)
            parts.append((
                mm(ds, k),
                mm(ds, q, ((0,), (0,))),
                mm(prob.astype(BF16), d_out, ((0,), (0,))),
            ))
        for i in range(3):
            r.dqkv[i, :, at] = jnp.where(first_half, parts[0][i], parts[1][i]).astype(BF16)
        advance((1, 1, 2, 1)[p])
    swap(9, r.dqkv, r.dqkvp)
    swapped(3, r.xtp.at[3])
    swapped(8, r.op)
    grad_tile(2, 3 * heads, heads, ((r.xt[3, core], r.o[...]), (r.xtp[3], r.op[...])))
    scatter_start(11)
    for c in range(4):
        total = None
        for i in range(3):
            w = r.wq[c * group : (c + 1) * group, :, i].reshape(quarter, heads)
            part = mm(r.dqkv[i], w, ((1,), (1,)))
            total = part if total is None else total + part
        r.ysend[3, :, pl.ds(c * quarter, quarter)] = total.astype(BF16)
        exchange(3, c)
        if c % 2 == 1:
            advance(1)
    for i in (0, 2):
        r.vec[4:5, pl.ds((i // 2) * heads, heads)] = jnp.sum(
            r.dqkv[i].astype(F32), axis=0, keepdims=True
        )
    swapped(0, r.xtp.at[0])
    swapped(9, r.dqkvp)
    for i in range(3):
        grad_tile(
            2, i * heads, heads, ((r.xt[0, core], r.dqkv[i]), (r.xtp[0], r.dqkvp[i]))
        )
        scatter_start(8 + i)
    advance(1)
    for i in range(4):
        scatter_end(i)
    put(r.g_fc2, r.far_gfc2)
    advance(1)
    exchanged(2)

    def finish_output(at, first, c):
        y = r.h1[at, :] + (r.ysend[2, at, :].astype(F32) + r.yrecv[2, at, :].astype(F32))
        y = jnp.where(is_live(first), y + r.b_fc2[...], 0.0)
        r.n2[at, :] = y.astype(BF16)
        return c

    row_loop(finish_output)
    put(r.n2, r.far_y)
    advance(4)
    exchanged(3)

    def store_tokens(at, g):
        r.gh1[at, :] = g

    sums = norm_back(3, 0, r.xh1, r.rs1, r.gh1, store_tokens)
    r.vec[0:1, :] = sums[0]
    r.vec[2:3, :] = sums[1]
    put(r.gh1, r.far_gtok)

    swap(10, r.vec, r.vecp)
    top_row = pl.multiple_of(8 * core, 8)

    def tile_of(ref, which):
        return ref.at[pl.ds(top_row, 8), pl.ds(pl.multiple_of(128 * which, 128), 128)]

    def tile_copy(stage, j, source, target):
        other = lax.rem(chip + j, chips)
        return remote(
            source, target, r.vr.at[stage, j], dp=2 * other + core
        )

    advance(1)
    swapped(10, r.vecp)
    r.vres[...] = r.vec[...] + r.vecp[...]
    pl.semaphore_wait(barrier, chips - 1)
    for j in range(1, chips):
        go(tile_copy(0, j, tile_of(r.vres, lax.rem(chip + j, chips)), r.vslots.at[chip]))
    r.vslots[chip] = tile_of(r.vres, chip)[...]
    advance(3)
    for i in range(4, 8):
        scatter_end(i)
    put(r.g_fc1, r.far_gfc1)
    advance(2)
    for j in range(1, chips):
        spot = r.vslots.at[lax.rem(chip + chips - j, chips)]
        tile_copy(0, j, spot, spot).wait_recv()
    mine = tile_of(r.vsum, chip)
    mine[...] = jnp.sum(r.vslots[...], axis=0)
    for j in range(1, chips):
        go(tile_copy(1, j, mine, mine))
    advance(2)
    assert next(steps, None) is None
    for j in range(1, chips):
        spot = tile_of(r.vsum, lax.rem(chip + chips - j, chips))
        tile_copy(1, j, spot, spot).wait_recv()
    rows_here = r.vsum.at[pl.ds(top_row, 8), :]
    swap(11, rows_here, rows_here)
    swapped(11, r.vsum.at[pl.ds(pl.multiple_of(8 * (1 - core), 8), 8), :])
    put(r.vsum, r.far_vec)
    for i in (11, 8, 9, 10):
        scatter_end(i)
    for copy in put_copies:
        copy.wait()
    for copy in slots:
        copy.wait_send()


def one_kernel(tokens, cotangent, seq_lens, gain, shift, w_qkv, b_qv, w_out, b_out, w_fc1, b_fc1, w_fc2, b_fc2):
    chips = lax.axis_size("dp") // 2
    row_count, width = tokens.shape
    rows, heads = w_out.shape
    hidden = w_fc1.shape[1]
    vmem, hbm = pl.BlockSpec(memory_space=pltpu.VMEM), pl.BlockSpec(memory_space=pl.ANY)
    scratch = layer_scratch(chips, rows, row_count, width, heads, hidden, seq_lens.shape[0])
    names = list(scratch)

    def made(*shape, kind=F32):
        return jax.ShapeDtypeStruct(shape, kind)

    outs = pl.pallas_call(
        lambda *refs: layer_kernel(chips, names, *refs),
        out_shape=(
            made(row_count, width, kind=BF16), made(row_count, width), made(3, rows, heads),
            made(rows, heads), made(rows, hidden), made(rows, hidden), made(16, width),
        ),
        in_specs=[hbm] * 13,
        out_specs=(hbm,) * 7,
        scratch_shapes=list(scratch.values()),
        compiler_params=pltpu.CompilerParams(
            collective_id=2, has_side_effects=True, vmem_limit_bytes=63 * 2**20
        ),
        name="layer",
    )(
        tokens, cotangent, seq_lens, gain, shift, w_qkv, b_qv, w_out, b_out[None], w_fc1,
        b_fc1[None], w_fc2, b_fc2[None],
    )
    small = ((2, width), (2, width), (2, heads), (1, width), (1, hidden), (1, width))
    outs = pl.pallas_call(
        lambda *refs: results_kernel(heads, *refs),
        out_shape=tuple(made(*o.shape, kind=o.dtype) for o in outs[:6])
        + tuple(made(*o) for o in small),
        in_specs=[vmem] * 7,
        out_specs=(hbm,) * 6 + (vmem,) * 6,
        scratch_shapes=[pltpu.SemaphoreType.DMA((6,))],
        name="results",
    )(*outs)
    y, g_tok, g_qkv, g_out, g_fc1, g_fc2, g_gain, g_shift, g_bqv, g_bout, g_bfc1, g_bfc2 = outs
    return (
        y, g_tok, g_gain, g_shift, g_qkv, g_bqv, g_out, g_bout.reshape(-1), g_fc1,
        g_bfc1.reshape(-1), g_fc2, g_bfc2.reshape(-1),
    )


def results_kernel(heads, *refs):
    sources, vec, targets, sem = refs[:6], refs[6], refs[7:13], refs[19]
    gain, shift, bqv, bout, bfc1, bfc2 = refs[13:19]
    copies = [
        pltpu.make_async_copy(source, target, sem.at[i])
        for i, (source, target) in enumerate(zip(sources, targets))
    ]
    for copy in copies:
        copy.start()
    width = vec.shape[1]
    gain[...] = vec[0:2, :]
    shift[...] = vec[2:4, :]
    bqv[0:1, :] = vec[4:5, :heads]
    bqv[1:2, :] = vec[4:5, heads : 2 * heads]
    bout[...] = vec[5:6, :]
    for j in range(bfc1.shape[1] // width):
        bfc1[:, j * width : (j + 1) * width] = vec[6 + j : 7 + j, :]
    bfc2[...] = vec[8:9, :]
    for copy in copies:
        copy.wait()


def fits_one_kernel(tokens, w_out, w_fc1):
    chips = lax.axis_size("dp") // 2
    rows, heads = w_out.shape
    width, hidden = tokens.shape[1], w_fc1.shape[1]
    return (
        lax.axis_size("tensor") == 2
        and chips == 2 * 4
        and width == 128 * chips
        and rows % 16 == 0
        and tokens.shape[0] % 32 == 0
        and 2 * heads == width
        and 4 * heads == hidden
    )


def body(
    tokens,
    cotangent,
    seq_lens,
    layer_norm_gain,
    layer_norm_bias,
    w_qkv,
    b_qv,
    w_out,
    b_out,
    w_fc1,
    b_fc1,
    w_fc2,
    b_fc2,
):
    if fits_one_kernel(tokens, w_out, w_fc1):
        return one_kernel(
            tokens, cotangent, seq_lens, layer_norm_gain, layer_norm_bias, w_qkv, b_qv, w_out,
            b_out, w_fc1, b_fc1, w_fc2, b_fc2,
        )
    heads_width, hidden_width = w_out.shape[1], w_fc1.shape[1]
    attn_shards = jnp.concatenate([w_qkv[0], w_qkv[1], w_qkv[2], w_out], axis=1)
    mlp_shards = jnp.concatenate([w_fc1, w_fc2], axis=1)
    mlp_full = lax.all_gather(mlp_shards, "dp", axis=0, tiled=True)
    attn_full = gather_rows(attn_shards)
    qkv_full, out_full = attn_full[:, : 3 * heads_width], attn_full[:, 3 * heads_width :]
    fc1_full, fc2_full = mlp_full[:, :hidden_width], mlp_full[:, hidden_width:]
    allowed, live_rows = seq_masks(seq_lens, tokens.shape[0])
    input_tokens = tokens.astype(jnp.float32)
    first_normalized, first_centered_scaled, first_inverse_deviation = layer_norm_forward(
        input_tokens, layer_norm_gain[0], layer_norm_bias[0]
    )
    low1 = first_normalized.astype(jnp.bfloat16)
    proj = product("td,dc->tc", low1, qkv_full)
    query = (proj[:, :heads_width] + b_qv[0]).astype(jnp.bfloat16)
    key_rows = proj[:, heads_width : 2 * heads_width].astype(jnp.bfloat16)
    value = (proj[:, 2 * heads_width :] + b_qv[1]).astype(jnp.bfloat16)
    heads_out, logsum = attend(query, key_rows, value, allowed)
    attn_part = product("tc,dc->td", heads_out, out_full)
    attn_mix = sum_tensor(attn_part)
    first_hidden_state = input_tokens + attn_mix + b_out
    second_normalized, second_centered_scaled, second_inverse_deviation = layer_norm_forward(
        first_hidden_state, layer_norm_gain[1], layer_norm_bias[1]
    )
    low2 = second_normalized.astype(jnp.bfloat16)
    pre_act = jnp.dot(low2, fc1_full, preferred_element_type=jnp.float32) + b_fc1
    act, slope = gelu_parts(pre_act)
    act_low = act.astype(jnp.bfloat16)
    mlp_part = product("tf,df->td", act_low, fc2_full)
    mlp_mix = sum_tensor(mlp_part)
    result = first_hidden_state + mlp_mix + b_fc2
    output = jnp.where(live_rows[:, None], result, 0.0).astype(jnp.bfloat16)
    qkv_back, out_back, fc1_back, fc2_back = (qkv_full, out_full, fc1_full, fc2_full)
    grad_y = jnp.where(live_rows[:, None], cotangent, jnp.zeros_like(cotangent))
    flat_output_gradient = grad_y.astype(jnp.float32)
    d_pre = (jnp.dot(grad_y, fc2_back, preferred_element_type=jnp.float32) * slope).astype(
        jnp.bfloat16
    )
    g_fc2 = product("td,tf->df", grad_y, act_low)
    g_bfc2 = jnp.sum(flat_output_gradient, axis=0)
    g_fc1 = product("td,tf->df", low2, d_pre)
    g_mlp = jnp.concatenate([g_fc1.astype(jnp.bfloat16), g_fc2.astype(jnp.bfloat16)], axis=1)
    shard_mlp = lax.psum_scatter(g_mlp, "dp", scatter_dimension=0, tiled=True)
    g_bfc1 = jnp.sum(d_pre.astype(jnp.float32), axis=0)
    d_norm2_part = product("tf,df->td", d_pre, fc1_back)
    second_norm_delta = sum_tensor(d_norm2_part)
    second_gain_gradient = jnp.sum(second_norm_delta * second_centered_scaled, axis=0)
    g_shift2 = jnp.sum(second_norm_delta, axis=0)
    hidden_first_gradient = flat_output_gradient + layer_norm_backward(
        second_norm_delta, layer_norm_gain[1], second_centered_scaled, second_inverse_deviation
    )
    grad_low = hidden_first_gradient.astype(jnp.bfloat16)
    g_out = product("td,tc->dc", grad_low, heads_out)
    g_bout = jnp.sum(hidden_first_gradient, axis=0)
    d_heads = jnp.dot(grad_low, out_back, preferred_element_type=jnp.float32).astype(jnp.bfloat16)
    d_query, d_key, d_value = attend_back(
        query, key_rows, value, heads_out, d_heads, logsum, allowed
    )
    stacked = jnp.concatenate([d_query, d_key, d_value], axis=1)
    g_qkv = product("td,tc->dc", low1, stacked)
    g_attn = jnp.concatenate([g_qkv.astype(jnp.bfloat16), g_out.astype(jnp.bfloat16)], axis=1)
    g_bqv = jnp.stack(
        [jnp.sum(d_query.astype(jnp.float32), axis=0), jnp.sum(d_value.astype(jnp.float32), axis=0)]
    )
    d_norm1_part = product("tc,dc->td", stacked, qkv_back)
    first_norm_delta = sum_tensor(d_norm1_part)
    first_gain_gradient = jnp.sum(first_norm_delta * first_centered_scaled, axis=0)
    g_shift1 = jnp.sum(first_norm_delta, axis=0)
    input_gradient = hidden_first_gradient + layer_norm_backward(
        first_norm_delta, layer_norm_gain[0], first_centered_scaled, first_inverse_deviation
    )
    shard_mlp = shard_mlp.astype(jnp.float32)
    shard_fc1, shard_fc2 = shard_mlp[:, :hidden_width], shard_mlp[:, hidden_width:]
    vectors = jnp.concatenate(
        [
            first_gain_gradient,
            second_gain_gradient,
            g_shift1,
            g_shift2,
            g_bqv.reshape(-1),
            g_bout,
            g_bfc1,
            g_bfc2,
        ]
    )
    shard_attn, vectors = scatter_rows(g_attn, vectors)
    shard_qkv = jnp.stack([shard_attn[:, i * heads_width : (i + 1) * heads_width] for i in range(3)])
    shard_out = shard_attn[:, 3 * heads_width :]
    width = tokens.shape[1]
    cuts = [2 * width, 4 * width, 4 * width + 2 * heads_width]
    cuts += [cuts[-1] + width, cuts[-1] + width + hidden_width]
    gain_sum, shift_sum, bqv_sum, bout_sum, bfc1_sum, bfc2_sum = jnp.split(vectors, cuts)
    gain_sum, shift_sum = gain_sum.reshape(2, width), shift_sum.reshape(2, width)
    bqv_sum = bqv_sum.reshape(2, heads_width)
    return (
        output,
        input_gradient,
        gain_sum,
        shift_sum,
        shard_qkv,
        bqv_sum,
        shard_out,
        bout_sum,
        shard_fc1,
        bfc1_sum,
        shard_fc2,
        bfc2_sum,
    )


def solution(mesh):
    in_specs = (
        P("dp", None),
        P("dp", None),
        P("dp"),
        P(),
        P(),
        P(None, "dp", "tensor"),
        P(None, "tensor"),
        P("dp", "tensor"),
        P(),
        P("dp", "tensor"),
        P("tensor"),
        P("dp", "tensor"),
        P(),
    )
    out_specs = (
        P("dp", None),
        P("dp", None),
        P(),
        P(),
        P(None, "dp", "tensor"),
        P(None, "tensor"),
        P("dp", "tensor"),
        P(),
        P("dp", "tensor"),
        P("tensor"),
        P("dp", "tensor"),
        P(),
    )
    return jax.shard_map(body, mesh=mesh, in_specs=in_specs, out_specs=out_specs, check_vma=False)
```
